32 devices in a mesh: group: 2 (over y), chan: 4 (over z), tm: 2 (over x), beam: 2 (over core).
Axes of the slice: x: 2, y: 2, z: 4, core: 2. Of those that a mesh axis runs over, the one named last changes fastest.
Arguments:
- samples: bfloat16 [1024, 2, 1024, 16], P(('group', 'chan', 'beam'), None, None, 'tm'), parts along dimension 0, may hold values from -6 to 6
- window_taps: float32 [4, 1024], replicated, may hold values from -1 to 1
- sky_model: bfloat16 [1024, 2, 512, 512], P(('group', 'chan', 'tm'), None, 'beam'), parts along dimension 0, may hold values from -0.0234375 to 0.0234375
- prior_gains: float32 [1024, 2, 512], P(('group', 'chan', 'tm')), parts along dimension 0, may hold values from -4.2 to 4.2
- beam_steering: int32 [2, 1024], P(None, ('group', 'beam')), parts along dimension 1, may hold values from 0 to 255
- input_flags: int32 [1024, 512], P(('group', 'chan', 'tm')), parts along dimension 0, may hold values 0 or 1
Outputs:
- visibilities: bfloat16 [1024, 2, 512, 512], P(('group', 'chan', 'tm'), None, 'beam'), parts along dimension 0
- new_gains: float32 [1024, 2, 512], P(('group', 'chan', 'tm'), None, 'beam'), parts along dimension 0
- beam_power: float32 [1024, 512, 16], P(('group', 'chan', 'tm'), 'beam'), parts along dimension 0
The draws below stay inside these ranges and needn't reach their ends.
There are 2 independent parts, one for each index of `group`. The reference program is written for one: setup_inputs(seed, part) draws one part's arguments, and reference() takes and returns one part's arrays. A program takes and returns all parts, laid end to end along the dimension named above; an argument that names none is the same for every part. Nothing has to cross between parts.
All inputs are finite; a program needn't handle non-finite values. No bound on the sum of `input_flags` on one device may be relied on, other than what follows from the above.
Results may differ from the reference program's by a relative error of at most 0.0076.
Values may be sent and summed in bfloat16 or wider, within the bound.
A program may use at most 384 MiB of HBM per device.

```python
import math
import jax
import jax.numpy as jnp
from jax import lax

NIN = 512
NFFT = 1024
NCH = 512
PT = 4
NBEAM = 512
ITERS = 2
FRAMES = 16


def touch_ends(drawn, key, smallest, top_value):
    index_at = [jax.random.randint(jax.random.fold_in(key, axis), (), 0, length) for axis, length in enumerate(drawn.shape)]
    widest = drawn.shape.index(max(drawn.shape))
    next_to = index_at[:widest] + [(index_at[widest] + 1) % drawn.shape[widest]] + index_at[widest + 1:]
    return drawn.at[tuple(index_at)].set(smallest).at[tuple(next_to)].set(top_value)


def shard_levels(own_key, dims, pieces, low, top_value):
    def one(dim, blocks):
        steps = jax.random.uniform(jax.random.fold_in(jax.random.fold_in(own_key, 6), dim), (blocks,), jnp.float32, low / len(pieces), top_value / len(pieces))
        return jnp.repeat(jnp.exp(steps), dims[dim] // blocks).reshape((-1,) + (1,) * (len(dims) - dim - 1))

    level = one(*pieces[0])
    for cut in pieces[1:]:
        level = level * one(*cut)
    return level


def noise(stream_key, dims, spread, bound, cuts=(), kind=jnp.bfloat16):
    array = spread * jax.random.normal(stream_key, dims, jnp.float32)
    if cuts:
        array = array * shard_levels(stream_key, dims, cuts, -0.22, 0.18)
    return jnp.clip(array, -bound, bound).astype(kind)


def setup_inputs(seed: int = 0, part: int = 0) -> dict:
    arg_keys = jax.random.split(jax.random.key(seed), 7)
    part_splits = jax.random.split(jax.random.fold_in(arg_keys[6], part), 7)
    return {
        "samples": noise(part_splits[0], (NIN, 2, NFFT, FRAMES), 1.0, 6.0, ((0, 8), (3, 2))),
        "window_taps": jnp.clip(jax.random.uniform(arg_keys[1], (PT, NFFT), jnp.float32, -1.0, 1.0), -1.0, 1.0),
        "sky_model": noise(part_splits[2], (NCH, 2, NIN, NIN), (NIN * NIN // 4) ** -0.5, 0.0234375, ((0, 8), (2, 2))),
        "prior_gains": noise(part_splits[3], (NCH, 2, NIN), 0.7, 4.2, ((0, 8),), jnp.float32),
        "beam_steering": touch_ends(jax.random.randint(part_splits[4], (2, NBEAM), 0, 256), jax.random.fold_in(part_splits[4], 1), 0, 255).astype(jnp.int32),
        "input_flags": touch_ends((jax.random.randint(part_splits[5], (NCH, NIN), 0, 16) < 15).astype(jnp.int32), jax.random.fold_in(part_splits[5], 1), 0, 1),
    }


damping = 0.5
epsilon = 1e-06

def pfb_table(window_taps, kept_count):
    transform_count = window_taps.shape[1]
    kept = jnp.arange(kept_count, dtype=jnp.int32)
    indices = jnp.arange(transform_count, dtype=jnp.int32)
    phases = (kept[:, None] * indices[None, :] % transform_count).astype(jnp.float32) * (2.0 * math.pi / transform_count)
    cosine = jnp.cos(phases)
    sine_part = jnp.sin(phases)
    real_row = jnp.concatenate([cosine, sine_part], axis=1)
    imag_row = jnp.concatenate([-sine_part, cosine], axis=1)
    base_matrix = jnp.stack([real_row, imag_row], axis=1).reshape(2 * kept_count, 2 * transform_count)
    doubled = jnp.concatenate([window_taps, window_taps], axis=1)
    return (base_matrix[None] * doubled[:, None, :] / math.sqrt(transform_count)).astype(jnp.bfloat16)

def steering_angles(beam_steering, channels, input_count, chan_total):
    positions = jnp.arange(input_count, dtype=jnp.int32)
    column = positions // (input_count // 4)
    within = positions % (input_count // 4)
    phase_index = (beam_steering[0][:, None] * column[None, :] * 64 + beam_steering[1][:, None] * within[None, :]) % 256
    scaled = phase_index[None] * (chan_total + channels)[:, None, None]
    return scaled.astype(jnp.float32) * (2.0 * math.pi / (512 * chan_total))

def reference(samples, window_taps, sky_model, prior_gains, beam_steering, input_flags):
    coeff_table = pfb_table(window_taps, NCH).astype(jnp.float32)
    stacked = samples.reshape(NIN, 2 * NFFT, FRAMES)
    group_size = math.gcd(NIN, 32)
    grouped = stacked.reshape(NIN // group_size, group_size, 2 * NFFT, FRAMES)

    def filter_group(group_block):
        values = jnp.pad(group_block.astype(jnp.float32), ((0, 0), (0, 0), (PT - 1, 0)))
        running = jnp.zeros((group_size, 2 * NCH, FRAMES), jnp.float32)
        for tap_index in range(PT):
            running = running + jnp.einsum('ab,ibf->iaf', coeff_table[tap_index], values[:, :, tap_index:tap_index + FRAMES], precision=lax.Precision.HIGHEST)
        return running.astype(jnp.bfloat16)
    spectra = lax.map(filter_group, grouped).reshape(NIN, NCH, 2, FRAMES)
    by_channel = jnp.transpose(spectra, (1, 0, 2, 3))
    channels = jnp.arange(NCH, dtype=jnp.int32)
    highest = lax.Precision.HIGHEST

    def one_channel(channel_items):
        channel_spectrum, model_part, gains_part, flags_part, channel = channel_items
        values = channel_spectrum.astype(jnp.float32)
        paired = values.reshape(NIN, 2 * FRAMES)
        rotated = jnp.stack([values[:, 1], -values[:, 0]], axis=1).reshape(NIN, 2 * FRAMES)
        vis_real = jnp.dot(paired, paired.T, precision=highest) / FRAMES
        vis_imag = jnp.dot(rotated, paired.T, precision=highest) / FRAMES
        vis_stored = jnp.stack([vis_real, vis_imag]).astype(jnp.bfloat16)
        vis_used = lax.optimization_barrier(vis_stored).astype(jnp.float32)
        model_values = model_part.astype(jnp.float32)
        weighted_real = vis_used[0] * model_values[0] + vis_used[1] * model_values[1]
        weighted_imag = vis_used[1] * model_values[0] - vis_used[0] * model_values[1]
        model_power = model_values[0] * model_values[0] + model_values[1] * model_values[1]
        weights = flags_part.astype(jnp.float32)
        current = gains_part
        for step_index in range(ITERS):
            masked_real = current[0] * weights
            masked_imag = current[1] * weights
            numer_real = jnp.dot(weighted_real, masked_real, precision=highest) - jnp.dot(weighted_imag, masked_imag, precision=highest)
            numer_imag = jnp.dot(weighted_real, masked_imag, precision=highest) + jnp.dot(weighted_imag, masked_real, precision=highest)
            denom = jnp.dot(model_power, weights * (current[0] * current[0] + current[1] * current[1]), precision=highest) + epsilon
            current = damping * current + (1.0 - damping) * jnp.stack([numer_real / denom, numer_imag / denom])
        angles = steering_angles(beam_steering, channel[None], NIN, NCH)[0]
        cosine = jnp.cos(angles)
        sine_part = jnp.sin(angles)
        scale_factor = 1.0 / math.sqrt(NIN)
        gain_real = (gains_part[0] * weights)[None, :]
        gain_imaginary = (gains_part[1] * weights)[None, :]
        steering_real = ((gain_real * cosine - gain_imaginary * sine_part) * scale_factor).astype(jnp.bfloat16).astype(jnp.float32)
        steering_imaginary = ((gain_real * sine_part + gain_imaginary * cosine) * scale_factor).astype(jnp.bfloat16).astype(jnp.float32)
        volt_real = jnp.dot(steering_real, values[:, 0], precision=highest) - jnp.dot(steering_imaginary, values[:, 1], precision=highest)
        volt_imag = jnp.dot(steering_real, values[:, 1], precision=highest) + jnp.dot(steering_imaginary, values[:, 0], precision=highest)
        power = volt_real * volt_real + volt_imag * volt_imag
        return (vis_stored, current, power)
    results = lax.map(one_channel, (by_channel, sky_model, prior_gains, input_flags, channels))
    return (results[0], results[1], results[2])
```

```python
import functools
import math

import jax
import jax.numpy as jnp
from jax import lax
from jax.experimental import pallas as pl
from jax.experimental.pallas import tpu as pltpu
from jax.sharding import PartitionSpec as P

NCH = 512
ITERS = 2


damping = 0.5
epsilon = 1e-06
F32 = jnp.float32
BF16 = jnp.bfloat16


def from_behind(block, axis, distance):
    devices = range(lax.axis_size(axis))
    route = [(i - distance, i) for i in devices if i - distance in devices]
    return lax.ppermute(block, axis, route)


def unit_rows(rows, columns, transform_count):
    phases = (rows[:, None] * columns[None, :] % transform_count).astype(F32) * (
        2.0 * math.pi / transform_count
    )
    return jnp.cos(phases), jnp.sin(phases)


def transform_table(kept_count, transform_count):
    fine = 1 << ((kept_count.bit_length() - 1) // 2)
    coarse = kept_count // fine
    columns = jnp.arange(transform_count, dtype=jnp.int32)
    high_c, high_s = unit_rows(jnp.arange(coarse, dtype=jnp.int32) * fine, columns, transform_count)
    low_c, low_s = unit_rows(jnp.arange(fine, dtype=jnp.int32), columns, transform_count)
    high_c, high_s, low_c, low_s = lax.optimization_barrier((high_c, high_s, low_c, low_s))
    scale = 1.0 / math.sqrt(transform_count)
    high_c, high_s = high_c * scale, high_s * scale
    cosine = high_c[:, None] * low_c[None] - high_s[:, None] * low_s[None]
    sine = high_s[:, None] * low_c[None] + high_c[:, None] * low_s[None]
    cosine = cosine.reshape(kept_count, transform_count).astype(BF16)
    sine = sine.reshape(kept_count, transform_count).astype(BF16)
    return cosine, sine


def windowed_frames(samples, window_taps, beside):
    frames = samples.shape[3]
    tap_count = window_taps.shape[0]
    framed = jnp.transpose(samples, (3, 1, 0, 2))
    previous = from_behind(framed[frames - tap_count + 1 :], "tm", 1)
    previous, beside = lax.optimization_barrier((previous, beside))
    extended = jnp.concatenate([previous, framed], axis=0).astype(F32)
    windowed = sum(
        extended[tap : tap + frames] * window_taps[tap][None, None, None, :]
        for tap in range(tap_count)
    )
    return windowed.astype(BF16), beside


def filter_bank(samples, window_taps, kept_count, beside):
    local_inputs, _, transform_count, frames = samples.shape
    windowed, beside = windowed_frames(samples, window_taps, beside)
    real_in = windowed[:, 0].reshape(frames * local_inputs, transform_count)
    imag_in = windowed[:, 1].reshape(frames * local_inputs, transform_count)
    cosine, sine = transform_table(kept_count, transform_count)
    real = dot_nt(cosine, real_in) + dot_nt(sine, imag_in)
    imag = dot_nt(cosine, imag_in) - dot_nt(sine, real_in)
    return real.astype(BF16), imag.astype(BF16), beside


NT = (((1,), (1,)), ((), ()))
TN = (((0,), (0,)), ((), ()))


def dot_nt(a, b):
    return lax.dot_general(a, b, NT, preferred_element_type=F32)


def complex_product(left_r, left_i, vr, vi):
    straight = jnp.concatenate([vr, vi], axis=0).astype(BF16)
    crossed = jnp.concatenate([-vi, vr], axis=0).astype(BF16)
    return (dot_nt(left_r, straight) + dot_nt(left_i, crossed)).T


def numerators(x, own, model, gains, flags):
    half = x.shape[0] // 2
    hr, hi = gains[0:1] * flags, gains[1:2] * flags
    xr, xi = x[:half].astype(F32), x[half:].astype(F32)
    z = complex_product(model[0], model[1], xr * hr + xi * hi, xi * hr - xr * hi)
    zr, zi = z[:half], z[half:]
    pr, pi = own[:half].astype(F32), own[half:].astype(F32)
    numer_r = jnp.sum(pr * zr + pi * zi, axis=0, keepdims=True) * (1.0 / half)
    numer_i = jnp.sum(pi * zr - pr * zi, axis=0, keepdims=True) * (1.0 / half)
    return jnp.concatenate([numer_r, numer_i], axis=0)


def denominators(model, gains, flags):
    power = flags * (gains[0:1] * gains[0:1] + gains[1:2] * gains[1:2])
    top = power.astype(BF16).astype(F32)
    wide = (8, top.shape[1])
    both = jnp.concatenate(
        [jnp.broadcast_to(top, wide), jnp.broadcast_to(power - top, wide)], axis=0
    ).astype(BF16)
    mr, mi = model[0], model[1]
    d = dot_nt(mr * mr + mi * mi, both).T
    return d[0:1] + d[8:9] + epsilon


def damped(older, numer, denom):
    return damping * older + (1.0 - damping) * (numer / denom)


def denominator_kernel(model_ref, gain_ref, flag_ref, out_ref):
    for c in range(model_ref.shape[0]):
        out_ref[c] = denominators(model_ref.at[c], gain_ref[c], flag_ref[c].astype(F32))


def first_denominators(model, gains, flags):
    channels, _, mine, inputs = model.shape
    block = math.gcd(channels, 8)
    whole = lambda *shape: pl.BlockSpec((block, *shape), lambda c: (c,) + (0,) * len(shape))
    return pl.pallas_call(
        denominator_kernel,
        out_shape=jax.ShapeDtypeStruct((channels, 1, mine), F32),
        grid=(channels // block,),
        in_specs=[whole(2, mine, inputs), whole(2, inputs), whole(1, inputs)],
        out_specs=whole(1, mine),
        cost_estimate=pl.CostEstimate(
            flops=16 * model.size, bytes_accessed=2 * model.size, transcendentals=0
        ),
        name="denominators",
    )(model, gains, flags)


def correlate_kernel(beam_ref, x_ref, own_ref, model_ref, gain_ref, older_ref, flag_ref, denom_ref, vis_ref, new_ref):
    for c in range(x_ref.shape[0]):
        x, own = x_ref[c], own_ref[c]
        half = x.shape[0] // 2
        exact = half & (half - 1) == 0
        before, after = (1.0 / half, 1.0) if exact else (1.0, 1.0 / half)
        scaled = (own.astype(F32) * before).astype(BF16)
        rotated = jnp.concatenate([scaled[half:], -scaled[:half]], axis=0)
        for part, left in enumerate((scaled, rotated)):
            terms = lax.dot_general(left, x, TN, preferred_element_type=F32)
            vis_ref[c, part] = (terms if exact else terms * after).astype(BF16)
        numer = numerators(x, own, model_ref.at[c], gain_ref[c], flag_ref[c].astype(F32))
        new_ref[c] = damped(older_ref[c], numer, denom_ref[c])


def update_kernel(beam_ref, x_ref, own_ref, model_ref, gain_ref, older_ref, flag_ref, new_ref):
    for c in range(x_ref.shape[0]):
        model, gains, flags = model_ref.at[c], gain_ref[c], flag_ref[c].astype(F32)
        numer = numerators(x_ref[c], own_ref[c], model, gains, flags)
        new_ref[c] = damped(older_ref[c], numer, denominators(model, gains, flags))


def turn_kernel(me_ref, in_ref, out_ref, rows_ref, *, inputs, chans, times):
    beams, _, paired, lanes = in_ref.shape
    frames = lanes // inputs
    planes = times * frames
    width = rows_ref.shape[2]
    for b in range(beams):
        for z in range(chans):
            column = (z * beams + b) * inputs
            at = column % width
            for t in range(times):
                slab = in_ref[b ^ me_ref[1], (z * times + t) ^ me_ref[0]].astype(F32)
                for f in range(frames):
                    plane = t * frames + f
                    rows_ref[
                        column // width, plane * paired : (plane + 1) * paired, at : at + inputs
                    ] = slab[:, f * inputs : (f + 1) * inputs]

    def gather(k, carry):
        for q in range(rows_ref.shape[0]):
            parts = [
                rows_ref.at[q][pl.ds(s * (paired // 2) + k, planes, stride=paired), :]
                for s in range(2)
            ]
            out_ref[k, :, q * width : (q + 1) * width] = jnp.concatenate(parts, axis=0).astype(BF16)
        return carry

    lax.fori_loop(0, paired // 2, gather, 0)


def turn(me, joined, inputs, chans, times):
    beams, _, paired, lanes = joined.shape
    planes = times * (lanes // inputs)
    total = chans * beams * inputs
    width = 128
    whole = lambda *shape: pl.BlockSpec(shape, lambda c, m: (0,) * len(shape))
    out_dims = (paired // 2, 2 * planes, total)
    return pl.pallas_call(
        functools.partial(turn_kernel, inputs=inputs, chans=chans, times=times),
        out_shape=jax.ShapeDtypeStruct(out_dims, BF16),
        grid_spec=pltpu.PrefetchScalarGridSpec(
            num_scalar_prefetch=1,
            grid=(1,),
            in_specs=[whole(*joined.shape)],
            out_specs=whole(*out_dims),
            scratch_shapes=[pltpu.VMEM((total // width, planes * paired, width), F32)],
        ),
        cost_estimate=pl.CostEstimate(
            flops=0, bytes_accessed=8 * joined.size, transcendentals=0
        ),
        name="turn",
    )(me, joined)


def other_core(block):
    return lax.ppermute(block, "beam", [(0, 1), (1, 0)])


def exchange(blocks, me, axes):
    owners = blocks.shape[0]
    if owners > 8 or owners & (owners - 1):
        mixed = lax.all_to_all(blocks, axes, split_axis=0, concat_axis=0, tiled=True)
        return [mixed], jnp.zeros_like(me)
    parts = []
    for step in range(owners):
        block = lax.dynamic_slice_in_dim(blocks, me ^ step, 1, 0)
        if step:
            block = lax.ppermute(block, axes, [(i, i ^ step) for i in range(owners)])
        parts.append(block)
    return parts, me


def gain_call(beam_index, x, model, gains, older, flags, denom=None):
    correlate = denom is not None
    channels, rows, inputs = x.shape
    mine = model.shape[2]
    block = math.gcd(channels, 8)
    whole = lambda *shape: pl.BlockSpec((block, *shape), lambda c, b: (c,) + (0,) * len(shape))
    part = lambda r: pl.BlockSpec((block, r, mine), lambda c, b: (c, 0, b[0]))
    older_spec = part(2) if older.shape[2] == inputs else whole(2, mine)
    new_shape = jax.ShapeDtypeStruct((channels, 2, mine), F32)
    if correlate:
        out_shape = [jax.ShapeDtypeStruct(model.shape, BF16), new_shape]
        out_specs = [whole(2, mine, inputs), whole(2, mine)]
    else:
        out_shape, out_specs = new_shape, whole(2, mine)
    return pl.pallas_call(
        correlate_kernel if correlate else update_kernel,
        out_shape=out_shape,
        grid_spec=pltpu.PrefetchScalarGridSpec(
            num_scalar_prefetch=1,
            grid=(channels // block,),
            in_specs=[whole(rows, inputs), part(rows), whole(2, mine, inputs), whole(2, inputs),
                      older_spec, whole(1, inputs)] + [whole(1, mine)] * correlate,
            out_specs=out_specs,
        ),
        cost_estimate=pl.CostEstimate(
            flops=8 * channels * mine * inputs * rows,
            bytes_accessed=(4 + 4 * correlate) * model.size // 2,
            transcendentals=0,
        ),
        name="correlate" if correlate else "update",
    )(beam_index, x, x, model, gains, older, flags, *([denom] if correlate else []))


def steering_kernel(base_ref, bits_ref, rot_r, rot_i, cur_r, cur_i, one_r, one_i, *, unit):
    block = rot_r.shape[0]
    beams, inputs = cur_r.shape
    step = 16

    @pl.when(pl.program_id(0) == 0)
    def _():
        first = base_ref[0]

        def fill(r, carry):
            rows = pl.ds(r * 8, 8)
            bits = bits_ref[rows, :]
            angle = (bits * first).astype(F32) * unit
            cur_r[rows, :] = jnp.cos(angle)
            cur_i[rows, :] = jnp.sin(angle)
            small = bits.astype(F32) * unit
            one_r[rows, :] = jnp.cos(small)
            one_i[rows, :] = jnp.sin(small)
            return carry

        lax.fori_loop(0, beams // 8, fill, 0)

    def advance(r, carry):
        rows = pl.ds(r * step, step)
        ar, ai = cur_r[rows, :], cur_i[rows, :]
        br, bi = one_r[rows, :], one_i[rows, :]
        for c in range(block):
            rot_r[c, rows, :] = ar.astype(BF16)
            rot_i[c, rows, :] = ai.astype(BF16)
            ar, ai = ar * br - ai * bi, ar * bi + ai * br
        cur_r[rows, :] = ar
        cur_i[rows, :] = ai
        return carry

    lax.fori_loop(0, beams // step, advance, 0)


def steering(beam_steering, inputs, channels, first_channel, chan_total):
    beams = beam_steering.shape[1]
    positions = jnp.arange(inputs, dtype=jnp.int32)
    column = positions // (inputs // 4)
    within = positions % (inputs // 4)
    bits = (
        beam_steering[0][:, None] * column[None, :] * 64
        + beam_steering[1][:, None] * within[None, :]
    ) % 256
    block = math.gcd(channels, 8)
    rot = jax.ShapeDtypeStruct((channels, beams, inputs), BF16)
    rot_spec = pl.BlockSpec((block, beams, inputs), lambda c, b: (c, 0, 0))
    return pl.pallas_call(
        functools.partial(steering_kernel, unit=2.0 * math.pi / (512 * chan_total)),
        out_shape=[rot, rot],
        grid_spec=pltpu.PrefetchScalarGridSpec(
            num_scalar_prefetch=1,
            grid=(channels // block,),
            in_specs=[pl.BlockSpec((beams, inputs), lambda c, b: (0, 0))],
            out_specs=[rot_spec, rot_spec],
            scratch_shapes=[pltpu.VMEM((beams, inputs), F32)] * 4,
        ),
        cost_estimate=pl.CostEstimate(
            flops=8 * rot.size, bytes_accessed=6 * rot.size, transcendentals=0
        ),
        name="steering",
    )(jnp.reshape(chan_total + first_channel, (1,)), bits)


def beam_kernel(x_ref, gain_ref, flag_ref, rot_r, rot_i, power_ref, *, scale):
    for c in range(x_ref.shape[0]):
        x, gains = x_ref[c], gain_ref[c]
        flags = flag_ref[c].astype(F32) * scale
        half = x.shape[0] // 2
        hr, hi = gains[0:1] * flags, gains[1:2] * flags
        xr, xi = x[:half].astype(F32), x[half:].astype(F32)
        v = complex_product(rot_r[c], rot_i[c], xr * hr - xi * hi, xi * hr + xr * hi)
        vr, vi = v[:half], v[half:]
        power_ref[c] = vr * vr + vi * vi


def form_beams(x, gains, flags, rot_r, rot_i):
    channels, rows, inputs = x.shape
    beams = rot_r.shape[1]
    block = math.gcd(channels, 16)
    whole = lambda *shape: pl.BlockSpec((block, *shape), lambda c: (c,) + (0,) * len(shape))
    return pl.pallas_call(
        functools.partial(beam_kernel, scale=1.0 / math.sqrt(inputs)),
        out_shape=jax.ShapeDtypeStruct((channels, rows // 2, beams), F32),
        grid=(channels // block,),
        in_specs=[whole(rows, inputs), whole(2, inputs), whole(1, inputs),
                  whole(beams, inputs), whole(beams, inputs)],
        out_specs=whole(rows // 2, beams),
        cost_estimate=pl.CostEstimate(
            flops=8 * channels * beams * inputs * rows,
            bytes_accessed=4 * rot_r.size, transcendentals=0,
        ),
        name="beams",
    )(x, gains, flags, rot_r, rot_i)


def shards(samples, window_taps, sky_model, prior_gains, beam_steering, input_flags):
    local_inputs = samples.shape[0]
    frames = samples.shape[3]
    kept_count = NCH
    time_count = lax.axis_size("tm")
    chan_count = lax.axis_size("chan")
    beam_count = lax.axis_size("beam")
    owners = time_count * chan_count
    chan_local = kept_count // owners
    me = (lax.axis_index("chan") * time_count + lax.axis_index("tm")).astype(jnp.int32)
    flags = input_flags[:, None, :]
    denom = first_denominators(sky_model, prior_gains, flags)
    real, imag, denom = filter_bank(samples, window_taps, kept_count, denom)
    by_owner = (owners, chan_local, frames * local_inputs)
    spectra = jnp.concatenate([real.reshape(by_owner), imag.reshape(by_owner)], axis=1)
    spectra, beam_steering = lax.optimization_barrier((spectra, beam_steering))
    parts, origin = exchange(spectra, me, ("chan", "tm"))
    input_count = local_inputs * chan_count * beam_count
    rot_r, rot_i = steering(
        beam_steering, input_count, chan_local, me * chan_local, kept_count
    )
    parts, rot_r, rot_i = lax.optimization_barrier((parts, rot_r, rot_i))
    beam = lax.axis_index("beam").astype(jnp.int32)
    mixed = jnp.concatenate(parts, axis=0)
    if beam_count == 2:
        joined, core = jnp.stack([mixed, other_core(mixed)]), beam
    else:
        joined, core = lax.all_gather(mixed, "beam", axis=0), jnp.zeros_like(beam)
    x = turn(jnp.stack([origin, core]), joined, local_inputs, chan_count, time_count)
    beam_index = jnp.reshape(lax.axis_index("beam"), (1,)).astype(jnp.int32)
    visibilities, updated = gain_call(
        beam_index, x, sky_model, prior_gains, prior_gains, flags, denom
    )
    beam_power = form_beams(x, prior_gains, flags, rot_r, rot_i)
    for _ in range(ITERS - 1):
        if beam_count == 2:
            other, beam_power = lax.optimization_barrier((other_core(updated), beam_power))
            current = jnp.where(
                beam == 0,
                jnp.concatenate([updated, other], axis=2),
                jnp.concatenate([other, updated], axis=2),
            )
        else:
            current = lax.all_gather(updated, "beam", axis=2, tiled=True)
        updated = gain_call(beam_index, x, sky_model, current, updated, flags)
    return (visibilities, updated, jnp.transpose(beam_power, (0, 2, 1)))


SPAN = 16
MESH = pl.DeviceIdType.MESH


def row_product(vr, vi, left):
    straight = jnp.concatenate([vr, vi], axis=0).astype(BF16)
    crossed = jnp.concatenate([-vi, vr], axis=0).astype(BF16)
    return dot_nt(straight, left[0]) + dot_nt(crossed, left[1])


def row_numerators(x, own, model, gains, flags):
    half = x.shape[0] // 2
    hr, hi = gains[0:1] * flags, gains[1:2] * flags
    xr, xi = x[:half].astype(F32), x[half:].astype(F32)
    z = row_product(xr * hr + xi * hi, xi * hr - xr * hi, model)
    zr, zi = z[:half], z[half:]
    pr, pi = own[:half].astype(F32), own[half:].astype(F32)
    numer_r = jnp.sum(pr * zr + pi * zi, axis=0, keepdims=True) * (1.0 / half)
    numer_i = jnp.sum(pi * zr - pr * zi, axis=0, keepdims=True) * (1.0 / half)
    return jnp.concatenate([numer_r, numer_i], axis=0)


def row_denominators(model, gains, flags):
    power = flags * (gains[0:1] * gains[0:1] + gains[1:2] * gains[1:2])
    top = power.astype(BF16).astype(F32)
    wide = (8, top.shape[1])
    both = jnp.concatenate(
        [jnp.broadcast_to(top, wide), jnp.broadcast_to(power - top, wide)], axis=0
    ).astype(BF16)
    mr, mi = model[0], model[1]
    d = dot_nt(both, mr * mr + mi * mi)
    return d[0:1] + d[8:9] + epsilon


def spectra_kernel(win_ref, cos_ref, sin_ref, out_ref, real_ref, imag_ref, rows_ref):
    owners, chunks, pairs, rows, lanes = out_ref.shape
    cosine, sine = cos_ref[...], sin_ref[...]
    real_ref[...] = dot_nt(cosine, win_ref[0]) + dot_nt(sine, win_ref[1])
    imag_ref[...] = dot_nt(cosine, win_ref[1]) - dot_nt(sine, win_ref[0])
    half = lanes // 2
    frames = rows // 2

    def pack(step, carry):
        base = step * 2 * pairs
        for s, ref in enumerate((real_ref, imag_ref)):
            for tile in range(frames // 2):
                at = slice(tile * lanes, (tile + 1) * lanes)
                low = ref[pl.ds(pl.multiple_of(base, pairs), pairs), at]
                high = ref[pl.ds(pl.multiple_of(base + pairs, pairs), pairs), at]
                for f, cut in enumerate((slice(0, half), slice(half, lanes))):
                    joined = jnp.concatenate([low[:, cut], high[:, cut]], axis=1)
                    row = s * frames + 2 * tile + f
                    rows_ref[pl.ds(row, pairs, stride=rows), :] = joined
        packed = rows_ref[...].reshape(pairs, rows, lanes).astype(BF16)
        out_ref[step // chunks, step % chunks] = packed
        return carry

    lax.fori_loop(0, owners * chunks, pack, 0)


def local_spectra(windowed, window_count, kept_count, owners):
    frames, _, local_inputs, transform_count = windowed.shape
    columns = frames * local_inputs
    win = jnp.transpose(windowed, (1, 0, 2, 3)).reshape(2, columns, transform_count)
    cosine, sine = transform_table(kept_count, transform_count)
    chunks = kept_count // owners // SPAN
    dims = (owners, chunks, SPAN // 2, 2 * frames, 2 * local_inputs)
    vmem = pl.BlockSpec(memory_space=pltpu.VMEM)
    return pl.pallas_call(
        spectra_kernel,
        out_shape=jax.ShapeDtypeStruct(dims, BF16),
        in_specs=[vmem] * 3,
        out_specs=vmem,
        scratch_shapes=[pltpu.VMEM((kept_count, columns), F32)] * 2
        + [pltpu.VMEM((SPAN // 2 * 2 * frames, 2 * local_inputs), F32)],
        cost_estimate=pl.CostEstimate(
            flops=8 * kept_count * columns * transform_count,
            bytes_accessed=8 * win.size, transcendentals=0,
        ),
        name="spectra",
    )(win, cosine, sine)


def gains_kernel(
    send_ref, model_hbm, gain_ref, flag_ref, denom_ref, x_ref, new_ref, recv, model, full,
    send_sem, recv_sem, keep_sem, pass_send, pass_recv, gain_send, gain_recv, load_sem,
    *, chans, times,
):
    z, t, b = lax.axis_index("chan"), lax.axis_index("tm"), lax.axis_index("beam")
    owners, chunks, pairs, rows, lanes = send_ref.shape
    mine = model.shape[2]
    me = z * times + t
    off = pl.multiple_of(b * mine, mine)
    frames, half = rows // 2, lanes // 2
    other = {"beam": 1 - b}

    def place(step):
        device = lax.rem(me + step, owners)
        return device, {"chan": lax.div(device, times), "tm": lax.rem(device, times)}

    barrier = pltpu.get_barrier_semaphore()
    for step in range(1, owners):
        pl.semaphore_signal(barrier, inc=1, device_id=place(step)[1], device_id_type=MESH)
    pl.semaphore_signal(barrier, inc=1, device_id=other, device_id_type=MESH)

    def load(q):
        part = pl.ds(q * SPAN, SPAN)
        return pltpu.make_async_copy(model_hbm.at[part], model.at[part], load_sem.at[q])

    for q in range(chunks):
        load(q).start()
    pl.semaphore_wait(barrier, owners)

    def outgoing(q, step):
        device, where = place(step)
        return pltpu.make_async_remote_copy(
            src_ref=send_ref.at[device, q], dst_ref=recv.at[b, q, me],
            send_sem=send_sem.at[q, step - 1], recv_sem=recv_sem.at[q, step - 1],
            device_id=where, device_id_type=MESH,
        )

    def incoming(q, step):
        device, where = place(owners - step)
        return pltpu.make_async_remote_copy(
            src_ref=send_ref.at[device, q], dst_ref=recv.at[b, q, device],
            send_sem=send_sem.at[q, step - 1], recv_sem=recv_sem.at[q, step - 1],
            device_id=where, device_id_type=MESH,
        )

    def keep(q):
        return pltpu.make_async_copy(send_ref.at[me, q], recv.at[b, q, me], keep_sem.at[q])

    def passing(q, core):
        return pltpu.make_async_remote_copy(
            src_ref=recv.at[core, q], dst_ref=recv.at[core, q],
            send_sem=pass_send.at[q], recv_sem=pass_recv.at[q],
            device_id=other, device_id_type=MESH,
        )

    def sharing(q, start):
        part = full.at[pl.ds(q * SPAN, SPAN), :, pl.ds(start, mine)]
        return pltpu.make_async_remote_copy(
            src_ref=part, dst_ref=part,
            send_sem=gain_send.at[q], recv_sem=gain_recv.at[q],
            device_id=other, device_id_type=MESH,
        )

    def send(q, carry):
        for step in range(1, owners):
            outgoing(q, step).start()
        keep(q).start()
        return carry

    lax.fori_loop(0, chunks, send, 0)

    def collect(q):
        for step in range(1, owners):
            incoming(q, step).wait_recv()
        keep(q).wait()
        passing(q, b).start()

    def merge(q):
        def pair(p, carry):
            for zz in range(chans):
                sides = []
                for core in range(2):
                    got = [recv[core, q, zz * times + tt, p].astype(F32) for tt in range(times)]
                    sides.append(jnp.concatenate(
                        [r[:frames] for r in got] + [r[frames:] for r in got], axis=0))
                at = slice(zz * lanes, (zz + 1) * lanes)
                for k, cut in enumerate((slice(0, half), slice(half, lanes))):
                    joined = jnp.concatenate([side[:, cut] for side in sides], axis=1)
                    x_ref[q * SPAN + k * pairs + p, :, at] = joined.astype(BF16)
            return carry

        lax.fori_loop(0, pairs, pair, 0)

    def first(c):
        flags = flag_ref[c].astype(F32)
        own = x_ref[c, :, pl.ds(off, mine)]
        numer = row_numerators(x_ref[c], own, model.at[c], gain_ref[c], flags)
        older = gain_ref[c, :, pl.ds(off, mine)]
        full[c, :, pl.ds(off, mine)] = damped(older, numer, denom_ref[c])

    def second(c):
        flags, gains = flag_ref[c].astype(F32), full[c]
        own = x_ref[c, :, pl.ds(off, mine)]
        numer = row_numerators(x_ref[c], own, model.at[c], gains, flags)
        denom = row_denominators(model.at[c], gains, flags)
        new_ref[c] = damped(full[c, :, pl.ds(off, mine)], numer, denom)

    def each(stage, start, count):
        block = 4

        def body(i, carry):
            for j in range(block):
                stage(start + i * block + j)
            return carry

        lax.fori_loop(0, count // block, body, 0)

    collect(0)

    def chunk(q, carry):
        @pl.when(q < chunks)
        def _():
            passing(q, 1 - b).wait_recv()
            merge(q)
            load(q).wait()
            each(first, q * SPAN, SPAN)

        @pl.when(q >= 1)
        def _():
            sharing(q - 1, pl.multiple_of((1 - b) * mine, mine)).wait_recv()
            each(second, (q - 1) * SPAN, SPAN // 2)

        @pl.when(q < chunks)
        def _():
            sharing(q, off).start()

        @pl.when(q + 1 < chunks)
        def _():
            collect(q + 1)

        @pl.when(q >= 1)
        def _():
            each(second, (q - 1) * SPAN + SPAN // 2, SPAN // 2)

        return carry

    lax.fori_loop(0, chunks + 1, chunk, 0)

    def drain(q, carry):
        for step in range(1, owners):
            outgoing(q, step).wait_send()
        passing(q, b).wait_send()
        sharing(q, off).wait_send()
        return carry

    lax.fori_loop(0, chunks, drain, 0)


def solve_gains(blocks, model, gains, flags, denom, chans, times):
    owners, chunks, pairs, rows, lanes = blocks.shape
    channels, _, mine, inputs = model.shape
    vmem = pl.BlockSpec(memory_space=pltpu.VMEM)
    dma = pltpu.SemaphoreType.DMA
    return pl.pallas_call(
        functools.partial(gains_kernel, chans=chans, times=times),
        out_shape=[
            jax.ShapeDtypeStruct((channels, times * rows, inputs), BF16),
            jax.ShapeDtypeStruct((channels, 2, mine), F32),
        ],
        in_specs=[vmem, pl.BlockSpec(memory_space=pl.ANY), vmem, vmem, vmem],
        out_specs=[vmem, vmem],
        scratch_shapes=[
            pltpu.VMEM((2, chunks, owners, pairs, rows, lanes), BF16),
            pltpu.VMEM(model.shape, BF16),
            pltpu.VMEM((channels, 2, inputs), F32),
            dma((chunks, owners - 1)), dma((chunks, owners - 1)), dma((chunks,)),
            dma((chunks,)), dma((chunks,)), dma((chunks,)), dma((chunks,)), dma((chunks,)),
        ],
        compiler_params=pltpu.CompilerParams(
            collective_id=0, has_side_effects=True, vmem_limit_bytes=60 << 20
        ),
        cost_estimate=pl.CostEstimate(
            flops=24 * channels * mine * inputs * rows * times,
            bytes_accessed=2 * model.size, transcendentals=0,
        ),
        name="gains",
    )(blocks, model, gains, flags, denom)


def correlate_only_kernel(beam_ref, x_ref, own_ref, new_in, vis_ref, new_out):
    for c in range(x_ref.shape[0]):
        x, own = x_ref[c], own_ref[c]
        half = x.shape[0] // 2
        exact = half & (half - 1) == 0
        before, after = (1.0 / half, 1.0) if exact else (1.0, 1.0 / half)
        scaled = (own.astype(F32) * before).astype(BF16)
        rotated = jnp.concatenate([scaled[half:], -scaled[:half]], axis=0)
        for part, left in enumerate((scaled, rotated)):
            terms = lax.dot_general(left, x, TN, preferred_element_type=F32)
            vis_ref[c, part] = (terms if exact else terms * after).astype(BF16)
    new_out[...] = new_in[...]


def correlate(beam_index, x, new):
    channels, rows, inputs = x.shape
    mine = new.shape[2]
    block = math.gcd(channels, 8)
    whole = lambda *shape: pl.BlockSpec((block, *shape), lambda c, b: (c,) + (0,) * len(shape))
    part = lambda r: pl.BlockSpec((block, r, mine), lambda c, b: (c, 0, b[0]))
    return pl.pallas_call(
        correlate_only_kernel,
        out_shape=[
            jax.ShapeDtypeStruct((channels, 2, mine, inputs), BF16),
            jax.ShapeDtypeStruct(new.shape, F32),
        ],
        grid_spec=pltpu.PrefetchScalarGridSpec(
            num_scalar_prefetch=1,
            grid=(channels // block,),
            in_specs=[whole(rows, inputs), part(rows), whole(2, mine)],
            out_specs=[whole(2, mine, inputs), whole(2, mine)],
        ),
        cost_estimate=pl.CostEstimate(
            flops=4 * channels * mine * inputs * rows,
            bytes_accessed=4 * channels * mine * inputs, transcendentals=0,
        ),
        name="correlate_only",
    )(beam_index, x, x, new)


def series_terms(channels, chan_total):
    reach = 128 * (channels / 2) * 2.0 * math.pi / (512 * chan_total)
    terms, left = 1, reach
    while left >= 2.0**-23:
        terms += 1
        left *= reach / terms
    return terms


def table_kernel(base_ref, bits_ref, out_ref, *, unit, reach):
    terms, _, wide = out_ref.shape
    inputs = wide // 2
    index = bits_ref[...] - 128
    angle = (index * base_ref[0]).astype(F32) * (0.5 * unit)
    real, imag = jnp.cos(angle), jnp.sin(angle)
    turned = index.astype(F32) * reach
    for k in range(terms):
        if k:
            scale = turned * (1.0 / k)
            real, imag = real * scale, imag * scale
        out_ref[k, :, :inputs] = real.astype(BF16)
        out_ref[k, :, inputs:] = imag.astype(BF16)


def steering_tables(beam_steering, inputs, channels, first_channel, chan_total):
    beams = beam_steering.shape[1]
    positions = jnp.arange(inputs, dtype=jnp.int32)
    column = positions // (inputs // 4)
    within = positions % (inputs // 4)
    bits = (
        beam_steering[0][:, None] * column[None, :] * 64
        + beam_steering[1][:, None] * within[None, :]
    ) % 256
    terms = series_terms(channels, chan_total)
    unit = 2.0 * math.pi / (512 * chan_total)
    block = math.gcd(beams, 32)
    middle = 2 * (chan_total + first_channel) + channels - 1
    return pl.pallas_call(
        functools.partial(table_kernel, unit=unit, reach=unit * channels / 2),
        out_shape=jax.ShapeDtypeStruct((terms, beams, 2 * inputs), BF16),
        grid_spec=pltpu.PrefetchScalarGridSpec(
            num_scalar_prefetch=1,
            grid=(beams // block,),
            in_specs=[pl.BlockSpec((block, inputs), lambda r, m: (r, 0))],
            out_specs=pl.BlockSpec((terms, block, 2 * inputs), lambda r, m: (0, r, 0)),
        ),
        cost_estimate=pl.CostEstimate(
            flops=100 * beams * inputs, bytes_accessed=16 * beams * inputs, transcendentals=0
        ),
        name="tables",
    )(jnp.reshape(middle, (1,)).astype(jnp.int32), bits)


def series_kernel(x_ref, gain_ref, flag_ref, table_ref, power_ref, y_ref, sum_ref, *, scale, channels):
    block, rows, inputs = x_ref.shape
    half = rows // 2
    terms = table_ref.shape[0]

    def prepare(c, carry):
        x, gains = x_ref[c], gain_ref[c]
        flags = flag_ref[c].astype(F32) * scale
        hr, hi = gains[0:1] * flags, gains[1:2] * flags
        xr, xi = x[:half].astype(F32), x[half:].astype(F32)
        yr = (xr * hr - xi * hi).astype(BF16)
        yi = (xi * hr + xr * hi).astype(BF16)
        y_ref[c, :half, :inputs] = yr
        y_ref[c, :half, inputs:] = -yi
        y_ref[c, half:, :inputs] = yi
        y_ref[c, half:, inputs:] = yr
        return carry

    lax.fori_loop(0, block, prepare, 0)
    y = y_ref[...].reshape(block * rows, 2 * inputs)
    for k in range(terms):
        sum_ref[k] = dot_nt(y, table_ref[k])
    start = pl.program_id(0) * block

    def finish(c, carry):
        u = ((start + c).astype(F32) - (channels - 1) / 2) * (2.0 / channels)
        at = pl.ds(pl.multiple_of(c * rows, rows), rows)
        last = sum_ref[terms - 1, at, :]
        vr, vi = last[:half], last[half:]
        for k in reversed(range(terms - 1)):
            term = sum_ref[k, at, :]
            vr, vi = term[:half] - u * vi, term[half:] + u * vr
        power_ref[c] = vr * vr + vi * vi
        return carry

    lax.fori_loop(0, block, finish, 0)


def series_beams(x, gains, flags, table):
    channels, rows, inputs = x.shape
    terms, beams, wide = table.shape
    block = math.gcd(channels, 32)
    whole = lambda *shape: pl.BlockSpec((block, *shape), lambda c: (c,) + (0,) * len(shape))
    return pl.pallas_call(
        functools.partial(series_kernel, scale=1.0 / math.sqrt(inputs), channels=channels),
        out_shape=jax.ShapeDtypeStruct((channels, rows // 2, beams), F32),
        grid=(channels // block,),
        in_specs=[whole(rows, inputs), whole(2, inputs), whole(1, inputs),
                  pl.BlockSpec(table.shape, lambda c: (0, 0, 0))],
        out_specs=whole(rows // 2, beams),
        scratch_shapes=[pltpu.VMEM((block, rows, wide), BF16),
                        pltpu.VMEM((terms, block * rows, beams), F32)],
        cost_estimate=pl.CostEstimate(
            flops=4 * terms * channels * beams * inputs * rows,
            bytes_accessed=2 * x.size + 2 * table.size, transcendentals=0,
        ),
        name="series",
    )(x, gains, flags, table)


def tiled_shards(samples, window_taps, sky_model, prior_gains, beam_steering, input_flags):
    local_inputs = samples.shape[0]
    kept_count = NCH
    time_count = lax.axis_size("tm")
    chan_count = lax.axis_size("chan")
    owners = time_count * chan_count
    chan_local = kept_count // owners
    inputs = local_inputs * chan_count * 2
    me = (lax.axis_index("chan") * time_count + lax.axis_index("tm")).astype(jnp.int32)
    flags = input_flags[:, None, :]
    denom = first_denominators(sky_model, prior_gains, flags)
    table = steering_tables(beam_steering, inputs, chan_local, me * chan_local, kept_count)
    windowed, (denom, table) = windowed_frames(samples, window_taps, (denom, table))
    blocks = local_spectra(windowed, window_taps.shape[0], kept_count, owners)
    x, new = solve_gains(blocks, sky_model, prior_gains, flags, denom, chan_count, time_count)
    beam_index = jnp.reshape(lax.axis_index("beam"), (1,)).astype(jnp.int32)
    visibilities, new = correlate(beam_index, x, new)
    power = series_beams(x, prior_gains, flags, table)
    return visibilities, new, jnp.transpose(power, (0, 2, 1))


def tiles(samples, window_taps, sky_model, prior_gains, beam_steering, input_flags):
    owners = lax.axis_size("tm") * lax.axis_size("chan")
    local_inputs, frames = samples.shape[0], samples.shape[3]
    return (
        ITERS == 2
        and lax.axis_size("beam") == 2
        and owners > 1
        and 2 * local_inputs == 128
        and frames == 8
        and lax.axis_size("tm") % 2 == 0
        and NCH % (owners * SPAN) == 0
        and sky_model.size <= 1 << 24
    )


def any_shards(*args):
    return tiled_shards(*args) if tiles(*args) else shards(*args)


def solution(mesh):
    return jax.shard_map(
        any_shards,
        mesh=mesh,
        in_specs=(
            P(("group", "chan", "beam"), None, None, "tm"),
            P(),
            P(("group", "chan", "tm"), None, "beam", None),
            P(("group", "chan", "tm"), None, None),
            P(None, ("group", "beam")),
            P(("group", "chan", "tm"), None),
        ),
        out_specs=(
            P(("group", "chan", "tm"), None, "beam", None),
            P(("group", "chan", "tm"), None, "beam"),
            P(("group", "chan", "tm"), "beam", None),
        ),
        check_vma=False,
    )
```

```python
import functools
import math

import jax
import jax.numpy as jnp
from jax import lax
from jax.experimental import pallas as pl
from jax.experimental.pallas import tpu as pltpu
from jax.sharding import PartitionSpec as P

NCH = 512
ITERS = 2


damping = 0.5
epsilon = 1e-06
F32 = jnp.float32
BF16 = jnp.bfloat16


def from_behind(block, axis, distance):
    devices = range(lax.axis_size(axis))
    route = [(i - distance, i) for i in devices if i - distance in devices]
    return lax.ppermute(block, axis, route)


def unit_rows(rows, columns, transform_count):
    phases = (rows[:, None] * columns[None, :] % transform_count).astype(F32) * (
        2.0 * math.pi / transform_count
    )
    return jnp.cos(phases), jnp.sin(phases)


def transform_rows(kept_count, transform_count):
    fine = 1 << ((kept_count.bit_length() - 1) // 2)
    coarse = kept_count // fine
    columns = jnp.arange(transform_count, dtype=jnp.int32)
    high_c, high_s = unit_rows(jnp.arange(coarse, dtype=jnp.int32) * fine, columns, transform_count)
    low_c, low_s = unit_rows(jnp.arange(fine, dtype=jnp.int32), columns, transform_count)
    high_c, high_s, low_c, low_s = lax.optimization_barrier((high_c, high_s, low_c, low_s))
    scale = 1.0 / math.sqrt(transform_count)
    return high_c * scale, high_s * scale, low_c, low_s


def transform_table(kept_count, transform_count):
    high_c, high_s, low_c, low_s = transform_rows(kept_count, transform_count)
    cosine = high_c[:, None] * low_c[None] - high_s[:, None] * low_s[None]
    sine = high_s[:, None] * low_c[None] + high_c[:, None] * low_s[None]
    cosine = cosine.reshape(kept_count, transform_count).astype(BF16)
    sine = sine.reshape(kept_count, transform_count).astype(BF16)
    return cosine, sine


def windowed_frames(samples, window_taps, beside):
    frames = samples.shape[3]
    tap_count = window_taps.shape[0]
    framed = jnp.transpose(samples, (3, 1, 0, 2))
    previous = from_behind(framed[frames - tap_count + 1 :], "tm", 1)
    previous, beside = lax.optimization_barrier((previous, beside))
    extended = jnp.concatenate([previous, framed], axis=0).astype(F32)
    windowed = sum(
        extended[tap : tap + frames] * window_taps[tap][None, None, None, :]
        for tap in range(tap_count)
    )
    return windowed.astype(BF16), beside


def filter_bank(samples, window_taps, kept_count, beside):
    local_inputs, _, transform_count, frames = samples.shape
    windowed, beside = windowed_frames(samples, window_taps, beside)
    real_in = windowed[:, 0].reshape(frames * local_inputs, transform_count)
    imag_in = windowed[:, 1].reshape(frames * local_inputs, transform_count)
    cosine, sine = transform_table(kept_count, transform_count)
    real = dot_nt(cosine, real_in) + dot_nt(sine, imag_in)
    imag = dot_nt(cosine, imag_in) - dot_nt(sine, real_in)
    return real.astype(BF16), imag.astype(BF16), beside


NT = (((1,), (1,)), ((), ()))
TN = (((0,), (0,)), ((), ()))


def dot_nt(a, b):
    return lax.dot_general(a, b, NT, preferred_element_type=F32)


def complex_product(left_r, left_i, vr, vi):
    straight = jnp.concatenate([vr, vi], axis=0).astype(BF16)
    crossed = jnp.concatenate([-vi, vr], axis=0).astype(BF16)
    return (dot_nt(left_r, straight) + dot_nt(left_i, crossed)).T


def numerators(x, own, model, gains, flags):
    half = x.shape[0] // 2
    hr, hi = gains[0:1] * flags, gains[1:2] * flags
    xr, xi = x[:half].astype(F32), x[half:].astype(F32)
    z = complex_product(model[0], model[1], xr * hr + xi * hi, xi * hr - xr * hi)
    zr, zi = z[:half], z[half:]
    pr, pi = own[:half].astype(F32), own[half:].astype(F32)
    numer_r = jnp.sum(pr * zr + pi * zi, axis=0, keepdims=True) * (1.0 / half)
    numer_i = jnp.sum(pi * zr - pr * zi, axis=0, keepdims=True) * (1.0 / half)
    return jnp.concatenate([numer_r, numer_i], axis=0)


def denominators(model, gains, flags):
    power = flags * (gains[0:1] * gains[0:1] + gains[1:2] * gains[1:2])
    top = power.astype(BF16).astype(F32)
    wide = (8, top.shape[1])
    both = jnp.concatenate(
        [jnp.broadcast_to(top, wide), jnp.broadcast_to(power - top, wide)], axis=0
    ).astype(BF16)
    mr, mi = model[0], model[1]
    d = dot_nt(mr * mr + mi * mi, both).T
    return d[0:1] + d[8:9] + epsilon


def damped(older, numer, denom):
    return damping * older + (1.0 - damping) * (numer / denom)


def denominator_kernel(model_ref, gain_ref, flag_ref, out_ref):
    for c in range(model_ref.shape[0]):
        out_ref[c] = denominators(model_ref.at[c], gain_ref[c], flag_ref[c].astype(F32))


def first_denominators(model, gains, flags):
    channels, _, mine, inputs = model.shape
    block = math.gcd(channels, 8)
    whole = lambda *shape: pl.BlockSpec((block, *shape), lambda c: (c,) + (0,) * len(shape))
    return pl.pallas_call(
        denominator_kernel,
        out_shape=jax.ShapeDtypeStruct((channels, 1, mine), F32),
        grid=(channels // block,),
        in_specs=[whole(2, mine, inputs), whole(2, inputs), whole(1, inputs)],
        out_specs=whole(1, mine),
        cost_estimate=pl.CostEstimate(
            flops=16 * model.size, bytes_accessed=2 * model.size, transcendentals=0
        ),
        name="denominators",
    )(model, gains, flags)


def correlate_kernel(beam_ref, x_ref, own_ref, model_ref, gain_ref, older_ref, flag_ref, denom_ref, vis_ref, new_ref):
    for c in range(x_ref.shape[0]):
        x, own = x_ref[c], own_ref[c]
        half = x.shape[0] // 2
        exact = half & (half - 1) == 0
        before, after = (1.0 / half, 1.0) if exact else (1.0, 1.0 / half)
        scaled = (own.astype(F32) * before).astype(BF16)
        rotated = jnp.concatenate([scaled[half:], -scaled[:half]], axis=0)
        for part, left in enumerate((scaled, rotated)):
            terms = lax.dot_general(left, x, TN, preferred_element_type=F32)
            vis_ref[c, part] = (terms if exact else terms * after).astype(BF16)
        numer = numerators(x, own, model_ref.at[c], gain_ref[c], flag_ref[c].astype(F32))
        new_ref[c] = damped(older_ref[c], numer, denom_ref[c])


def update_kernel(beam_ref, x_ref, own_ref, model_ref, gain_ref, older_ref, flag_ref, new_ref):
    for c in range(x_ref.shape[0]):
        model, gains, flags = model_ref.at[c], gain_ref[c], flag_ref[c].astype(F32)
        numer = numerators(x_ref[c], own_ref[c], model, gains, flags)
        new_ref[c] = damped(older_ref[c], numer, denominators(model, gains, flags))


def turn_kernel(me_ref, in_ref, out_ref, rows_ref, *, inputs, chans, times):
    beams, _, paired, lanes = in_ref.shape
    frames = lanes // inputs
    planes = times * frames
    width = rows_ref.shape[2]
    for b in range(beams):
        for z in range(chans):
            column = (z * beams + b) * inputs
            at = column % width
            for t in range(times):
                slab = in_ref[b ^ me_ref[1], (z * times + t) ^ me_ref[0]].astype(F32)
                for f in range(frames):
                    plane = t * frames + f
                    rows_ref[
                        column // width, plane * paired : (plane + 1) * paired, at : at + inputs
                    ] = slab[:, f * inputs : (f + 1) * inputs]

    def gather(k, carry):
        for q in range(rows_ref.shape[0]):
            parts = [
                rows_ref.at[q][pl.ds(s * (paired // 2) + k, planes, stride=paired), :]
                for s in range(2)
            ]
            out_ref[k, :, q * width : (q + 1) * width] = jnp.concatenate(parts, axis=0).astype(BF16)
        return carry

    lax.fori_loop(0, paired // 2, gather, 0)


def turn(me, joined, inputs, chans, times):
    beams, _, paired, lanes = joined.shape
    planes = times * (lanes // inputs)
    total = chans * beams * inputs
    width = 128
    whole = lambda *shape: pl.BlockSpec(shape, lambda c, m: (0,) * len(shape))
    out_dims = (paired // 2, 2 * planes, total)
    return pl.pallas_call(
        functools.partial(turn_kernel, inputs=inputs, chans=chans, times=times),
        out_shape=jax.ShapeDtypeStruct(out_dims, BF16),
        grid_spec=pltpu.PrefetchScalarGridSpec(
            num_scalar_prefetch=1,
            grid=(1,),
            in_specs=[whole(*joined.shape)],
            out_specs=whole(*out_dims),
            scratch_shapes=[pltpu.VMEM((total // width, planes * paired, width), F32)],
        ),
        cost_estimate=pl.CostEstimate(
            flops=0, bytes_accessed=8 * joined.size, transcendentals=0
        ),
        name="turn",
    )(me, joined)


def other_core(block):
    return lax.ppermute(block, "beam", [(0, 1), (1, 0)])


def exchange(blocks, me, axes):
    owners = blocks.shape[0]
    if owners > 8 or owners & (owners - 1):
        mixed = lax.all_to_all(blocks, axes, split_axis=0, concat_axis=0, tiled=True)
        return [mixed], jnp.zeros_like(me)
    parts = []
    for step in range(owners):
        block = lax.dynamic_slice_in_dim(blocks, me ^ step, 1, 0)
        if step:
            block = lax.ppermute(block, axes, [(i, i ^ step) for i in range(owners)])
        parts.append(block)
    return parts, me


def gain_call(beam_index, x, model, gains, older, flags, denom=None):
    correlate = denom is not None
    channels, rows, inputs = x.shape
    mine = model.shape[2]
    block = math.gcd(channels, 8)
    whole = lambda *shape: pl.BlockSpec((block, *shape), lambda c, b: (c,) + (0,) * len(shape))
    part = lambda r: pl.BlockSpec((block, r, mine), lambda c, b: (c, 0, b[0]))
    older_spec = part(2) if older.shape[2] == inputs else whole(2, mine)
    new_shape = jax.ShapeDtypeStruct((channels, 2, mine), F32)
    if correlate:
        out_shape = [jax.ShapeDtypeStruct(model.shape, BF16), new_shape]
        out_specs = [whole(2, mine, inputs), whole(2, mine)]
    else:
        out_shape, out_specs = new_shape, whole(2, mine)
    return pl.pallas_call(
        correlate_kernel if correlate else update_kernel,
        out_shape=out_shape,
        grid_spec=pltpu.PrefetchScalarGridSpec(
            num_scalar_prefetch=1,
            grid=(channels // block,),
            in_specs=[whole(rows, inputs), part(rows), whole(2, mine, inputs), whole(2, inputs),
                      older_spec, whole(1, inputs)] + [whole(1, mine)] * correlate,
            out_specs=out_specs,
        ),
        cost_estimate=pl.CostEstimate(
            flops=8 * channels * mine * inputs * rows,
            bytes_accessed=(4 + 4 * correlate) * model.size // 2,
            transcendentals=0,
        ),
        name="correlate" if correlate else "update",
    )(beam_index, x, x, model, gains, older, flags, *([denom] if correlate else []))


def steering_kernel(base_ref, bits_ref, rot_r, rot_i, cur_r, cur_i, one_r, one_i, *, unit):
    block = rot_r.shape[0]
    beams, inputs = cur_r.shape
    step = 16

    @pl.when(pl.program_id(0) == 0)
    def _():
        first = base_ref[0]

        def fill(r, carry):
            rows = pl.ds(r * 8, 8)
            bits = bits_ref[rows, :]
            angle = (bits * first).astype(F32) * unit
            cur_r[rows, :] = jnp.cos(angle)
            cur_i[rows, :] = jnp.sin(angle)
            small = bits.astype(F32) * unit
            one_r[rows, :] = jnp.cos(small)
            one_i[rows, :] = jnp.sin(small)
            return carry

        lax.fori_loop(0, beams // 8, fill, 0)

    def advance(r, carry):
        rows = pl.ds(r * step, step)
        ar, ai = cur_r[rows, :], cur_i[rows, :]
        br, bi = one_r[rows, :], one_i[rows, :]
        for c in range(block):
            rot_r[c, rows, :] = ar.astype(BF16)
            rot_i[c, rows, :] = ai.astype(BF16)
            ar, ai = ar * br - ai * bi, ar * bi + ai * br
        cur_r[rows, :] = ar
        cur_i[rows, :] = ai
        return carry

    lax.fori_loop(0, beams // step, advance, 0)


def steering(beam_steering, inputs, channels, first_channel, chan_total):
    beams = beam_steering.shape[1]
    positions = jnp.arange(inputs, dtype=jnp.int32)
    column = positions // (inputs // 4)
    within = positions % (inputs // 4)
    bits = (
        beam_steering[0][:, None] * column[None, :] * 64
        + beam_steering[1][:, None] * within[None, :]
    ) % 256
    block = math.gcd(channels, 8)
    rot = jax.ShapeDtypeStruct((channels, beams, inputs), BF16)
    rot_spec = pl.BlockSpec((block, beams, inputs), lambda c, b: (c, 0, 0))
    return pl.pallas_call(
        functools.partial(steering_kernel, unit=2.0 * math.pi / (512 * chan_total)),
        out_shape=[rot, rot],
        grid_spec=pltpu.PrefetchScalarGridSpec(
            num_scalar_prefetch=1,
            grid=(channels // block,),
            in_specs=[pl.BlockSpec((beams, inputs), lambda c, b: (0, 0))],
            out_specs=[rot_spec, rot_spec],
            scratch_shapes=[pltpu.VMEM((beams, inputs), F32)] * 4,
        ),
        cost_estimate=pl.CostEstimate(
            flops=8 * rot.size, bytes_accessed=6 * rot.size, transcendentals=0
        ),
        name="steering",
    )(jnp.reshape(chan_total + first_channel, (1,)), bits)


def beam_kernel(x_ref, gain_ref, flag_ref, rot_r, rot_i, power_ref, *, scale):
    for c in range(x_ref.shape[0]):
        x, gains = x_ref[c], gain_ref[c]
        flags = flag_ref[c].astype(F32) * scale
        half = x.shape[0] // 2
        hr, hi = gains[0:1] * flags, gains[1:2] * flags
        xr, xi = x[:half].astype(F32), x[half:].astype(F32)
        v = complex_product(rot_r[c], rot_i[c], xr * hr - xi * hi, xi * hr + xr * hi)
        vr, vi = v[:half], v[half:]
        power_ref[c] = vr * vr + vi * vi


def form_beams(x, gains, flags, rot_r, rot_i):
    channels, rows, inputs = x.shape
    beams = rot_r.shape[1]
    block = math.gcd(channels, 16)
    whole = lambda *shape: pl.BlockSpec((block, *shape), lambda c: (c,) + (0,) * len(shape))
    return pl.pallas_call(
        functools.partial(beam_kernel, scale=1.0 / math.sqrt(inputs)),
        out_shape=jax.ShapeDtypeStruct((channels, rows // 2, beams), F32),
        grid=(channels // block,),
        in_specs=[whole(rows, inputs), whole(2, inputs), whole(1, inputs),
                  whole(beams, inputs), whole(beams, inputs)],
        out_specs=whole(rows // 2, beams),
        cost_estimate=pl.CostEstimate(
            flops=8 * channels * beams * inputs * rows,
            bytes_accessed=4 * rot_r.size, transcendentals=0,
        ),
        name="beams",
    )(x, gains, flags, rot_r, rot_i)


def shards(samples, window_taps, sky_model, prior_gains, beam_steering, input_flags):
    local_inputs = samples.shape[0]
    frames = samples.shape[3]
    kept_count = NCH
    time_count = lax.axis_size("tm")
    chan_count = lax.axis_size("chan")
    beam_count = lax.axis_size("beam")
    owners = time_count * chan_count
    chan_local = kept_count // owners
    me = (lax.axis_index("chan") * time_count + lax.axis_index("tm")).astype(jnp.int32)
    flags = input_flags[:, None, :]
    denom = first_denominators(sky_model, prior_gains, flags)
    real, imag, denom = filter_bank(samples, window_taps, kept_count, denom)
    by_owner = (owners, chan_local, frames * local_inputs)
    spectra = jnp.concatenate([real.reshape(by_owner), imag.reshape(by_owner)], axis=1)
    spectra, beam_steering = lax.optimization_barrier((spectra, beam_steering))
    parts, origin = exchange(spectra, me, ("chan", "tm"))
    input_count = local_inputs * chan_count * beam_count
    rot_r, rot_i = steering(
        beam_steering, input_count, chan_local, me * chan_local, kept_count
    )
    parts, rot_r, rot_i = lax.optimization_barrier((parts, rot_r, rot_i))
    beam = lax.axis_index("beam").astype(jnp.int32)
    mixed = jnp.concatenate(parts, axis=0)
    if beam_count == 2:
        joined, core = jnp.stack([mixed, other_core(mixed)]), beam
    else:
        joined, core = lax.all_gather(mixed, "beam", axis=0), jnp.zeros_like(beam)
    x = turn(jnp.stack([origin, core]), joined, local_inputs, chan_count, time_count)
    beam_index = jnp.reshape(lax.axis_index("beam"), (1,)).astype(jnp.int32)
    visibilities, updated = gain_call(
        beam_index, x, sky_model, prior_gains, prior_gains, flags, denom
    )
    beam_power = form_beams(x, prior_gains, flags, rot_r, rot_i)
    for _ in range(ITERS - 1):
        if beam_count == 2:
            other, beam_power = lax.optimization_barrier((other_core(updated), beam_power))
            current = jnp.where(
                beam == 0,
                jnp.concatenate([updated, other], axis=2),
                jnp.concatenate([other, updated], axis=2),
            )
        else:
            current = lax.all_gather(updated, "beam", axis=2, tiled=True)
        updated = gain_call(beam_index, x, sky_model, current, updated, flags)
    return (visibilities, updated, jnp.transpose(beam_power, (0, 2, 1)))


SPAN = 16
MESH = pl.DeviceIdType.MESH


def row_product(vr, vi, left):
    straight = jnp.concatenate([vr, vi], axis=0).astype(BF16)
    crossed = jnp.concatenate([-vi, vr], axis=0).astype(BF16)
    return dot_nt(straight, left[0]) + dot_nt(crossed, left[1])


def row_numerators(x, own, model, gains, flags):
    half = x.shape[0] // 2
    hr, hi = gains[0:1] * flags, gains[1:2] * flags
    xr, xi = x[:half].astype(F32), x[half:].astype(F32)
    z = row_product(xr * hr + xi * hi, xi * hr - xr * hi, model)
    zr, zi = z[:half], z[half:]
    pr, pi = own[:half].astype(F32), own[half:].astype(F32)
    numer_r = jnp.sum(pr * zr + pi * zi, axis=0, keepdims=True) * (1.0 / half)
    numer_i = jnp.sum(pi * zr - pr * zi, axis=0, keepdims=True) * (1.0 / half)
    return jnp.concatenate([numer_r, numer_i], axis=0)


def row_denominators(model, gains, flags):
    power = flags * (gains[0:1] * gains[0:1] + gains[1:2] * gains[1:2])
    top = power.astype(BF16).astype(F32)
    wide = (8, top.shape[1])
    both = jnp.concatenate(
        [jnp.broadcast_to(top, wide), jnp.broadcast_to(power - top, wide)], axis=0
    ).astype(BF16)
    mr, mi = model[0], model[1]
    d = dot_nt(both, mr * mr + mi * mi)
    return d[0:1] + d[8:9] + epsilon


def short_sincos(angle):
    q = angle * 0.25
    w = q * q
    sine = q * (1.0 + w * (-1.0 / 6 + w * (1.0 / 120 + w * (-1.0 / 5040 + w * (1.0 / 362880)))))
    less = w * (0.5 + w * (-1.0 / 24 + w * (1.0 / 720 + w * (-1.0 / 40320 + w * (1.0 / 3628800)))))
    for _ in range(2):
        cosine = 1.0 - less
        less, sine = 2.0 * sine * sine, 2.0 * sine * cosine
    return sine, 1.0 - less


def phase_rows(count, stride, width):
    row = lax.broadcasted_iota(jnp.int32, (count, width), 0) * stride
    column = lax.broadcasted_iota(jnp.int32, (count, width), 1)
    index = (row * column) & (width - 1)
    index = jnp.where(index >= width // 2, index - width, index)
    return short_sincos(index.astype(F32) * (2.0 * math.pi / width))


def spread_samples(sample_ref, frame_ref, r):
    inputs, _, frames, width = sample_ref.shape

    def spread(i, carry):
        for tile in range(width // 128):
            piece = sample_ref[i, r, :, tile * 128 : (tile + 1) * 128].astype(F32)
            frame_ref[r, tile, pl.ds(i, frames, stride=inputs), :] = piece
        return carry

    lax.fori_loop(0, inputs, spread, 0, unroll=8)


def fill_transform(cos_ref, sin_ref, high_ref):
    kept, width = cos_ref.shape
    coarse = high_ref.shape[1]
    fine = kept // coarse
    scale = 1.0 / math.sqrt(width)
    high_s, high_c = phase_rows(coarse, fine, width)
    high_ref[0], high_ref[1] = high_c * scale, high_s * scale
    low_s, low_c = phase_rows(fine, 1, width)
    high_ref[2, :fine], high_ref[3, :fine] = low_c, low_s

    def rotate(h, carry):
        hc, hs = high_ref[0, pl.ds(h, 1), :], high_ref[1, pl.ds(h, 1), :]
        lc, ls = high_ref[2, :fine], high_ref[3, :fine]
        at = pl.ds(pl.multiple_of(h * fine, fine), fine)
        cos_ref[at, :] = (hc * lc - hs * ls).astype(BF16)
        sin_ref[at, :] = (hs * lc + hc * ls).astype(BF16)
        return carry

    lax.fori_loop(0, coarse, rotate, 0, unroll=2)


def window_frames(frame_ref, tap_ref, win_ref, inputs):
    taps = tap_ref.shape[0]
    after = taps - 1
    frames = frame_ref.shape[2] // inputs

    def window(tile, carry):
        at = pl.ds(pl.multiple_of(tile * 128, 128), 128)
        weight = [jnp.broadcast_to(tap_ref[tap : tap + 1, at], (16, 128)) for tap in range(taps)]
        for r in range(2):
            for block in range(inputs // 16):
                held = [
                    frame_ref[r, tile, f * inputs + block * 16 : f * inputs + block * 16 + 16, :]
                    for f in range(frames)
                ]
                for g in range(frames + after):
                    terms = [
                        held[g + tap - after] * weight[tap]
                        for tap in range(taps) if 0 <= g + tap - after < frames
                    ]
                    to = g * inputs + block * 16
                    win_ref[r, to : to + 16, at] = sum(terms[1:], terms[0]).astype(BF16)
        return carry

    lax.fori_loop(0, frame_ref.shape[1], window, 0)


def pack_blocks(real_ref, imag_ref, rows_ref, out_ref, tail_ref, group):
    owners, groups, pairs, rows, lanes = out_ref.shape
    half, frames = lanes // 2, rows // 2
    planes = real_ref.shape[1] // half

    def pack(owner, carry):
        base = (owner * groups + group) * 2 * pairs
        low_rows = pl.ds(pl.multiple_of(base, pairs), pairs)
        high_rows = pl.ds(pl.multiple_of(base + pairs, pairs), pairs)
        tails = []
        for s, ref in enumerate((real_ref, imag_ref)):
            for g in range(planes):
                at = slice(g * half, (g + 1) * half)
                joined = jnp.concatenate([ref[low_rows, at], ref[high_rows, at]], axis=1)
                if g < frames:
                    to = pl.ds(s * frames + g, pairs, stride=rows)
                    rows_ref.at[lax.rem(owner, 2)][to, :] = joined
                else:
                    tails.append(joined)
        packed = rows_ref[lax.rem(owner, 2)].reshape(pairs, rows, lanes).astype(BF16)
        out_ref[owner, group] = packed
        tail_ref[owner, group] = jnp.concatenate(tails, axis=0).astype(BF16)
        return carry

    lax.fori_loop(0, owners, pack, 0, unroll=2)


def gains_kernel(
    sample_hbm, tap_ref, model_hbm, gain_ref, flag_ref, steer_ref, x_hbm, new_ref, power_hbm,
    send_ref, tail_ref, recv, tails, model, full, denom, added, table, x_ref, power_ref,
    send_sem, recv_sem, keep_sem, tail_send, tail_recv, tail_keep,
    pass_send, pass_recv, over_send, over_recv, gain_send, gain_recv, load_sem,
    sample_sem, x_sem, power_sem,
    *, chans, times, kept,
):
    z, t, b = lax.axis_index("chan"), lax.axis_index("tm"), lax.axis_index("beam")
    owners, groups, pairs, rows, lanes = send_ref.shape
    channels, _, mine, inputs = model.shape
    local_inputs, _, frames, width = sample_hbm.shape
    terms, beam_count, _ = table.shape
    taps = tap_ref.shape[0]
    me = z * times + t
    off = pl.multiple_of(b * mine, mine)
    half = lanes // 2
    late = tail_ref.shape[2] // pairs // 2
    ahead = times - 1
    planes = frames * times
    quad = pairs // 2
    other = {"beam": 1 - b}

    def place(step):
        device = lax.rem(me + step, owners)
        return device, {"chan": lax.div(device, times), "tm": lax.rem(device, times)}

    barrier = pltpu.get_barrier_semaphore()
    for step in range(1, owners):
        pl.semaphore_signal(barrier, inc=1, device_id=place(step)[1], device_id_type=MESH)
    pl.semaphore_signal(barrier, inc=1, device_id=other, device_id_type=MESH)

    def load(g):
        part = pl.ds(g * SPAN, SPAN)
        return pltpu.make_async_copy(model_hbm.at[part], model.at[part], load_sem.at[g])

    def slot(device):
        return lax.div(device, times) * ahead + lax.rem(device, times)

    def has_tail(device):
        return lax.rem(device, times) < ahead

    def quarter(q):
        return lax.div(q, 2), pl.ds(lax.rem(q, 2) * quad, quad)

    def body_copy(q, step, device, source, where):
        g, cut = quarter(q)
        return pltpu.make_async_remote_copy(
            src_ref=send_ref.at[device, g, cut], dst_ref=recv.at[b, g, source, cut],
            send_sem=send_sem.at[q, step - 1], recv_sem=recv_sem.at[q, step - 1],
            device_id=where, device_id_type=MESH,
        )

    def tail_copy(g, step, device, source, where):
        return pltpu.make_async_remote_copy(
            src_ref=tail_ref.at[device, g], dst_ref=tails.at[b, g, slot(source)],
            send_sem=tail_send.at[g, step - 1], recv_sem=tail_recv.at[g, step - 1],
            device_id=where, device_id_type=MESH,
        )

    def outgoing(make, q, step):
        device, where = place(step)
        return make(q, step, device, me, where)

    def incoming(make, q, step):
        device, where = place(owners - step)
        return make(q, step, device, device, where)

    def keep(g):
        return pltpu.make_async_copy(send_ref.at[me, g], recv.at[b, g, me], keep_sem.at[g])

    def keep_tail(g):
        return pltpu.make_async_copy(tail_ref.at[me, g], tails.at[b, g, slot(me)], tail_keep.at[g])

    def passing(q, core):
        g, cut = quarter(q)
        part = recv.at[core, g, :, cut]
        return pltpu.make_async_remote_copy(
            src_ref=part, dst_ref=part, send_sem=pass_send.at[q], recv_sem=pass_recv.at[q],
            device_id=other, device_id_type=MESH,
        )

    def passing_tail(g, core):
        return pltpu.make_async_remote_copy(
            src_ref=tails.at[core, g], dst_ref=tails.at[core, g],
            send_sem=over_send.at[g], recv_sem=over_recv.at[g],
            device_id=other, device_id_type=MESH,
        )

    def sharing(g, start):
        part = full.at[pl.ds(g * SPAN, SPAN), :, pl.ds(start, mine)]
        return pltpu.make_async_remote_copy(
            src_ref=part, dst_ref=part, send_sem=gain_send.at[g], recv_sem=gain_recv.at[g],
            device_id=other, device_id_type=MESH,
        )

    def store_x(g):
        part = pl.ds(g * SPAN, SPAN)
        return pltpu.make_async_copy(x_ref.at[part], x_hbm.at[part], x_sem.at[g])

    def store_power(g):
        part = pl.ds(g * SPAN, SPAN)
        return pltpu.make_async_copy(power_ref.at[part], power_hbm.at[part], power_sem.at[g])

    def send(g):
        for h in range(2):
            for step in range(1, owners):
                outgoing(body_copy, 2 * g + h, step).start()
            if h == 0:
                keep(g).start()

                @pl.when(has_tail(me))
                def _():
                    for step in range(1, owners):
                        outgoing(tail_copy, g, step).start()
                    keep_tail(g).start()

    def collect(q, g, h):
        for step in range(1, owners):
            incoming(body_copy, q, step).wait_recv()
        if h == 0:
            keep(g).wait()
            for step in range(1, owners):
                @pl.when(has_tail(place(owners - step)[0]))
                def _():
                    incoming(tail_copy, g, step).wait_recv()

            @pl.when(has_tail(me))
            def _():
                keep_tail(g).wait()

            passing_tail(g, b).start()
        passing(q, b).start()

    def merge(q, g, h):
        if h == 0:
            passing_tail(g, 1 - b).wait_recv()
            for core in range(2):
                for k in range(chans * ahead):
                    got = tails[core, g, k].astype(F32)
                    for s in range(2):
                        to = s * frames * pairs
                        part = got[s * late * pairs : (s + 1) * late * pairs]
                        added[core, k, to : to + late * pairs, :] = part
        passing(q, 1 - b).wait_recv()

        def pair(i, carry):
            p = h * quad + i
            for zz in range(chans):
                sides = []
                for core in range(2):
                    got = []
                    for tt in range(times):
                        rows_in = recv[core, g, zz * times + tt, p].astype(F32)
                        if tt:
                            more = added.at[core, zz * ahead + tt - 1]
                            rows_in = rows_in + more[pl.ds(p, rows, stride=pairs), :]
                        got.append(rows_in)
                    sides.append(jnp.concatenate(
                        [r[:frames] for r in got] + [r[frames:] for r in got], axis=0))
                at = slice(zz * lanes, (zz + 1) * lanes)
                for k, cut in enumerate((slice(0, half), slice(half, lanes))):
                    joined = jnp.concatenate([side[:, cut] for side in sides], axis=1)
                    x_ref[g * SPAN + k * pairs + p, :, at] = joined.astype(BF16)
            return carry

        lax.fori_loop(0, quad, pair, 0, unroll=2)

    def zeroth(c):
        flags = flag_ref[pl.ds(c, 1), :].astype(F32)
        denom[c] = row_denominators(model.at[c], gain_ref[c], flags)

    def first(c):
        flags = flag_ref[pl.ds(c, 1), :].astype(F32)
        own = x_ref[c, :, pl.ds(off, mine)]
        numer = row_numerators(x_ref[c], own, model.at[c], gain_ref[c], flags)
        older = gain_ref[c, :, pl.ds(off, mine)]
        full[c, :, pl.ds(off, mine)] = damped(older, numer, denom[c])

    def second(c):
        flags, gains = flag_ref[pl.ds(c, 1), :].astype(F32), full[c]
        own = x_ref[c, :, pl.ds(off, mine)]
        numer = row_numerators(x_ref[c], own, model.at[c], gains, flags)
        new_ref[c] = damped(
            full[c, :, pl.ds(off, mine)], numer, row_denominators(model.at[c], gains, flags)
        )

    def each(stage, g, h):
        start = g * SPAN + h * quad
        for k in range(2):
            for j in range(quad):
                stage(start + k * pairs + j)

    unit = 2.0 * math.pi / (512 * kept)
    middle = 2 * (kept + me * channels) + channels - 1

    def front(sample_ref, frame_ref, win_ref, cos_ref, sin_ref, high_ref, real_ref, imag_ref, rows_ref):
        def fetch(r):
            return pltpu.make_async_copy(
                sample_hbm.at[:, pl.ds(r, 1)], sample_ref.at[:, pl.ds(r, 1)], sample_sem.at[r])

        for r in range(2):
            fetch(r).start()
        for g in range(groups):
            load(g).start()
        fill_transform(cos_ref, sin_ref, high_ref)
        for r in range(2):
            fetch(r).wait()
            spread_samples(sample_ref, frame_ref, r)
        window_frames(frame_ref, tap_ref, win_ref, local_inputs)
        real_ref[...] = dot_nt(cos_ref[...], win_ref[0]) + dot_nt(sin_ref[...], win_ref[1])
        imag_ref[...] = dot_nt(cos_ref[...], win_ref[1]) - dot_nt(sin_ref[...], win_ref[0])
        added[...] = jnp.zeros_like(added)
        for g in range(groups):
            pack_blocks(real_ref, imag_ref, rows_ref, send_ref, tail_ref, g)
            if g == 0:
                pl.semaphore_wait(barrier, owners)
            if g:
                send(g - 1)

    columns = (frames + taps - 1) * local_inputs
    coarse = kept >> ((kept.bit_length() - 1) // 2)
    pl.run_scoped(
        front,
        pltpu.VMEM((local_inputs, 2, frames, width), BF16),
        pltpu.VMEM((2, width // 128, frames * local_inputs, 128), F32),
        pltpu.VMEM((2, columns, width), BF16),
        pltpu.VMEM((kept, width), BF16),
        pltpu.VMEM((kept, width), BF16),
        pltpu.VMEM((4, coarse, width), F32),
        pltpu.VMEM((kept, columns), F32),
        pltpu.VMEM((kept, columns), F32),
        pltpu.VMEM((2, pairs * rows, lanes), F32),
    )

    def back(y_ref, sum_ref, bits_ref):
        position = lax.broadcasted_iota(jnp.int32, (8, inputs), 1)
        column = lax.div(position, inputs // 4)
        row = lax.broadcasted_iota(jnp.int32, (8, inputs), 0)
        factor = jnp.where(row == 0, column * 64, position - column * (inputs // 4))
        factor = jnp.where(row < 2, factor, 0).astype(F32).astype(BF16)
        chosen = steer_ref[...].astype(F32)
        chosen = jnp.concatenate([chosen, jnp.zeros((6, beam_count), F32)], axis=0).astype(BF16)
        product = lax.dot_general(chosen, factor, TN, preferred_element_type=F32)
        bits_ref[...] = product.astype(jnp.int32) & 255

        def tabulate(block, carry):
            at = pl.ds(pl.multiple_of(block * 16, 16), 16)
            index = bits_ref[at, :] - 128
            imag, real = short_sincos((index * middle).astype(F32) * (0.5 * unit))
            turned = index.astype(F32) * (unit * channels / 2)
            for k in range(terms):
                if k:
                    scale = turned * (1.0 / k)
                    real, imag = real * scale, imag * scale
                table[k, at, :inputs] = real.astype(BF16)
                table[k, at, inputs:] = imag.astype(BF16)
            return carry

        lax.fori_loop(0, beam_count // 16, tabulate, 0)
        send(groups - 1)

        def ready(g, carry):
            load(g).wait()

            def some(i, carry):
                for j in range(8):
                    zeroth(g * SPAN + i * 8 + j)
                return carry

            return lax.fori_loop(0, SPAN // 8, some, carry)

        lax.fori_loop(0, groups, ready, 0)

        def beams(g):
            def prepare(c, carry):
                x, gains = x_ref[g * SPAN + c], gain_ref[g * SPAN + c]
                flags = flag_ref[pl.ds(g * SPAN + c, 1), :].astype(F32) * (1.0 / math.sqrt(inputs))
                hr, hi = gains[0:1] * flags, gains[1:2] * flags
                xr, xi = x[:planes].astype(F32), x[planes:].astype(F32)
                yr = (xr * hr - xi * hi).astype(BF16)
                yi = (xi * hr + xr * hi).astype(BF16)
                y_ref[c, :planes, :inputs] = yr
                y_ref[c, :planes, inputs:] = -yi
                y_ref[c, planes:, :inputs] = yi
                y_ref[c, planes:, inputs:] = yr
                return carry

            lax.fori_loop(0, SPAN, prepare, 0, unroll=4)
            y = y_ref[...].reshape(SPAN * 2 * planes, 2 * inputs)
            for k in range(terms):
                sum_ref[k] = dot_nt(y, table[k])

            def finish(c, carry):
                u = ((g * SPAN + c).astype(F32) - (channels - 1) / 2) * (2.0 / channels)
                at = pl.ds(pl.multiple_of(c * 2 * planes, 2 * planes), 2 * planes)
                last = sum_ref[terms - 1, at, :]
                vr, vi = last[:planes], last[planes:]
                for k in reversed(range(terms - 1)):
                    term = sum_ref[k, at, :]
                    vr, vi = term[:planes] - u * vi, term[planes:] + u * vr
                power_ref[g * SPAN + c] = vr * vr + vi * vi
                return carry

            lax.fori_loop(0, SPAN, finish, 0, unroll=4)

        collect(0, 0, 0)

        def group(g, carry):
            @pl.when(g < groups)
            def _():
                merge(2 * g, g, 0)
                each(first, g, 0)
                collect(2 * g + 1, g, 1)

            @pl.when(g >= 1)
            def _():
                sharing(g - 1, pl.multiple_of((1 - b) * mine, mine)).wait_recv()
                each(second, g - 1, 0)

            @pl.when(g < groups)
            def _():
                merge(2 * g + 1, g, 1)
                each(first, g, 1)
                store_x(g).start()
                beams(g)
                sharing(g, off).start()

            @pl.when(g + 1 < groups)
            def _():
                collect(2 * g + 2, g + 1, 0)

            @pl.when(g >= 1)
            def _():
                each(second, g - 1, 1)
                store_power(g - 1).start()

            return carry

        lax.fori_loop(0, groups + 1, group, 0)

    wide = SPAN * 2 * planes
    pl.run_scoped(
        back,
        pltpu.VMEM((SPAN, 2 * planes, 2 * inputs), BF16),
        pltpu.VMEM((terms, wide, beam_count), F32),
        pltpu.VMEM((beam_count, inputs), jnp.int32),
    )

    def drain(g, carry):
        for h in range(2):
            for step in range(1, owners):
                outgoing(body_copy, 2 * g + h, step).wait_send()
            passing(2 * g + h, b).wait_send()

        @pl.when(has_tail(me))
        def _():
            for step in range(1, owners):
                outgoing(tail_copy, g, step).wait_send()

        passing_tail(g, b).wait_send()
        sharing(g, off).wait_send()
        store_x(g).wait()
        store_power(g).wait()
        return carry

    lax.fori_loop(0, groups, drain, 0)


def solve_gains(samples, window_taps, model, gains, flags, beam_steering, chans, times, kept):
    local_inputs, _, width, frames = samples.shape
    taps = window_taps.shape[0]
    natural = jnp.transpose(samples, (0, 1, 3, 2))
    channels, _, mine, inputs = model.shape
    beams = beam_steering.shape[1]
    owners = chans * times
    groups, pairs, rows, lanes = channels // SPAN, SPAN // 2, 2 * frames, 2 * local_inputs
    terms = series_terms(channels, kept)
    vmem, apart = pl.BlockSpec(memory_space=pltpu.VMEM), pl.BlockSpec(memory_space=pl.ANY)
    dma = pltpu.SemaphoreType.DMA
    joint = chans * (times - 1)
    late = (taps - 1) * SPAN
    planes = times * frames
    return pl.pallas_call(
        functools.partial(gains_kernel, chans=chans, times=times, kept=kept),
        out_shape=[
            jax.ShapeDtypeStruct((channels, 2 * planes, inputs), BF16),
            jax.ShapeDtypeStruct((channels, 2, mine), F32),
            jax.ShapeDtypeStruct((channels, planes, beams), F32),
        ],
        in_specs=[apart, vmem, apart, vmem, vmem, vmem],
        out_specs=[apart, vmem, apart],
        scratch_shapes=[
            pltpu.VMEM((owners, groups, pairs, rows, lanes), BF16),
            pltpu.VMEM((owners, groups, late, lanes), BF16),
            pltpu.VMEM((2, groups, owners, pairs, rows, lanes), BF16),
            pltpu.VMEM((2, groups, joint, late, lanes), BF16),
            pltpu.VMEM(model.shape, BF16),
            pltpu.VMEM((channels, 2, inputs), F32),
            pltpu.VMEM((channels, 1, mine), F32),
            pltpu.VMEM((2, joint, rows * pairs, lanes), F32),
            pltpu.VMEM((terms, beams, 2 * inputs), BF16),
            pltpu.VMEM((channels, 2 * planes, inputs), BF16),
            pltpu.VMEM((channels, planes, beams), F32),
            dma((2 * groups, owners - 1)), dma((2 * groups, owners - 1)), dma((groups,)),
            dma((groups, owners - 1)), dma((groups, owners - 1)), dma((groups,)),
            dma((2 * groups,)), dma((2 * groups,)),
            *[dma((groups,))] * 5,
            dma((2,)), dma((groups,)), dma((groups,)),
        ],
        compiler_params=pltpu.CompilerParams(
            collective_id=0, has_side_effects=True, vmem_limit_bytes=67043328
        ),
        cost_estimate=pl.CostEstimate(
            flops=40 * channels * mine * inputs * planes,
            bytes_accessed=2 * model.size, transcendentals=0,
        ),
        name="gains",
    )(natural, window_taps, model, gains, flags, beam_steering)


def correlate_only_kernel(beam_ref, x_ref, own_ref, new_in, power_in, vis_ref, new_out, power_out):
    for c in range(x_ref.shape[0]):
        x, own = x_ref[c], own_ref[c]
        half = x.shape[0] // 2
        exact = half & (half - 1) == 0
        before, after = (1.0 / half, 1.0) if exact else (1.0, 1.0 / half)
        scaled = (own.astype(F32) * before).astype(BF16)
        rotated = jnp.concatenate([scaled[half:], -scaled[:half]], axis=0)
        for part, left in enumerate((scaled, rotated)):
            terms = lax.dot_general(left, x, TN, preferred_element_type=F32)
            vis_ref[c, part] = (terms if exact else terms * after).astype(BF16)
    new_out[...] = new_in[...]
    power_out[...] = power_in[...]


def correlate(beam_index, x, new, power):
    channels, rows, inputs = x.shape
    mine = new.shape[2]
    block = math.gcd(channels, 8)
    whole = lambda *shape: pl.BlockSpec((block, *shape), lambda c, b: (c,) + (0,) * len(shape))
    part = lambda r: pl.BlockSpec((block, r, mine), lambda c, b: (c, 0, b[0]))
    kept = [whole(2, mine), whole(*power.shape[1:])]
    return pl.pallas_call(
        correlate_only_kernel,
        out_shape=[
            jax.ShapeDtypeStruct((channels, 2, mine, inputs), BF16),
            jax.ShapeDtypeStruct(new.shape, F32),
            jax.ShapeDtypeStruct(power.shape, F32),
        ],
        grid_spec=pltpu.PrefetchScalarGridSpec(
            num_scalar_prefetch=1,
            grid=(channels // block,),
            in_specs=[whole(rows, inputs), part(rows), *kept],
            out_specs=[whole(2, mine, inputs), *kept],
        ),
        cost_estimate=pl.CostEstimate(
            flops=4 * channels * mine * inputs * rows,
            bytes_accessed=4 * channels * mine * inputs, transcendentals=0,
        ),
        name="correlate_only",
    )(beam_index, x, x, new, power)


def series_terms(channels, chan_total):
    reach = 128 * (channels / 2) * 2.0 * math.pi / (512 * chan_total)
    terms, left = 1, reach
    while left >= 2.0**-23:
        terms += 1
        left *= reach / terms
    return terms


def tiled_shards(samples, window_taps, sky_model, prior_gains, beam_steering, input_flags):
    x, new, power = solve_gains(
        samples, window_taps, sky_model, prior_gains, input_flags, beam_steering,
        lax.axis_size("chan"), lax.axis_size("tm"), NCH,
    )
    beam_index = jnp.reshape(lax.axis_index("beam"), (1,)).astype(jnp.int32)
    visibilities, new, power = correlate(beam_index, x, new, power)
    return visibilities, new, jnp.transpose(power, (0, 2, 1))


def tiles(samples, window_taps, sky_model, prior_gains, beam_steering, input_flags):
    owners = lax.axis_size("tm") * lax.axis_size("chan")
    local_inputs, frames = samples.shape[0], samples.shape[3]
    return (
        ITERS == 2
        and lax.axis_size("beam") == 2
        and owners > 1
        and 2 * local_inputs == 128
        and frames == 8
        and 1 < window_taps.shape[0] <= frames
        and samples.shape[2] & (samples.shape[2] - 1) == 0
        and lax.axis_size("tm") % 2 == 0
        and NCH % (owners * SPAN) == 0
        and sky_model.size <= 1 << 24
    )


def any_shards(*args):
    return tiled_shards(*args) if tiles(*args) else shards(*args)


def solution(mesh):
    return jax.shard_map(
        any_shards,
        mesh=mesh,
        in_specs=(
            P(("group", "chan", "beam"), None, None, "tm"),
            P(),
            P(("group", "chan", "tm"), None, "beam", None),
            P(("group", "chan", "tm"), None, None),
            P(None, ("group", "beam")),
            P(("group", "chan", "tm"), None),
        ),
        out_specs=(
            P(("group", "chan", "tm"), None, "beam", None),
            P(("group", "chan", "tm"), None, "beam"),
            P(("group", "chan", "tm"), "beam", None),
        ),
        check_vma=False,
    )
```

```python
import functools
import math

import jax
import jax.numpy as jnp
from jax import lax
from jax.experimental import pallas as pl
from jax.experimental.pallas import tpu as pltpu
from jax.sharding import PartitionSpec as P

NCH = 512
ITERS = 2


damping = 0.5
epsilon = 1e-06
F32 = jnp.float32
BF16 = jnp.bfloat16


def from_behind(block, axis, distance):
    devices = range(lax.axis_size(axis))
    route = [(i - distance, i) for i in devices if i - distance in devices]
    return lax.ppermute(block, axis, route)


def unit_rows(rows, columns, transform_count):
    phases = (rows[:, None] * columns[None, :] % transform_count).astype(F32) * (
        2.0 * math.pi / transform_count
    )
    return jnp.cos(phases), jnp.sin(phases)


def transform_rows(kept_count, transform_count):
    fine = 1 << ((kept_count.bit_length() - 1) // 2)
    coarse = kept_count // fine
    columns = jnp.arange(transform_count, dtype=jnp.int32)
    high_c, high_s = unit_rows(jnp.arange(coarse, dtype=jnp.int32) * fine, columns, transform_count)
    low_c, low_s = unit_rows(jnp.arange(fine, dtype=jnp.int32), columns, transform_count)
    high_c, high_s, low_c, low_s = lax.optimization_barrier((high_c, high_s, low_c, low_s))
    scale = 1.0 / math.sqrt(transform_count)
    return high_c * scale, high_s * scale, low_c, low_s


def transform_table(kept_count, transform_count):
    high_c, high_s, low_c, low_s = transform_rows(kept_count, transform_count)
    cosine = high_c[:, None] * low_c[None] - high_s[:, None] * low_s[None]
    sine = high_s[:, None] * low_c[None] + high_c[:, None] * low_s[None]
    cosine = cosine.reshape(kept_count, transform_count).astype(BF16)
    sine = sine.reshape(kept_count, transform_count).astype(BF16)
    return cosine, sine


def windowed_frames(samples, window_taps, beside):
    frames = samples.shape[3]
    tap_count = window_taps.shape[0]
    framed = jnp.transpose(samples, (3, 1, 0, 2))
    previous = from_behind(framed[frames - tap_count + 1 :], "tm", 1)
    previous, beside = lax.optimization_barrier((previous, beside))
    extended = jnp.concatenate([previous, framed], axis=0).astype(F32)
    windowed = sum(
        extended[tap : tap + frames] * window_taps[tap][None, None, None, :]
        for tap in range(tap_count)
    )
    return windowed.astype(BF16), beside


def filter_bank(samples, window_taps, kept_count, beside):
    local_inputs, _, transform_count, frames = samples.shape
    windowed, beside = windowed_frames(samples, window_taps, beside)
    real_in = windowed[:, 0].reshape(frames * local_inputs, transform_count)
    imag_in = windowed[:, 1].reshape(frames * local_inputs, transform_count)
    cosine, sine = transform_table(kept_count, transform_count)
    real = dot_nt(cosine, real_in) + dot_nt(sine, imag_in)
    imag = dot_nt(cosine, imag_in) - dot_nt(sine, real_in)
    return real.astype(BF16), imag.astype(BF16), beside


NT = (((1,), (1,)), ((), ()))
TN = (((0,), (0,)), ((), ()))


def dot_nt(a, b):
    return lax.dot_general(a, b, NT, preferred_element_type=F32)


def complex_product(left_r, left_i, vr, vi):
    straight = jnp.concatenate([vr, vi], axis=0).astype(BF16)
    crossed = jnp.concatenate([-vi, vr], axis=0).astype(BF16)
    return (dot_nt(left_r, straight) + dot_nt(left_i, crossed)).T


def numerators(x, own, model, gains, flags):
    half = x.shape[0] // 2
    hr, hi = gains[0:1] * flags, gains[1:2] * flags
    xr, xi = x[:half].astype(F32), x[half:].astype(F32)
    z = complex_product(model[0], model[1], xr * hr + xi * hi, xi * hr - xr * hi)
    zr, zi = z[:half], z[half:]
    pr, pi = own[:half].astype(F32), own[half:].astype(F32)
    numer_r = jnp.sum(pr * zr + pi * zi, axis=0, keepdims=True) * (1.0 / half)
    numer_i = jnp.sum(pi * zr - pr * zi, axis=0, keepdims=True) * (1.0 / half)
    return jnp.concatenate([numer_r, numer_i], axis=0)


def denominators(model, gains, flags):
    power = flags * (gains[0:1] * gains[0:1] + gains[1:2] * gains[1:2])
    top = power.astype(BF16).astype(F32)
    wide = (8, top.shape[1])
    both = jnp.concatenate(
        [jnp.broadcast_to(top, wide), jnp.broadcast_to(power - top, wide)], axis=0
    ).astype(BF16)
    mr, mi = model[0], model[1]
    d = dot_nt(mr * mr + mi * mi, both).T
    return d[0:1] + d[8:9] + epsilon


def damped(older, numer, denom):
    return damping * older + (1.0 - damping) * (numer / denom)


def denominator_kernel(model_ref, gain_ref, flag_ref, out_ref):
    for c in range(model_ref.shape[0]):
        out_ref[c] = denominators(model_ref.at[c], gain_ref[c], flag_ref[c].astype(F32))


def first_denominators(model, gains, flags):
    channels, _, mine, inputs = model.shape
    block = math.gcd(channels, 8)
    whole = lambda *shape: pl.BlockSpec((block, *shape), lambda c: (c,) + (0,) * len(shape))
    return pl.pallas_call(
        denominator_kernel,
        out_shape=jax.ShapeDtypeStruct((channels, 1, mine), F32),
        grid=(channels // block,),
        in_specs=[whole(2, mine, inputs), whole(2, inputs), whole(1, inputs)],
        out_specs=whole(1, mine),
        cost_estimate=pl.CostEstimate(
            flops=16 * model.size, bytes_accessed=2 * model.size, transcendentals=0
        ),
        name="denominators",
    )(model, gains, flags)


def correlate_kernel(beam_ref, x_ref, own_ref, model_ref, gain_ref, older_ref, flag_ref, denom_ref, vis_ref, new_ref):
    for c in range(x_ref.shape[0]):
        x, own = x_ref[c], own_ref[c]
        half = x.shape[0] // 2
        exact = half & (half - 1) == 0
        before, after = (1.0 / half, 1.0) if exact else (1.0, 1.0 / half)
        scaled = (own.astype(F32) * before).astype(BF16)
        rotated = jnp.concatenate([scaled[half:], -scaled[:half]], axis=0)
        for part, left in enumerate((scaled, rotated)):
            terms = lax.dot_general(left, x, TN, preferred_element_type=F32)
            vis_ref[c, part] = (terms if exact else terms * after).astype(BF16)
        numer = numerators(x, own, model_ref.at[c], gain_ref[c], flag_ref[c].astype(F32))
        new_ref[c] = damped(older_ref[c], numer, denom_ref[c])


def update_kernel(beam_ref, x_ref, own_ref, model_ref, gain_ref, older_ref, flag_ref, new_ref):
    for c in range(x_ref.shape[0]):
        model, gains, flags = model_ref.at[c], gain_ref[c], flag_ref[c].astype(F32)
        numer = numerators(x_ref[c], own_ref[c], model, gains, flags)
        new_ref[c] = damped(older_ref[c], numer, denominators(model, gains, flags))


def turn_kernel(me_ref, in_ref, out_ref, rows_ref, *, inputs, chans, times):
    beams, _, paired, lanes = in_ref.shape
    frames = lanes // inputs
    planes = times * frames
    width = rows_ref.shape[2]
    for b in range(beams):
        for z in range(chans):
            column = (z * beams + b) * inputs
            at = column % width
            for t in range(times):
                slab = in_ref[b ^ me_ref[1], (z * times + t) ^ me_ref[0]].astype(F32)
                for f in range(frames):
                    plane = t * frames + f
                    rows_ref[
                        column // width, plane * paired : (plane + 1) * paired, at : at + inputs
                    ] = slab[:, f * inputs : (f + 1) * inputs]

    def gather(k, carry):
        for q in range(rows_ref.shape[0]):
            parts = [
                rows_ref.at[q][pl.ds(s * (paired // 2) + k, planes, stride=paired), :]
                for s in range(2)
            ]
            out_ref[k, :, q * width : (q + 1) * width] = jnp.concatenate(parts, axis=0).astype(BF16)
        return carry

    lax.fori_loop(0, paired // 2, gather, 0)


def turn(me, joined, inputs, chans, times):
    beams, _, paired, lanes = joined.shape
    planes = times * (lanes // inputs)
    total = chans * beams * inputs
    width = 128
    whole = lambda *shape: pl.BlockSpec(shape, lambda c, m: (0,) * len(shape))
    out_dims = (paired // 2, 2 * planes, total)
    return pl.pallas_call(
        functools.partial(turn_kernel, inputs=inputs, chans=chans, times=times),
        out_shape=jax.ShapeDtypeStruct(out_dims, BF16),
        grid_spec=pltpu.PrefetchScalarGridSpec(
            num_scalar_prefetch=1,
            grid=(1,),
            in_specs=[whole(*joined.shape)],
            out_specs=whole(*out_dims),
            scratch_shapes=[pltpu.VMEM((total // width, planes * paired, width), F32)],
        ),
        cost_estimate=pl.CostEstimate(
            flops=0, bytes_accessed=8 * joined.size, transcendentals=0
        ),
        name="turn",
    )(me, joined)


def other_core(block):
    return lax.ppermute(block, "beam", [(0, 1), (1, 0)])


def exchange(blocks, me, axes):
    owners = blocks.shape[0]
    if owners > 8 or owners & (owners - 1):
        mixed = lax.all_to_all(blocks, axes, split_axis=0, concat_axis=0, tiled=True)
        return [mixed], jnp.zeros_like(me)
    parts = []
    for step in range(owners):
        block = lax.dynamic_slice_in_dim(blocks, me ^ step, 1, 0)
        if step:
            block = lax.ppermute(block, axes, [(i, i ^ step) for i in range(owners)])
        parts.append(block)
    return parts, me


def gain_call(beam_index, x, model, gains, older, flags, denom=None):
    correlate = denom is not None
    channels, rows, inputs = x.shape
    mine = model.shape[2]
    block = math.gcd(channels, 8)
    whole = lambda *shape: pl.BlockSpec((block, *shape), lambda c, b: (c,) + (0,) * len(shape))
    part = lambda r: pl.BlockSpec((block, r, mine), lambda c, b: (c, 0, b[0]))
    older_spec = part(2) if older.shape[2] == inputs else whole(2, mine)
    new_shape = jax.ShapeDtypeStruct((channels, 2, mine), F32)
    if correlate:
        out_shape = [jax.ShapeDtypeStruct(model.shape, BF16), new_shape]
        out_specs = [whole(2, mine, inputs), whole(2, mine)]
    else:
        out_shape, out_specs = new_shape, whole(2, mine)
    return pl.pallas_call(
        correlate_kernel if correlate else update_kernel,
        out_shape=out_shape,
        grid_spec=pltpu.PrefetchScalarGridSpec(
            num_scalar_prefetch=1,
            grid=(channels // block,),
            in_specs=[whole(rows, inputs), part(rows), whole(2, mine, inputs), whole(2, inputs),
                      older_spec, whole(1, inputs)] + [whole(1, mine)] * correlate,
            out_specs=out_specs,
        ),
        cost_estimate=pl.CostEstimate(
            flops=8 * channels * mine * inputs * rows,
            bytes_accessed=(4 + 4 * correlate) * model.size // 2,
            transcendentals=0,
        ),
        name="correlate" if correlate else "update",
    )(beam_index, x, x, model, gains, older, flags, *([denom] if correlate else []))


def steering_kernel(base_ref, bits_ref, rot_r, rot_i, cur_r, cur_i, one_r, one_i, *, unit):
    block = rot_r.shape[0]
    beams, inputs = cur_r.shape
    step = 16

    @pl.when(pl.program_id(0) == 0)
    def _():
        first = base_ref[0]

        def fill(r, carry):
            rows = pl.ds(r * 8, 8)
            bits = bits_ref[rows, :]
            angle = (bits * first).astype(F32) * unit
            cur_r[rows, :] = jnp.cos(angle)
            cur_i[rows, :] = jnp.sin(angle)
            small = bits.astype(F32) * unit
            one_r[rows, :] = jnp.cos(small)
            one_i[rows, :] = jnp.sin(small)
            return carry

        lax.fori_loop(0, beams // 8, fill, 0)

    def advance(r, carry):
        rows = pl.ds(r * step, step)
        ar, ai = cur_r[rows, :], cur_i[rows, :]
        br, bi = one_r[rows, :], one_i[rows, :]
        for c in range(block):
            rot_r[c, rows, :] = ar.astype(BF16)
            rot_i[c, rows, :] = ai.astype(BF16)
            ar, ai = ar * br - ai * bi, ar * bi + ai * br
        cur_r[rows, :] = ar
        cur_i[rows, :] = ai
        return carry

    lax.fori_loop(0, beams // step, advance, 0)


def steering(beam_steering, inputs, channels, first_channel, chan_total):
    beams = beam_steering.shape[1]
    positions = jnp.arange(inputs, dtype=jnp.int32)
    column = positions // (inputs // 4)
    within = positions % (inputs // 4)
    bits = (
        beam_steering[0][:, None] * column[None, :] * 64
        + beam_steering[1][:, None] * within[None, :]
    ) % 256
    block = math.gcd(channels, 8)
    rot = jax.ShapeDtypeStruct((channels, beams, inputs), BF16)
    rot_spec = pl.BlockSpec((block, beams, inputs), lambda c, b: (c, 0, 0))
    return pl.pallas_call(
        functools.partial(steering_kernel, unit=2.0 * math.pi / (512 * chan_total)),
        out_shape=[rot, rot],
        grid_spec=pltpu.PrefetchScalarGridSpec(
            num_scalar_prefetch=1,
            grid=(channels // block,),
            in_specs=[pl.BlockSpec((beams, inputs), lambda c, b: (0, 0))],
            out_specs=[rot_spec, rot_spec],
            scratch_shapes=[pltpu.VMEM((beams, inputs), F32)] * 4,
        ),
        cost_estimate=pl.CostEstimate(
            flops=8 * rot.size, bytes_accessed=6 * rot.size, transcendentals=0
        ),
        name="steering",
    )(jnp.reshape(chan_total + first_channel, (1,)), bits)


def beam_kernel(x_ref, gain_ref, flag_ref, rot_r, rot_i, power_ref, *, scale):
    for c in range(x_ref.shape[0]):
        x, gains = x_ref[c], gain_ref[c]
        flags = flag_ref[c].astype(F32) * scale
        half = x.shape[0] // 2
        hr, hi = gains[0:1] * flags, gains[1:2] * flags
        xr, xi = x[:half].astype(F32), x[half:].astype(F32)
        v = complex_product(rot_r[c], rot_i[c], xr * hr - xi * hi, xi * hr + xr * hi)
        vr, vi = v[:half], v[half:]
        power_ref[c] = vr * vr + vi * vi


def form_beams(x, gains, flags, rot_r, rot_i):
    channels, rows, inputs = x.shape
    beams = rot_r.shape[1]
    block = math.gcd(channels, 16)
    whole = lambda *shape: pl.BlockSpec((block, *shape), lambda c: (c,) + (0,) * len(shape))
    return pl.pallas_call(
        functools.partial(beam_kernel, scale=1.0 / math.sqrt(inputs)),
        out_shape=jax.ShapeDtypeStruct((channels, rows // 2, beams), F32),
        grid=(channels // block,),
        in_specs=[whole(rows, inputs), whole(2, inputs), whole(1, inputs),
                  whole(beams, inputs), whole(beams, inputs)],
        out_specs=whole(rows // 2, beams),
        cost_estimate=pl.CostEstimate(
            flops=8 * channels * beams * inputs * rows,
            bytes_accessed=4 * rot_r.size, transcendentals=0,
        ),
        name="beams",
    )(x, gains, flags, rot_r, rot_i)


def shards(samples, window_taps, sky_model, prior_gains, beam_steering, input_flags):
    local_inputs = samples.shape[0]
    frames = samples.shape[3]
    kept_count = NCH
    time_count = lax.axis_size("tm")
    chan_count = lax.axis_size("chan")
    beam_count = lax.axis_size("beam")
    owners = time_count * chan_count
    chan_local = kept_count // owners
    me = (lax.axis_index("chan") * time_count + lax.axis_index("tm")).astype(jnp.int32)
    flags = input_flags[:, None, :]
    denom = first_denominators(sky_model, prior_gains, flags)
    real, imag, denom = filter_bank(samples, window_taps, kept_count, denom)
    by_owner = (owners, chan_local, frames * local_inputs)
    spectra = jnp.concatenate([real.reshape(by_owner), imag.reshape(by_owner)], axis=1)
    spectra, beam_steering = lax.optimization_barrier((spectra, beam_steering))
    parts, origin = exchange(spectra, me, ("chan", "tm"))
    input_count = local_inputs * chan_count * beam_count
    rot_r, rot_i = steering(
        beam_steering, input_count, chan_local, me * chan_local, kept_count
    )
    parts, rot_r, rot_i = lax.optimization_barrier((parts, rot_r, rot_i))
    beam = lax.axis_index("beam").astype(jnp.int32)
    mixed = jnp.concatenate(parts, axis=0)
    if beam_count == 2:
        joined, core = jnp.stack([mixed, other_core(mixed)]), beam
    else:
        joined, core = lax.all_gather(mixed, "beam", axis=0), jnp.zeros_like(beam)
    x = turn(jnp.stack([origin, core]), joined, local_inputs, chan_count, time_count)
    beam_index = jnp.reshape(lax.axis_index("beam"), (1,)).astype(jnp.int32)
    visibilities, updated = gain_call(
        beam_index, x, sky_model, prior_gains, prior_gains, flags, denom
    )
    beam_power = form_beams(x, prior_gains, flags, rot_r, rot_i)
    for _ in range(ITERS - 1):
        if beam_count == 2:
            other, beam_power = lax.optimization_barrier((other_core(updated), beam_power))
            current = jnp.where(
                beam == 0,
                jnp.concatenate([updated, other], axis=2),
                jnp.concatenate([other, updated], axis=2),
            )
        else:
            current = lax.all_gather(updated, "beam", axis=2, tiled=True)
        updated = gain_call(beam_index, x, sky_model, current, updated, flags)
    return (visibilities, updated, jnp.transpose(beam_power, (0, 2, 1)))


SPAN = 16
MESH = pl.DeviceIdType.MESH


def row_product(vr, vi, left):
    straight = jnp.concatenate([vr, vi], axis=0).astype(BF16)
    crossed = jnp.concatenate([-vi, vr], axis=0).astype(BF16)
    return dot_nt(straight, left[0]) + dot_nt(crossed, left[1])


def row_numerators(x, own, model, gains, flags):
    half = x.shape[0] // 2
    hr, hi = gains[0:1] * flags, gains[1:2] * flags
    xr, xi = x[:half].astype(F32), x[half:].astype(F32)
    z = row_product(xr * hr + xi * hi, xi * hr - xr * hi, model)
    zr, zi = z[:half], z[half:]
    pr, pi = own[:half].astype(F32), own[half:].astype(F32)
    numer_r = jnp.sum(pr * zr + pi * zi, axis=0, keepdims=True) * (1.0 / half)
    numer_i = jnp.sum(pi * zr - pr * zi, axis=0, keepdims=True) * (1.0 / half)
    return jnp.concatenate([numer_r, numer_i], axis=0)


def row_denominators(model, gains, flags):
    power = flags * (gains[0:1] * gains[0:1] + gains[1:2] * gains[1:2])
    top = power.astype(BF16).astype(F32)
    wide = (8, top.shape[1])
    both = jnp.concatenate(
        [jnp.broadcast_to(top, wide), jnp.broadcast_to(power - top, wide)], axis=0
    ).astype(BF16)
    mr, mi = model[0], model[1]
    d = dot_nt(both, mr * mr + mi * mi)
    return d[0:1] + d[8:9] + epsilon


def short_sincos(angle):
    q = angle * 0.25
    w = q * q
    sine = q * (1.0 + w * (-1.0 / 6 + w * (1.0 / 120 + w * (-1.0 / 5040 + w * (1.0 / 362880)))))
    less = w * (0.5 + w * (-1.0 / 24 + w * (1.0 / 720 + w * (-1.0 / 40320 + w * (1.0 / 3628800)))))
    for _ in range(2):
        cosine = 1.0 - less
        less, sine = 2.0 * sine * sine, 2.0 * sine * cosine
    return sine, 1.0 - less


def phase_rows(count, stride, width):
    row = lax.broadcasted_iota(jnp.int32, (count, width), 0) * stride
    column = lax.broadcasted_iota(jnp.int32, (count, width), 1)
    index = (row * column) & (width - 1)
    index = jnp.where(index >= width // 2, index - width, index)
    return short_sincos(index.astype(F32) * (2.0 * math.pi / width))


def spread_samples(sample_ref, frame_ref, r):
    inputs, _, frames, width = sample_ref.shape

    def spread(i, carry):
        for tile in range(width // 128):
            piece = sample_ref[i, r, :, tile * 128 : (tile + 1) * 128].astype(F32)
            frame_ref[r, tile, pl.ds(i, frames, stride=inputs), :] = piece
        return carry

    lax.fori_loop(0, inputs, spread, 0, unroll=8)


def fill_transform(cos_ref, sin_ref, high_ref):
    kept, width = cos_ref.shape
    coarse = high_ref.shape[1]
    fine = kept // coarse
    scale = 1.0 / math.sqrt(width)
    high_s, high_c = phase_rows(coarse, fine, width)
    high_ref[0], high_ref[1] = high_c * scale, high_s * scale
    low_s, low_c = phase_rows(fine, 1, width)
    high_ref[2, :fine], high_ref[3, :fine] = low_c, low_s

    def rotate(h, carry):
        hc, hs = high_ref[0, pl.ds(h, 1), :], high_ref[1, pl.ds(h, 1), :]
        lc, ls = high_ref[2, :fine], high_ref[3, :fine]
        at = pl.ds(pl.multiple_of(h * fine, fine), fine)
        cos_ref[at, :] = (hc * lc - hs * ls).astype(BF16)
        sin_ref[at, :] = (hs * lc + hc * ls).astype(BF16)
        return carry

    lax.fori_loop(0, coarse, rotate, 0, unroll=2)


def window_frames(frame_ref, tap_ref, win_ref, inputs):
    taps = tap_ref.shape[0]
    after = taps - 1
    frames = frame_ref.shape[2] // inputs

    def window(tile, carry):
        at = pl.ds(pl.multiple_of(tile * 128, 128), 128)
        weight = [jnp.broadcast_to(tap_ref[tap : tap + 1, at], (16, 128)) for tap in range(taps)]
        for r in range(2):
            for block in range(inputs // 16):
                held = [
                    frame_ref[r, tile, f * inputs + block * 16 : f * inputs + block * 16 + 16, :]
                    for f in range(frames)
                ]
                for g in range(frames + after):
                    terms = [
                        held[g + tap - after] * weight[tap]
                        for tap in range(taps) if 0 <= g + tap - after < frames
                    ]
                    to = g * inputs + block * 16
                    win_ref[r, to : to + 16, at] = sum(terms[1:], terms[0]).astype(BF16)
        return carry

    lax.fori_loop(0, frame_ref.shape[1], window, 0)


def paired_denominators(models, gains, flags):
    sums = []
    for model, g, flag in zip(models, gains, flags):
        power = (flag * (g[0:1] * g[0:1] + g[1:2] * g[1:2])).astype(BF16)
        total = None
        for tile in range(power.shape[1] // 128):
            at = slice(tile * 128, (tile + 1) * 128)
            mr, mi = model[0, :, at], model[1, :, at]
            term = (mr * mr + mi * mi) * power[:, at]
            total = term if total is None else total + term
        sums.append(total)
    lane = lax.broadcasted_iota(jnp.int32, (16, 256), 1)
    row = lax.broadcasted_iota(jnp.int32, (16, 256), 0)
    chosen = jnp.where((lane < 128) == (row < 8), 1.0, 0.0).astype(BF16)
    d = dot_nt(chosen, jnp.concatenate(sums, axis=1))
    return d[0:1] + epsilon, d[8:9] + epsilon


def joined_rows(ref, row, pairs, plane, half):
    at = slice(plane * half, (plane + 1) * half)
    low = ref[pl.ds(pl.multiple_of(row, pairs), pairs), at]
    high = ref[pl.ds(pl.multiple_of(row + pairs, pairs), pairs), at]
    return jnp.concatenate([low, high], axis=1)


def pack_tails(real_ref, imag_ref, tail_ref, pairs):
    groups, owners, rows, lanes = tail_ref.shape
    half, late = lanes // 2, rows // (2 * pairs)

    def pack(owner, carry):
        for group in range(groups):
            row = (owner * groups + group) * 2 * pairs
            planes = [
                joined_rows(ref, row, pairs, plane, half)
                for ref in (real_ref, imag_ref) for plane in range(late)
            ]
            tail_ref[group, owner] = jnp.concatenate(planes, axis=0).astype(BF16)
        return carry

    lax.fori_loop(0, owners, pack, 0)


def pack_bodies(real_ref, imag_ref, rows_ref, early_ref, out_ref, group):
    owners, groups, pairs, rows, lanes = out_ref.shape
    half, frames = lanes // 2, rows // 2
    late = early_ref.shape[2] // (2 * pairs)

    def pack(owner, carry):
        row = (owner * groups + group) * 2 * pairs
        early = early_ref[group, owner].astype(F32)
        for s, ref in enumerate((real_ref, imag_ref)):
            for plane in range(frames):
                joined = joined_rows(ref, row, pairs, plane, half)
                if plane < late:
                    at = (s * late + plane) * pairs
                    joined = joined + early[at : at + pairs]
                to = pl.ds(s * frames + plane, pairs, stride=rows)
                rows_ref.at[lax.rem(owner, 2)][to, :] = joined
        packed = rows_ref[lax.rem(owner, 2)].reshape(pairs, rows, lanes).astype(BF16)
        out_ref[owner, group] = packed
        return carry

    lax.fori_loop(0, owners, pack, 0, unroll=2)


def gains_kernel(
    sample_hbm, tap_ref, model_hbm, gain_ref, flag_ref, steer_ref, x_hbm, new_ref, power_hbm,
    send_ref, tail_ref, early_ref, recv, model, full, denom, table, x_ref, power_ref,
    real_ref, imag_ref, rows_ref, send_sem, recv_sem, keep_sem, tail_send, tail_recv,
    pass_send, pass_recv, gain_send, gain_recv, load_sem,
    sample_sem, x_sem, power_sem,
    *, chans, times, kept,
):
    z, t, b = lax.axis_index("chan"), lax.axis_index("tm"), lax.axis_index("beam")
    owners, groups, pairs, rows, lanes = send_ref.shape
    channels, _, mine, inputs = model.shape
    local_inputs, _, frames, width = sample_hbm.shape
    terms, beam_count, _ = table.shape
    taps = tap_ref.shape[0]
    me = z * times + t
    off = pl.multiple_of(b * mine, mine)
    half = lanes // 2
    late = taps - 1
    planes = frames * times
    quad = pairs // 2
    other = {"beam": 1 - b}

    def place(step):
        device = lax.rem(me + step, owners)
        return device, {"chan": lax.div(device, times), "tm": lax.rem(device, times)}

    barrier = pltpu.get_barrier_semaphore()
    for step in range(1, owners):
        pl.semaphore_signal(barrier, inc=1, device_id=place(step)[1], device_id_type=MESH)
    pl.semaphore_signal(barrier, inc=1, device_id=other, device_id_type=MESH)

    def load(g):
        part = pl.ds(g * SPAN, SPAN)
        return pltpu.make_async_copy(model_hbm.at[part], model.at[part], load_sem.at[g])

    def quarter(q):
        return lax.div(q, 2), pl.ds(lax.rem(q, 2) * quad, quad)

    def body_copy(q, step, device, source, where):
        g, cut = quarter(q)
        return pltpu.make_async_remote_copy(
            src_ref=send_ref.at[device, g, cut], dst_ref=recv.at[b, g, source, cut],
            send_sem=send_sem.at[q, step - 1], recv_sem=recv_sem.at[q, step - 1],
            device_id=where, device_id_type=MESH,
        )

    def tail_copy(g, where):
        return pltpu.make_async_remote_copy(
            src_ref=tail_ref.at[g], dst_ref=early_ref.at[g],
            send_sem=tail_send.at[g], recv_sem=tail_recv.at[g],
            device_id={"tm": where}, device_id_type=MESH,
        )

    def outgoing(q, step):
        device, where = place(step)
        return body_copy(q, step, device, me, where)

    def incoming(q, step):
        device, where = place(owners - step)
        return body_copy(q, step, device, device, where)

    def keep(g):
        return pltpu.make_async_copy(send_ref.at[me, g], recv.at[b, g, me], keep_sem.at[g])

    def passing(q, core):
        g, cut = quarter(q)
        part = recv.at[core, g, :, cut]
        return pltpu.make_async_remote_copy(
            src_ref=part, dst_ref=part, send_sem=pass_send.at[q], recv_sem=pass_recv.at[q],
            device_id=other, device_id_type=MESH,
        )

    def sharing(g, start):
        part = full.at[pl.ds(g * SPAN, SPAN), :, pl.ds(start, mine)]
        return pltpu.make_async_remote_copy(
            src_ref=part, dst_ref=part, send_sem=gain_send.at[g], recv_sem=gain_recv.at[g],
            device_id=other, device_id_type=MESH,
        )

    def store_x(g):
        part = pl.ds(g * SPAN, SPAN)
        return pltpu.make_async_copy(x_ref.at[part], x_hbm.at[part], x_sem.at[g])

    def store_power(g):
        part = pl.ds(g * SPAN, SPAN)
        return pltpu.make_async_copy(power_ref.at[part], power_hbm.at[part], power_sem.at[g])

    def send(q, h):
        for step in range(1, owners):
            outgoing(q, step).start()
        if h == 0:
            keep(lax.div(q, 2)).start()

    def sent(q):
        for step in range(1, owners):
            outgoing(q, step).wait_send()

    def pump(q, h):
        sent(q)
        send(q + 2, h)

    def pack(g):
        @pl.when(t > 0)
        def _():
            tail_copy(g, t - 1).wait_recv()

        pack_bodies(real_ref, imag_ref, rows_ref, early_ref, send_ref, g)

    def collect(q, g, h):
        for step in range(1, owners):
            incoming(q, step).wait_recv()
        if h == 0:
            keep(g).wait()
        passing(q, b).start()

    def merge(q, g, h):
        passing(q, 1 - b).wait_recv()

        def pair(i, carry):
            p = h * quad + i
            for zz in range(chans):
                sides = []
                for core in range(2):
                    got = [recv[core, g, zz * times + tt, p].astype(F32) for tt in range(times)]
                    sides.append(jnp.concatenate(
                        [r[:frames] for r in got] + [r[frames:] for r in got], axis=0))
                at = slice(zz * lanes, (zz + 1) * lanes)
                for k, cut in enumerate((slice(0, half), slice(half, lanes))):
                    joined = jnp.concatenate([side[:, cut] for side in sides], axis=1)
                    x_ref[g * SPAN + k * pairs + p, :, at] = joined.astype(BF16)
            return carry

        lax.fori_loop(0, quad, pair, 0, unroll=2)

    def zeroth(c):
        flags = flag_ref[pl.ds(c, 1), :].astype(F32)
        denom[c] = row_denominators(model.at[c], gain_ref[c], flags)

    def first(c):
        flags = flag_ref[pl.ds(c, 1), :].astype(F32)
        own = x_ref[c, :, pl.ds(off, mine)]
        numer = row_numerators(x_ref[c], own, model.at[c], gain_ref[c], flags)
        older = gain_ref[c, :, pl.ds(off, mine)]
        full[c, :, pl.ds(off, mine)] = damped(older, numer, denom[c])

    def second(*pair):
        flags = [flag_ref[pl.ds(c, 1), :].astype(F32) for c in pair]
        denoms = paired_denominators([model.at[c] for c in pair], [full[c] for c in pair], flags)
        for c, flag, denominator in zip(pair, flags, denoms):
            own = x_ref[c, :, pl.ds(off, mine)]
            numer = row_numerators(x_ref[c], own, model.at[c], full[c], flag)
            new_ref[c] = damped(full[c, :, pl.ds(off, mine)], numer, denominator)

    def seconds(g, h):
        start = g * SPAN + h * quad
        for k in range(2):
            for j in range(0, quad, 2):
                second(start + k * pairs + j, start + k * pairs + j + 1)

    def each(stage, g, h):
        start = g * SPAN + h * quad
        for k in range(2):
            for j in range(quad):
                stage(start + k * pairs + j)

    unit = 2.0 * math.pi / (512 * kept)
    middle = 2 * (kept + me * channels) + channels - 1

    def front(
        sample_ref, frame_ref, win_ref, cos_ref, sin_ref, high_ref, real_late, imag_late,
    ):
        def fetch(r):
            return pltpu.make_async_copy(
                sample_hbm.at[:, pl.ds(r, 1)], sample_ref.at[:, pl.ds(r, 1)], sample_sem.at[r])

        for r in range(2):
            fetch(r).start()
        for g in range(groups):
            load(g).start()
        fill_transform(cos_ref, sin_ref, high_ref)
        for r in range(2):
            fetch(r).wait()
            spread_samples(sample_ref, frame_ref, r)
        window_frames(frame_ref, tap_ref, win_ref, local_inputs)

        def transform(real_out, imag_out, start):
            at = pl.ds(start, real_out.shape[1])
            real_in, imag_in = win_ref[0, at, :], win_ref[1, at, :]
            real_out[...] = dot_nt(cos_ref[...], real_in) + dot_nt(sin_ref[...], imag_in)
            imag_out[...] = dot_nt(cos_ref[...], imag_in) - dot_nt(sin_ref[...], real_in)

        transform(real_late, imag_late, frames * local_inputs)
        pack_tails(real_late, imag_late, tail_ref, pairs)
        pl.semaphore_wait(barrier, owners)

        @pl.when(t < times - 1)
        def _():
            for g in range(min(2, groups)):
                tail_copy(g, t + 1).start()

        @pl.when(t == 0)
        def _():
            early_ref[...] = jnp.zeros_like(early_ref)

        transform(real_ref, imag_ref, 0)

        @pl.when(t < times - 1)
        def _():
            for g in range(2, groups):
                tail_copy(g - 2, t + 1).wait_send()
                tail_copy(g, t + 1).start()

    columns = (frames + taps - 1) * local_inputs
    coarse = kept >> ((kept.bit_length() - 1) // 2)
    pl.run_scoped(
        front,
        pltpu.VMEM((local_inputs, 2, frames, width), BF16),
        pltpu.VMEM((2, width // 128, frames * local_inputs, 128), F32),
        pltpu.VMEM((2, columns, width), BF16),
        pltpu.VMEM((kept, width), BF16),
        pltpu.VMEM((kept, width), BF16),
        pltpu.VMEM((4, coarse, width), F32),
        pltpu.VMEM((kept, late * local_inputs), F32),
        pltpu.VMEM((kept, late * local_inputs), F32),
    )

    def back(y_ref, sum_ref, bits_ref):
        position = lax.broadcasted_iota(jnp.int32, (8, inputs), 1)
        column = lax.div(position, inputs // 4)
        row = lax.broadcasted_iota(jnp.int32, (8, inputs), 0)
        factor = jnp.where(row == 0, column * 64, position - column * (inputs // 4))
        factor = jnp.where(row < 2, factor, 0).astype(F32).astype(BF16)
        chosen = steer_ref[...].astype(F32)
        chosen = jnp.concatenate([chosen, jnp.zeros((6, beam_count), F32)], axis=0).astype(BF16)
        product = lax.dot_general(chosen, factor, TN, preferred_element_type=F32)
        bits_ref[...] = product.astype(jnp.int32) & 255

        def tabulate(block, carry):
            at = pl.ds(pl.multiple_of(block * 16, 16), 16)
            index = bits_ref[at, :] - 128
            imag, real = short_sincos((index * middle).astype(F32) * (0.5 * unit))
            turned = index.astype(F32) * (unit * channels / 2)
            for k in range(terms):
                if k:
                    scale = turned * (1.0 / k)
                    real, imag = real * scale, imag * scale
                table[k, at, :inputs] = real.astype(BF16)
                table[k, at, inputs:] = imag.astype(BF16)
            return carry

        pack(0)
        lax.fori_loop(0, beam_count // 16, tabulate, 0)
        for h in range(2):
            send(h, h)

        def ready(g):
            load(g).wait()

            def some(i, carry):
                for j in range(8):
                    zeroth(g * SPAN + i * 8 + j)
                return carry

            lax.fori_loop(0, SPAN // 8, some, 0)

        for g in range(groups):
            if g + 1 < groups:
                pack(g + 1)
            ready(g)
            if g in (1, 2) and g + 1 < 2 * groups:
                pump(g - 1, (g - 1) % 2)

        def beams(start):
            count = y_ref.shape[0]

            def prepare(c, carry):
                x, gains = x_ref[start + c], gain_ref[start + c]
                flags = flag_ref[pl.ds(start + c, 1), :].astype(F32) * (1.0 / math.sqrt(inputs))
                hr, hi = gains[0:1] * flags, gains[1:2] * flags
                xr, xi = x[:planes].astype(F32), x[planes:].astype(F32)
                yr = (xr * hr - xi * hi).astype(BF16)
                yi = (xi * hr + xr * hi).astype(BF16)
                y_ref[c, :planes, :inputs] = yr
                y_ref[c, :planes, inputs:] = -yi
                y_ref[c, planes:, :inputs] = yi
                y_ref[c, planes:, inputs:] = yr
                return carry

            lax.fori_loop(0, count, prepare, 0, unroll=4)
            y = y_ref[...].reshape(count * 2 * planes, 2 * inputs)
            for k in range(terms):
                sum_ref[k] = dot_nt(y, table[k])

            def finish(c, carry):
                u = ((start + c).astype(F32) - (channels - 1) / 2) * (2.0 / channels)
                at = pl.ds(pl.multiple_of(c * 2 * planes, 2 * planes), 2 * planes)
                last = sum_ref[terms - 1, at, :]
                vr, vi = last[:planes], last[planes:]
                for k in reversed(range(terms - 1)):
                    term = sum_ref[k, at, :]
                    vr, vi = term[:planes] - u * vi, term[planes:] + u * vr
                power_ref[start + c] = vr * vr + vi * vi
                return carry

            lax.fori_loop(0, count, finish, 0, unroll=4)

        for q in range(2):
            if q + 2 < 2 * groups and not 1 <= q + 1 < groups:
                pump(q, q)
        collect(0, 0, 0)

        def group(g, carry):
            @pl.when(g < groups)
            def _():
                @pl.when(2 * g + 4 < 2 * groups)
                def _():
                    pump(2 * g + 2, 0)

                merge(2 * g, g, 0)
                each(first, g, 0)
                collect(2 * g + 1, g, 1)

                @pl.when(2 * g + 5 < 2 * groups)
                def _():
                    pump(2 * g + 3, 1)

            @pl.when(g >= 1)
            def _():
                sharing(g - 1, pl.multiple_of((1 - b) * mine, mine)).wait_recv()
                seconds(g - 1, 0)

            @pl.when(g < groups)
            def _():
                merge(2 * g + 1, g, 1)
                each(first, g, 1)
                store_x(g).start()

                @pl.when(lax.rem(g, 2) == 1)
                def _():
                    beams((g - 1) * SPAN)

                sharing(g, off).start()

            @pl.when(g + 1 < groups)
            def _():
                collect(2 * g + 2, g + 1, 0)

            @pl.when(g >= 1)
            def _():
                seconds(g - 1, 1)
                store_power(g - 1).start()

            return carry

        lax.fori_loop(0, groups + 1, group, 0)

    wide = 2 * SPAN * 2 * planes
    pl.run_scoped(
        back,
        pltpu.VMEM((2 * SPAN, 2 * planes, 2 * inputs), BF16),
        pltpu.VMEM((terms, wide, beam_count), F32),
        pltpu.VMEM((beam_count, inputs), jnp.int32),
    )

    def drain(g, carry):
        for h in range(2):
            passing(2 * g + h, b).wait_send()

        sharing(g, off).wait_send()
        store_x(g).wait()
        store_power(g).wait()
        return carry

    lax.fori_loop(0, groups, drain, 0)
    for h in range(2):
        sent(2 * groups - 2 + h)

    @pl.when(t < times - 1)
    def _():
        for g in range(max(groups - 2, 0), groups):
            tail_copy(g, t + 1).wait_send()


def solve_gains(samples, window_taps, model, gains, flags, beam_steering, chans, times, kept):
    local_inputs, _, width, frames = samples.shape
    taps = window_taps.shape[0]
    natural = jnp.transpose(samples, (0, 1, 3, 2))
    channels, _, mine, inputs = model.shape
    beams = beam_steering.shape[1]
    owners = chans * times
    groups, pairs, rows, lanes = channels // SPAN, SPAN // 2, 2 * frames, 2 * local_inputs
    terms = series_terms(channels, kept)
    vmem, apart = pl.BlockSpec(memory_space=pltpu.VMEM), pl.BlockSpec(memory_space=pl.ANY)
    dma = pltpu.SemaphoreType.DMA
    late = (taps - 1) * SPAN
    planes = times * frames
    return pl.pallas_call(
        functools.partial(gains_kernel, chans=chans, times=times, kept=kept),
        out_shape=[
            jax.ShapeDtypeStruct((channels, 2 * planes, inputs), BF16),
            jax.ShapeDtypeStruct((channels, 2, mine), F32),
            jax.ShapeDtypeStruct((channels, planes, beams), F32),
        ],
        in_specs=[apart, vmem, apart, vmem, vmem, vmem],
        out_specs=[apart, vmem, apart],
        scratch_shapes=[
            pltpu.VMEM((owners, groups, pairs, rows, lanes), BF16),
            pltpu.VMEM((groups, owners, late, lanes), BF16),
            pltpu.VMEM((groups, owners, late, lanes), BF16),
            pltpu.VMEM((2, groups, owners, pairs, rows, lanes), BF16),
            pltpu.VMEM(model.shape, BF16),
            pltpu.VMEM((channels, 2, inputs), F32),
            pltpu.VMEM((channels, 1, mine), F32),
            pltpu.VMEM((terms, beams, 2 * inputs), BF16),
            pltpu.VMEM((channels, 2 * planes, inputs), BF16),
            pltpu.VMEM((channels, planes, beams), F32),
            pltpu.VMEM((kept, frames * local_inputs), F32),
            pltpu.VMEM((kept, frames * local_inputs), F32),
            pltpu.VMEM((2, pairs * rows, lanes), F32),
            dma((2 * groups, owners - 1)), dma((2 * groups, owners - 1)), dma((groups,)),
            dma((groups,)), dma((groups,)),
            dma((2 * groups,)), dma((2 * groups,)),
            *[dma((groups,))] * 3,
            dma((2,)), dma((groups,)), dma((groups,)),
        ],
        compiler_params=pltpu.CompilerParams(
            collective_id=0, has_side_effects=True, vmem_limit_bytes=67043328
        ),
        cost_estimate=pl.CostEstimate(
            flops=40 * channels * mine * inputs * planes,
            bytes_accessed=2 * model.size, transcendentals=0,
        ),
        name="gains",
    )(natural, window_taps, model, gains, flags, beam_steering)


def correlate_only_kernel(
    x_hbm, new_hbm, power_hbm, vis_hbm, new_out, power_out,
    x_ref, new_ref, power_ref, vis_ref, x_sem, in_sem, out_sem, vis_sem,
):
    slots, block, _, mine, _ = vis_ref.shape
    channels, rows, _ = x_ref.shape
    half = rows // 2
    parts = x_sem.shape[0]
    off = pl.multiple_of(lax.axis_index("beam") * mine, mine)
    exact = half & (half - 1) == 0
    before, after = (1.0 / half, 1.0) if exact else (1.0, 1.0 / half)

    def fetch(k):
        part = pl.ds(k * (channels // parts), channels // parts)
        return pltpu.make_async_copy(x_hbm.at[part], x_ref.at[part], x_sem.at[k])

    for k in range(parts):
        fetch(k).start()
    ins = [pltpu.make_async_copy(new_hbm, new_ref, in_sem.at[0]),
           pltpu.make_async_copy(power_hbm, power_ref, in_sem.at[1])]
    outs = [pltpu.make_async_copy(new_ref, new_out, out_sem.at[0]),
            pltpu.make_async_copy(power_ref, power_out, out_sem.at[1])]
    for copy in ins:
        copy.start()

    def store(i, slot):
        part = pl.ds(i * block, block)
        return pltpu.make_async_copy(vis_ref.at[slot], vis_hbm.at[part], vis_sem.at[slot])

    def step(i, carry):
        slot = lax.rem(i, slots)

        @pl.when(i >= slots)
        def _():
            store(i - slots, slot).wait()

        for j in range(block):
            x = x_ref[i * block + j]
            own = x_ref[i * block + j, :, pl.ds(off, mine)]
            scaled = (own.astype(F32) * before).astype(BF16)
            rotated = jnp.concatenate([scaled[half:], -scaled[:half]], axis=0)
            for part, left in enumerate((scaled, rotated)):
                terms = lax.dot_general(left, x, TN, preferred_element_type=F32)
                vis_ref[slot, j, part] = (terms if exact else terms * after).astype(BF16)
        store(i, slot).start()
        return carry

    steps = channels // block
    each = steps // parts
    for k in range(parts):
        fetch(k).wait()
        lax.fori_loop(k * each, (k + 1) * each, step, 0)
        if k == 0:
            for first, last in zip(ins, outs):
                first.wait()
                last.start()
    for copy in outs:
        copy.wait()
    for i in range(max(steps - slots, 0), steps):
        store(i, i % slots).wait()


def correlate(x, new, power):
    channels, rows, inputs = x.shape
    mine = new.shape[2]
    block, parts, slots = 4, 4, 3
    apart = pl.BlockSpec(memory_space=pl.ANY)
    dma = pltpu.SemaphoreType.DMA
    return pl.pallas_call(
        correlate_only_kernel,
        out_shape=[
            jax.ShapeDtypeStruct((channels, 2, mine, inputs), BF16),
            jax.ShapeDtypeStruct(new.shape, F32),
            jax.ShapeDtypeStruct(power.shape, F32),
        ],
        in_specs=[apart] * 3,
        out_specs=[apart] * 3,
        scratch_shapes=[
            pltpu.VMEM(x.shape, BF16), pltpu.VMEM(new.shape, F32), pltpu.VMEM(power.shape, F32),
            pltpu.VMEM((slots, block, 2, mine, inputs), BF16),
            dma((parts,)), dma((2,)), dma((2,)), dma((slots,)),
        ],
        cost_estimate=pl.CostEstimate(
            flops=4 * channels * mine * inputs * rows,
            bytes_accessed=4 * channels * mine * inputs, transcendentals=0,
        ),
        name="correlate_only",
    )(x, new, power)


def series_terms(channels, chan_total):
    reach = 128 * (channels / 2) * 2.0 * math.pi / (512 * chan_total)
    terms, left = 1, reach
    while left >= 2.0**-23:
        terms += 1
        left *= reach / terms
    return terms


def tiled_shards(samples, window_taps, sky_model, prior_gains, beam_steering, input_flags):
    x, new, power = solve_gains(
        samples, window_taps, sky_model, prior_gains, input_flags, beam_steering,
        lax.axis_size("chan"), lax.axis_size("tm"), NCH,
    )
    visibilities, new, power = correlate(x, new, power)
    return visibilities, new, jnp.transpose(power, (0, 2, 1))


def tiles(samples, window_taps, sky_model, prior_gains, beam_steering, input_flags):
    owners = lax.axis_size("tm") * lax.axis_size("chan")
    local_inputs, frames = samples.shape[0], samples.shape[3]
    return (
        ITERS == 2
        and lax.axis_size("beam") == 2
        and owners > 1
        and 2 * local_inputs == 128
        and frames == 8
        and 1 < window_taps.shape[0] <= frames
        and samples.shape[2] & (samples.shape[2] - 1) == 0
        and lax.axis_size("tm") % 2 == 0
        and NCH % (2 * owners * SPAN) == 0
        and sky_model.size <= 1 << 24
    )


def any_shards(*args):
    return tiled_shards(*args) if tiles(*args) else shards(*args)


def solution(mesh):
    return jax.shard_map(
        any_shards,
        mesh=mesh,
        in_specs=(
            P(("group", "chan", "beam"), None, None, "tm"),
            P(),
            P(("group", "chan", "tm"), None, "beam", None),
            P(("group", "chan", "tm"), None, None),
            P(None, ("group", "beam")),
            P(("group", "chan", "tm"), None),
        ),
        out_specs=(
            P(("group", "chan", "tm"), None, "beam", None),
            P(("group", "chan", "tm"), None, "beam"),
            P(("group", "chan", "tm"), "beam", None),
        ),
        check_vma=False,
    )
```

```python
import functools
import math

import jax
import jax.numpy as jnp
from jax import lax
from jax.experimental import pallas as pl
from jax.experimental.pallas import tpu as pltpu
from jax.sharding import PartitionSpec as P

NCH = 512
ITERS = 2


damping = 0.5
epsilon = 1e-06
F32 = jnp.float32
BF16 = jnp.bfloat16


def from_behind(block, axis, distance):
    devices = range(lax.axis_size(axis))
    route = [(i - distance, i) for i in devices if i - distance in devices]
    return lax.ppermute(block, axis, route)


def unit_rows(rows, columns, transform_count):
    phases = (rows[:, None] * columns[None, :] % transform_count).astype(F32) * (
        2.0 * math.pi / transform_count
    )
    return jnp.cos(phases), jnp.sin(phases)


def transform_rows(kept_count, transform_count):
    fine = 1 << ((kept_count.bit_length() - 1) // 2)
    coarse = kept_count // fine
    columns = jnp.arange(transform_count, dtype=jnp.int32)
    high_c, high_s = unit_rows(jnp.arange(coarse, dtype=jnp.int32) * fine, columns, transform_count)
    low_c, low_s = unit_rows(jnp.arange(fine, dtype=jnp.int32), columns, transform_count)
    high_c, high_s, low_c, low_s = lax.optimization_barrier((high_c, high_s, low_c, low_s))
    scale = 1.0 / math.sqrt(transform_count)
    return high_c * scale, high_s * scale, low_c, low_s


def transform_table(kept_count, transform_count):
    high_c, high_s, low_c, low_s = transform_rows(kept_count, transform_count)
    cosine = high_c[:, None] * low_c[None] - high_s[:, None] * low_s[None]
    sine = high_s[:, None] * low_c[None] + high_c[:, None] * low_s[None]
    cosine = cosine.reshape(kept_count, transform_count).astype(BF16)
    sine = sine.reshape(kept_count, transform_count).astype(BF16)
    return cosine, sine


def windowed_frames(samples, window_taps, beside):
    frames = samples.shape[3]
    tap_count = window_taps.shape[0]
    framed = jnp.transpose(samples, (3, 1, 0, 2))
    previous = from_behind(framed[frames - tap_count + 1 :], "tm", 1)
    previous, beside = lax.optimization_barrier((previous, beside))
    extended = jnp.concatenate([previous, framed], axis=0).astype(F32)
    windowed = sum(
        extended[tap : tap + frames] * window_taps[tap][None, None, None, :]
        for tap in range(tap_count)
    )
    return windowed.astype(BF16), beside


def filter_bank(samples, window_taps, kept_count, beside):
    local_inputs, _, transform_count, frames = samples.shape
    windowed, beside = windowed_frames(samples, window_taps, beside)
    real_in = windowed[:, 0].reshape(frames * local_inputs, transform_count)
    imag_in = windowed[:, 1].reshape(frames * local_inputs, transform_count)
    cosine, sine = transform_table(kept_count, transform_count)
    real = dot_nt(cosine, real_in) + dot_nt(sine, imag_in)
    imag = dot_nt(cosine, imag_in) - dot_nt(sine, real_in)
    return real.astype(BF16), imag.astype(BF16), beside


NT = (((1,), (1,)), ((), ()))
TN = (((0,), (0,)), ((), ()))


def dot_nt(a, b):
    return lax.dot_general(a, b, NT, preferred_element_type=F32)


def complex_product(left_r, left_i, vr, vi):
    straight = jnp.concatenate([vr, vi], axis=0).astype(BF16)
    crossed = jnp.concatenate([-vi, vr], axis=0).astype(BF16)
    return (dot_nt(left_r, straight) + dot_nt(left_i, crossed)).T


def numerators(x, own, model, gains, flags):
    half = x.shape[0] // 2
    hr, hi = gains[0:1] * flags, gains[1:2] * flags
    xr, xi = x[:half].astype(F32), x[half:].astype(F32)
    z = complex_product(model[0], model[1], xr * hr + xi * hi, xi * hr - xr * hi)
    zr, zi = z[:half], z[half:]
    pr, pi = own[:half].astype(F32), own[half:].astype(F32)
    numer_r = jnp.sum(pr * zr + pi * zi, axis=0, keepdims=True) * (1.0 / half)
    numer_i = jnp.sum(pi * zr - pr * zi, axis=0, keepdims=True) * (1.0 / half)
    return jnp.concatenate([numer_r, numer_i], axis=0)


def denominators(model, gains, flags):
    power = flags * (gains[0:1] * gains[0:1] + gains[1:2] * gains[1:2])
    top = power.astype(BF16).astype(F32)
    wide = (8, top.shape[1])
    both = jnp.concatenate(
        [jnp.broadcast_to(top, wide), jnp.broadcast_to(power - top, wide)], axis=0
    ).astype(BF16)
    mr, mi = model[0], model[1]
    d = dot_nt(mr * mr + mi * mi, both).T
    return d[0:1] + d[8:9] + epsilon


def damped(older, numer, denom):
    return damping * older + (1.0 - damping) * (numer / denom)


def denominator_kernel(model_ref, gain_ref, flag_ref, out_ref):
    for c in range(model_ref.shape[0]):
        out_ref[c] = denominators(model_ref.at[c], gain_ref[c], flag_ref[c].astype(F32))


def first_denominators(model, gains, flags):
    channels, _, mine, inputs = model.shape
    block = math.gcd(channels, 8)
    whole = lambda *shape: pl.BlockSpec((block, *shape), lambda c: (c,) + (0,) * len(shape))
    return pl.pallas_call(
        denominator_kernel,
        out_shape=jax.ShapeDtypeStruct((channels, 1, mine), F32),
        grid=(channels // block,),
        in_specs=[whole(2, mine, inputs), whole(2, inputs), whole(1, inputs)],
        out_specs=whole(1, mine),
        cost_estimate=pl.CostEstimate(
            flops=16 * model.size, bytes_accessed=2 * model.size, transcendentals=0
        ),
        name="denominators",
    )(model, gains, flags)


def correlate_kernel(beam_ref, x_ref, own_ref, model_ref, gain_ref, older_ref, flag_ref, denom_ref, vis_ref, new_ref):
    for c in range(x_ref.shape[0]):
        x, own = x_ref[c], own_ref[c]
        half = x.shape[0] // 2
        exact = half & (half - 1) == 0
        before, after = (1.0 / half, 1.0) if exact else (1.0, 1.0 / half)
        scaled = (own.astype(F32) * before).astype(BF16)
        rotated = jnp.concatenate([scaled[half:], -scaled[:half]], axis=0)
        for part, left in enumerate((scaled, rotated)):
            terms = lax.dot_general(left, x, TN, preferred_element_type=F32)
            vis_ref[c, part] = (terms if exact else terms * after).astype(BF16)
        numer = numerators(x, own, model_ref.at[c], gain_ref[c], flag_ref[c].astype(F32))
        new_ref[c] = damped(older_ref[c], numer, denom_ref[c])


def update_kernel(beam_ref, x_ref, own_ref, model_ref, gain_ref, older_ref, flag_ref, new_ref):
    for c in range(x_ref.shape[0]):
        model, gains, flags = model_ref.at[c], gain_ref[c], flag_ref[c].astype(F32)
        numer = numerators(x_ref[c], own_ref[c], model, gains, flags)
        new_ref[c] = damped(older_ref[c], numer, denominators(model, gains, flags))


def turn_kernel(me_ref, in_ref, out_ref, rows_ref, *, inputs, chans, times):
    beams, _, paired, lanes = in_ref.shape
    frames = lanes // inputs
    planes = times * frames
    width = rows_ref.shape[2]
    for b in range(beams):
        for z in range(chans):
            column = (z * beams + b) * inputs
            at = column % width
            for t in range(times):
                slab = in_ref[b ^ me_ref[1], (z * times + t) ^ me_ref[0]].astype(F32)
                for f in range(frames):
                    plane = t * frames + f
                    rows_ref[
                        column // width, plane * paired : (plane + 1) * paired, at : at + inputs
                    ] = slab[:, f * inputs : (f + 1) * inputs]

    def gather(k, carry):
        for q in range(rows_ref.shape[0]):
            parts = [
                rows_ref.at[q][pl.ds(s * (paired // 2) + k, planes, stride=paired), :]
                for s in range(2)
            ]
            out_ref[k, :, q * width : (q + 1) * width] = jnp.concatenate(parts, axis=0).astype(BF16)
        return carry

    lax.fori_loop(0, paired // 2, gather, 0)


def turn(me, joined, inputs, chans, times):
    beams, _, paired, lanes = joined.shape
    planes = times * (lanes // inputs)
    total = chans * beams * inputs
    width = 128
    whole = lambda *shape: pl.BlockSpec(shape, lambda c, m: (0,) * len(shape))
    out_dims = (paired // 2, 2 * planes, total)
    return pl.pallas_call(
        functools.partial(turn_kernel, inputs=inputs, chans=chans, times=times),
        out_shape=jax.ShapeDtypeStruct(out_dims, BF16),
        grid_spec=pltpu.PrefetchScalarGridSpec(
            num_scalar_prefetch=1,
            grid=(1,),
            in_specs=[whole(*joined.shape)],
            out_specs=whole(*out_dims),
            scratch_shapes=[pltpu.VMEM((total // width, planes * paired, width), F32)],
        ),
        cost_estimate=pl.CostEstimate(
            flops=0, bytes_accessed=8 * joined.size, transcendentals=0
        ),
        name="turn",
    )(me, joined)


def other_core(block):
    return lax.ppermute(block, "beam", [(0, 1), (1, 0)])


def exchange(blocks, me, axes):
    owners = blocks.shape[0]
    if owners > 8 or owners & (owners - 1):
        mixed = lax.all_to_all(blocks, axes, split_axis=0, concat_axis=0, tiled=True)
        return [mixed], jnp.zeros_like(me)
    parts = []
    for step in range(owners):
        block = lax.dynamic_slice_in_dim(blocks, me ^ step, 1, 0)
        if step:
            block = lax.ppermute(block, axes, [(i, i ^ step) for i in range(owners)])
        parts.append(block)
    return parts, me


def gain_call(beam_index, x, model, gains, older, flags, denom=None):
    correlate = denom is not None
    channels, rows, inputs = x.shape
    mine = model.shape[2]
    block = math.gcd(channels, 8)
    whole = lambda *shape: pl.BlockSpec((block, *shape), lambda c, b: (c,) + (0,) * len(shape))
    part = lambda r: pl.BlockSpec((block, r, mine), lambda c, b: (c, 0, b[0]))
    older_spec = part(2) if older.shape[2] == inputs else whole(2, mine)
    new_shape = jax.ShapeDtypeStruct((channels, 2, mine), F32)
    if correlate:
        out_shape = [jax.ShapeDtypeStruct(model.shape, BF16), new_shape]
        out_specs = [whole(2, mine, inputs), whole(2, mine)]
    else:
        out_shape, out_specs = new_shape, whole(2, mine)
    return pl.pallas_call(
        correlate_kernel if correlate else update_kernel,
        out_shape=out_shape,
        grid_spec=pltpu.PrefetchScalarGridSpec(
            num_scalar_prefetch=1,
            grid=(channels // block,),
            in_specs=[whole(rows, inputs), part(rows), whole(2, mine, inputs), whole(2, inputs),
                      older_spec, whole(1, inputs)] + [whole(1, mine)] * correlate,
            out_specs=out_specs,
        ),
        cost_estimate=pl.CostEstimate(
            flops=8 * channels * mine * inputs * rows,
            bytes_accessed=(4 + 4 * correlate) * model.size // 2,
            transcendentals=0,
        ),
        name="correlate" if correlate else "update",
    )(beam_index, x, x, model, gains, older, flags, *([denom] if correlate else []))


def steering_kernel(base_ref, bits_ref, rot_r, rot_i, cur_r, cur_i, one_r, one_i, *, unit):
    block = rot_r.shape[0]
    beams, inputs = cur_r.shape
    step = 16

    @pl.when(pl.program_id(0) == 0)
    def _():
        first = base_ref[0]

        def fill(r, carry):
            rows = pl.ds(r * 8, 8)
            bits = bits_ref[rows, :]
            angle = (bits * first).astype(F32) * unit
            cur_r[rows, :] = jnp.cos(angle)
            cur_i[rows, :] = jnp.sin(angle)
            small = bits.astype(F32) * unit
            one_r[rows, :] = jnp.cos(small)
            one_i[rows, :] = jnp.sin(small)
            return carry

        lax.fori_loop(0, beams // 8, fill, 0)

    def advance(r, carry):
        rows = pl.ds(r * step, step)
        ar, ai = cur_r[rows, :], cur_i[rows, :]
        br, bi = one_r[rows, :], one_i[rows, :]
        for c in range(block):
            rot_r[c, rows, :] = ar.astype(BF16)
            rot_i[c, rows, :] = ai.astype(BF16)
            ar, ai = ar * br - ai * bi, ar * bi + ai * br
        cur_r[rows, :] = ar
        cur_i[rows, :] = ai
        return carry

    lax.fori_loop(0, beams // step, advance, 0)


def steering(beam_steering, inputs, channels, first_channel, chan_total):
    beams = beam_steering.shape[1]
    positions = jnp.arange(inputs, dtype=jnp.int32)
    column = positions // (inputs // 4)
    within = positions % (inputs // 4)
    bits = (
        beam_steering[0][:, None] * column[None, :] * 64
        + beam_steering[1][:, None] * within[None, :]
    ) % 256
    block = math.gcd(channels, 8)
    rot = jax.ShapeDtypeStruct((channels, beams, inputs), BF16)
    rot_spec = pl.BlockSpec((block, beams, inputs), lambda c, b: (c, 0, 0))
    return pl.pallas_call(
        functools.partial(steering_kernel, unit=2.0 * math.pi / (512 * chan_total)),
        out_shape=[rot, rot],
        grid_spec=pltpu.PrefetchScalarGridSpec(
            num_scalar_prefetch=1,
            grid=(channels // block,),
            in_specs=[pl.BlockSpec((beams, inputs), lambda c, b: (0, 0))],
            out_specs=[rot_spec, rot_spec],
            scratch_shapes=[pltpu.VMEM((beams, inputs), F32)] * 4,
        ),
        cost_estimate=pl.CostEstimate(
            flops=8 * rot.size, bytes_accessed=6 * rot.size, transcendentals=0
        ),
        name="steering",
    )(jnp.reshape(chan_total + first_channel, (1,)), bits)


def beam_kernel(x_ref, gain_ref, flag_ref, rot_r, rot_i, power_ref, *, scale):
    for c in range(x_ref.shape[0]):
        x, gains = x_ref[c], gain_ref[c]
        flags = flag_ref[c].astype(F32) * scale
        half = x.shape[0] // 2
        hr, hi = gains[0:1] * flags, gains[1:2] * flags
        xr, xi = x[:half].astype(F32), x[half:].astype(F32)
        v = complex_product(rot_r[c], rot_i[c], xr * hr - xi * hi, xi * hr + xr * hi)
        vr, vi = v[:half], v[half:]
        power_ref[c] = vr * vr + vi * vi


def form_beams(x, gains, flags, rot_r, rot_i):
    channels, rows, inputs = x.shape
    beams = rot_r.shape[1]
    block = math.gcd(channels, 16)
    whole = lambda *shape: pl.BlockSpec((block, *shape), lambda c: (c,) + (0,) * len(shape))
    return pl.pallas_call(
        functools.partial(beam_kernel, scale=1.0 / math.sqrt(inputs)),
        out_shape=jax.ShapeDtypeStruct((channels, rows // 2, beams), F32),
        grid=(channels // block,),
        in_specs=[whole(rows, inputs), whole(2, inputs), whole(1, inputs),
                  whole(beams, inputs), whole(beams, inputs)],
        out_specs=whole(rows // 2, beams),
        cost_estimate=pl.CostEstimate(
            flops=8 * channels * beams * inputs * rows,
            bytes_accessed=4 * rot_r.size, transcendentals=0,
        ),
        name="beams",
    )(x, gains, flags, rot_r, rot_i)


def shards(samples, window_taps, sky_model, prior_gains, beam_steering, input_flags):
    local_inputs = samples.shape[0]
    frames = samples.shape[3]
    kept_count = NCH
    time_count = lax.axis_size("tm")
    chan_count = lax.axis_size("chan")
    beam_count = lax.axis_size("beam")
    owners = time_count * chan_count
    chan_local = kept_count // owners
    me = (lax.axis_index("chan") * time_count + lax.axis_index("tm")).astype(jnp.int32)
    flags = input_flags[:, None, :]
    denom = first_denominators(sky_model, prior_gains, flags)
    real, imag, denom = filter_bank(samples, window_taps, kept_count, denom)
    by_owner = (owners, chan_local, frames * local_inputs)
    spectra = jnp.concatenate([real.reshape(by_owner), imag.reshape(by_owner)], axis=1)
    spectra, beam_steering = lax.optimization_barrier((spectra, beam_steering))
    parts, origin = exchange(spectra, me, ("chan", "tm"))
    input_count = local_inputs * chan_count * beam_count
    rot_r, rot_i = steering(
        beam_steering, input_count, chan_local, me * chan_local, kept_count
    )
    parts, rot_r, rot_i = lax.optimization_barrier((parts, rot_r, rot_i))
    beam = lax.axis_index("beam").astype(jnp.int32)
    mixed = jnp.concatenate(parts, axis=0)
    if beam_count == 2:
        joined, core = jnp.stack([mixed, other_core(mixed)]), beam
    else:
        joined, core = lax.all_gather(mixed, "beam", axis=0), jnp.zeros_like(beam)
    x = turn(jnp.stack([origin, core]), joined, local_inputs, chan_count, time_count)
    beam_index = jnp.reshape(lax.axis_index("beam"), (1,)).astype(jnp.int32)
    visibilities, updated = gain_call(
        beam_index, x, sky_model, prior_gains, prior_gains, flags, denom
    )
    beam_power = form_beams(x, prior_gains, flags, rot_r, rot_i)
    for _ in range(ITERS - 1):
        if beam_count == 2:
            other, beam_power = lax.optimization_barrier((other_core(updated), beam_power))
            current = jnp.where(
                beam == 0,
                jnp.concatenate([updated, other], axis=2),
                jnp.concatenate([other, updated], axis=2),
            )
        else:
            current = lax.all_gather(updated, "beam", axis=2, tiled=True)
        updated = gain_call(beam_index, x, sky_model, current, updated, flags)
    return (visibilities, updated, jnp.transpose(beam_power, (0, 2, 1)))


SPAN = 16
MESH = pl.DeviceIdType.MESH


def row_product(vr, vi, left):
    straight = jnp.concatenate([vr, vi], axis=0).astype(BF16)
    crossed = jnp.concatenate([-vi, vr], axis=0).astype(BF16)
    return dot_nt(straight, left[0]) + dot_nt(crossed, left[1])


def row_numerators(x, own, model, gains, flags):
    half = x.shape[0] // 2
    hr, hi = gains[0:1] * flags, gains[1:2] * flags
    xr, xi = x[:half].astype(F32), x[half:].astype(F32)
    z = row_product(xr * hr + xi * hi, xi * hr - xr * hi, model)
    zr, zi = z[:half], z[half:]
    pr, pi = own[:half].astype(F32), own[half:].astype(F32)
    numer_r = jnp.sum(pr * zr + pi * zi, axis=0, keepdims=True) * (1.0 / half)
    numer_i = jnp.sum(pi * zr - pr * zi, axis=0, keepdims=True) * (1.0 / half)
    return jnp.concatenate([numer_r, numer_i], axis=0)


def row_denominators(model, gains, flags):
    power = flags * (gains[0:1] * gains[0:1] + gains[1:2] * gains[1:2])
    top = power.astype(BF16).astype(F32)
    wide = (8, top.shape[1])
    both = jnp.concatenate(
        [jnp.broadcast_to(top, wide), jnp.broadcast_to(power - top, wide)], axis=0
    ).astype(BF16)
    mr, mi = model[0], model[1]
    d = dot_nt(both, mr * mr + mi * mi)
    return d[0:1] + d[8:9] + epsilon


def short_sincos(angle):
    q = angle * 0.25
    w = q * q
    sine = q * (1.0 + w * (-1.0 / 6 + w * (1.0 / 120 + w * (-1.0 / 5040 + w * (1.0 / 362880)))))
    less = w * (0.5 + w * (-1.0 / 24 + w * (1.0 / 720 + w * (-1.0 / 40320 + w * (1.0 / 3628800)))))
    for _ in range(2):
        cosine = 1.0 - less
        less, sine = 2.0 * sine * sine, 2.0 * sine * cosine
    return sine, 1.0 - less


def phase_rows(count, stride, width):
    row = lax.broadcasted_iota(jnp.int32, (count, width), 0) * stride
    column = lax.broadcasted_iota(jnp.int32, (count, width), 1)
    index = (row * column) & (width - 1)
    index = jnp.where(index >= width // 2, index - width, index)
    return short_sincos(index.astype(F32) * (2.0 * math.pi / width))


def spread_samples(sample_ref, frame_ref, r):
    inputs, _, frames, width = sample_ref.shape

    def spread(i, carry):
        for tile in range(width // 128):
            piece = sample_ref[i, r, :, tile * 128 : (tile + 1) * 128].astype(F32)
            frame_ref[r, tile, pl.ds(i, frames, stride=inputs), :] = piece
        return carry

    lax.fori_loop(0, inputs, spread, 0, unroll=8)


def fill_transform(cos_ref, sin_ref, high_ref):
    kept, width = cos_ref.shape
    coarse = high_ref.shape[1]
    fine = kept // coarse
    scale = 1.0 / math.sqrt(width)
    high_s, high_c = phase_rows(coarse, fine, width)
    high_ref[0], high_ref[1] = high_c * scale, high_s * scale
    low_s, low_c = phase_rows(fine, 1, width)
    high_ref[2, :fine], high_ref[3, :fine] = low_c, low_s

    def rotate(h, carry):
        hc, hs = high_ref[0, pl.ds(h, 1), :], high_ref[1, pl.ds(h, 1), :]
        lc, ls = high_ref[2, :fine], high_ref[3, :fine]
        at = pl.ds(pl.multiple_of(h * fine, fine), fine)
        cos_ref[at, :] = (hc * lc - hs * ls).astype(BF16)
        sin_ref[at, :] = (hs * lc + hc * ls).astype(BF16)
        return carry

    lax.fori_loop(0, coarse, rotate, 0, unroll=2)


def window_frames(frame_ref, tap_ref, win_ref, inputs):
    taps = tap_ref.shape[0]
    after = taps - 1
    frames = frame_ref.shape[2] // inputs

    def window(tile, carry):
        at = pl.ds(pl.multiple_of(tile * 128, 128), 128)
        weight = [jnp.broadcast_to(tap_ref[tap : tap + 1, at], (16, 128)) for tap in range(taps)]
        for r in range(2):
            for block in range(inputs // 16):
                held = [
                    frame_ref[r, tile, f * inputs + block * 16 : f * inputs + block * 16 + 16, :]
                    for f in range(frames)
                ]
                for g in range(frames + after):
                    terms = [
                        held[g + tap - after] * weight[tap]
                        for tap in range(taps) if 0 <= g + tap - after < frames
                    ]
                    to = g * inputs + block * 16
                    win_ref[r, to : to + 16, at] = sum(terms[1:], terms[0]).astype(BF16)
        return carry

    lax.fori_loop(0, frame_ref.shape[1], window, 0)


def paired_denominators(models, gains, flags):
    sums = []
    for model, g, flag in zip(models, gains, flags):
        power = (flag * (g[0:1] * g[0:1] + g[1:2] * g[1:2])).astype(BF16)
        total = None
        for tile in range(power.shape[1] // 128):
            at = slice(tile * 128, (tile + 1) * 128)
            mr, mi = model[0, :, at], model[1, :, at]
            term = (mr * mr + mi * mi) * power[:, at]
            total = term if total is None else total + term
        sums.append(total)
    lane = lax.broadcasted_iota(jnp.int32, (16, 256), 1)
    row = lax.broadcasted_iota(jnp.int32, (16, 256), 0)
    chosen = jnp.where((lane < 128) == (row < 8), 1.0, 0.0).astype(BF16)
    d = dot_nt(chosen, jnp.concatenate(sums, axis=1))
    return d[0:1] + epsilon, d[8:9] + epsilon


def joined_rows(ref, row, pairs, plane, half):
    at = slice(plane * half, (plane + 1) * half)
    low = ref[pl.ds(pl.multiple_of(row, pairs), pairs), at]
    high = ref[pl.ds(pl.multiple_of(row + pairs, pairs), pairs), at]
    return jnp.concatenate([low, high], axis=1)


def pack_tails(real_ref, imag_ref, tail_ref, pairs):
    groups, owners, rows, lanes = tail_ref.shape
    half, late = lanes // 2, rows // (2 * pairs)

    def pack(owner, carry):
        for group in range(groups):
            row = (owner * groups + group) * 2 * pairs
            planes = [
                joined_rows(ref, row, pairs, plane, half)
                for ref in (real_ref, imag_ref) for plane in range(late)
            ]
            tail_ref[group, owner] = jnp.concatenate(planes, axis=0).astype(BF16)
        return carry

    lax.fori_loop(0, owners, pack, 0)


def pack_bodies(real_ref, imag_ref, rows_ref, early_ref, out_ref, group):
    owners, groups, pairs, rows, lanes = out_ref.shape
    half, frames = lanes // 2, rows // 2
    late = early_ref.shape[2] // (2 * pairs)

    def pack(owner, carry):
        row = (owner * groups + group) * 2 * pairs
        early = early_ref[group, owner].astype(F32)
        for s, ref in enumerate((real_ref, imag_ref)):
            for plane in range(frames):
                joined = joined_rows(ref, row, pairs, plane, half)
                if plane < late:
                    at = (s * late + plane) * pairs
                    joined = joined + early[at : at + pairs]
                to = pl.ds(s * frames + plane, pairs, stride=rows)
                rows_ref.at[lax.rem(owner, 2)][to, :] = joined
        packed = rows_ref[lax.rem(owner, 2)].reshape(pairs, rows, lanes).astype(BF16)
        out_ref[owner, group] = packed
        return carry

    lax.fori_loop(0, owners, pack, 0, unroll=2)


def gains_kernel(
    sample_hbm, tap_ref, model_hbm, gain_ref, flag_ref, steer_ref, x_hbm, new_ref, power_hbm,
    send_ref, tail_ref, early_ref, recv, model, full, denom, table, x_ref, power_ref,
    real_ref, imag_ref, rows_ref, send_sem, recv_sem, keep_sem, tail_send, tail_recv,
    pass_send, pass_recv, gain_send, gain_recv, load_sem,
    sample_sem, x_sem, power_sem,
    *, chans, times, kept,
):
    z, t, b = lax.axis_index("chan"), lax.axis_index("tm"), lax.axis_index("beam")
    owners, groups, pairs, rows, lanes = send_ref.shape
    channels, _, mine, inputs = model.shape
    local_inputs, _, frames, width = sample_hbm.shape
    terms, beam_count, _ = table.shape
    taps = tap_ref.shape[0]
    me = z * times + t
    off = pl.multiple_of(b * mine, mine)
    half = lanes // 2
    late = taps - 1
    planes = frames * times
    quad = pairs // 2
    other = {"beam": 1 - b}

    def place(step):
        device = lax.rem(me + step, owners)
        return device, {"chan": lax.div(device, times), "tm": lax.rem(device, times)}

    barrier = pltpu.get_barrier_semaphore()
    for step in range(1, owners):
        pl.semaphore_signal(barrier, inc=1, device_id=place(step)[1], device_id_type=MESH)
    pl.semaphore_signal(barrier, inc=1, device_id=other, device_id_type=MESH)

    def load(g):
        part = pl.ds(g * SPAN, SPAN)
        return pltpu.make_async_copy(model_hbm.at[part], model.at[part], load_sem.at[g])

    def quarter(q):
        return lax.div(q, 2), pl.ds(lax.rem(q, 2) * quad, quad)

    def body_copy(q, step, device, source, where):
        g, cut = quarter(q)
        return pltpu.make_async_remote_copy(
            src_ref=send_ref.at[device, g, cut], dst_ref=recv.at[b, g, source, cut],
            send_sem=send_sem.at[q, step - 1], recv_sem=recv_sem.at[q, step - 1],
            device_id=where, device_id_type=MESH,
        )

    def tail_copy(g, where):
        return pltpu.make_async_remote_copy(
            src_ref=tail_ref.at[g], dst_ref=early_ref.at[g],
            send_sem=tail_send.at[g], recv_sem=tail_recv.at[g],
            device_id={"tm": where}, device_id_type=MESH,
        )

    def outgoing(q, step):
        device, where = place(step)
        return body_copy(q, step, device, me, where)

    def incoming(q, step):
        device, where = place(owners - step)
        return body_copy(q, step, device, device, where)

    def keep(g):
        return pltpu.make_async_copy(send_ref.at[me, g], recv.at[b, g, me], keep_sem.at[g])

    def passing(q, core):
        g, cut = quarter(q)
        part = recv.at[core, g, :, cut]
        return pltpu.make_async_remote_copy(
            src_ref=part, dst_ref=part, send_sem=pass_send.at[q], recv_sem=pass_recv.at[q],
            device_id=other, device_id_type=MESH,
        )

    def sharing(g, start):
        part = full.at[pl.ds(g * SPAN, SPAN), :, pl.ds(start, mine)]
        return pltpu.make_async_remote_copy(
            src_ref=part, dst_ref=part, send_sem=gain_send.at[g], recv_sem=gain_recv.at[g],
            device_id=other, device_id_type=MESH,
        )

    def store_x(g):
        part = pl.ds(g * SPAN, SPAN)
        return pltpu.make_async_copy(x_ref.at[part], x_hbm.at[part], x_sem.at[g])

    def store_power(g):
        part = pl.ds(g * SPAN, SPAN)
        return pltpu.make_async_copy(power_ref.at[part], power_hbm.at[part], power_sem.at[g])

    def send(q, h):
        for step in range(1, owners):
            outgoing(q, step).start()
        if h == 0:
            keep(lax.div(q, 2)).start()

    def sent(q):
        for step in range(1, owners):
            outgoing(q, step).wait_send()

    def pump(q, h):
        send(q + 2, h)

    def pack(g):
        @pl.when(t > 0)
        def _():
            tail_copy(g, t - 1).wait_recv()

        pack_bodies(real_ref, imag_ref, rows_ref, early_ref, send_ref, g)

    def collect(q, g, h):
        for step in range(1, owners):
            incoming(q, step).wait_recv()
        if h == 0:
            keep(g).wait()
        passing(q, b).start()

    def merge(q, g, h):
        passing(q, 1 - b).wait_recv()

        def pair(i, carry):
            p = h * quad + i
            for zz in range(chans):
                sides = []
                for core in range(2):
                    got = [recv[core, g, zz * times + tt, p].astype(F32) for tt in range(times)]
                    sides.append(jnp.concatenate(
                        [r[:frames] for r in got] + [r[frames:] for r in got], axis=0))
                at = slice(zz * lanes, (zz + 1) * lanes)
                for k, cut in enumerate((slice(0, half), slice(half, lanes))):
                    joined = jnp.concatenate([side[:, cut] for side in sides], axis=1)
                    x_ref[g * SPAN + k * pairs + p, :, at] = joined.astype(BF16)
            return carry

        lax.fori_loop(0, quad, pair, 0, unroll=2)

    def zeroth(c):
        flags = flag_ref[pl.ds(c, 1), :].astype(F32)
        denom[c] = row_denominators(model.at[c], gain_ref[c], flags)

    def first(c):
        flags = flag_ref[pl.ds(c, 1), :].astype(F32)
        own = x_ref[c, :, pl.ds(off, mine)]
        numer = row_numerators(x_ref[c], own, model.at[c], gain_ref[c], flags)
        older = gain_ref[c, :, pl.ds(off, mine)]
        full[c, :, pl.ds(off, mine)] = damped(older, numer, denom[c])

    def second(*pair):
        flags = [flag_ref[pl.ds(c, 1), :].astype(F32) for c in pair]
        denoms = paired_denominators([model.at[c] for c in pair], [full[c] for c in pair], flags)
        for c, flag, denominator in zip(pair, flags, denoms):
            own = x_ref[c, :, pl.ds(off, mine)]
            numer = row_numerators(x_ref[c], own, model.at[c], full[c], flag)
            new_ref[c] = damped(full[c, :, pl.ds(off, mine)], numer, denominator)

    def seconds(g, h):
        start = g * SPAN + h * quad
        for k in range(2):
            for j in range(0, quad, 2):
                second(start + k * pairs + j, start + k * pairs + j + 1)

    def each(stage, g, h):
        start = g * SPAN + h * quad
        for k in range(2):
            for j in range(quad):
                stage(start + k * pairs + j)

    unit = 2.0 * math.pi / (512 * kept)
    middle = 2 * (kept + me * channels) + channels - 1

    def front(
        sample_ref, frame_ref, win_ref, cos_ref, sin_ref, high_ref, real_late, imag_late,
    ):
        def fetch(r):
            return pltpu.make_async_copy(
                sample_hbm.at[:, pl.ds(r, 1)], sample_ref.at[:, pl.ds(r, 1)], sample_sem.at[r])

        for r in range(2):
            fetch(r).start()
        for g in range(groups):
            load(g).start()
        fill_transform(cos_ref, sin_ref, high_ref)
        for r in range(2):
            fetch(r).wait()
            spread_samples(sample_ref, frame_ref, r)
        window_frames(frame_ref, tap_ref, win_ref, local_inputs)

        def transform(real_out, imag_out, start):
            at = pl.ds(start, real_out.shape[1])
            real_in, imag_in = win_ref[0, at, :], win_ref[1, at, :]
            real_out[...] = dot_nt(cos_ref[...], real_in) + dot_nt(sin_ref[...], imag_in)
            imag_out[...] = dot_nt(cos_ref[...], imag_in) - dot_nt(sin_ref[...], real_in)

        transform(real_late, imag_late, frames * local_inputs)
        pack_tails(real_late, imag_late, tail_ref, pairs)
        pl.semaphore_wait(barrier, owners)

        @pl.when(t < times - 1)
        def _():
            for g in range(min(2, groups)):
                tail_copy(g, t + 1).start()

        @pl.when(t == 0)
        def _():
            early_ref[...] = jnp.zeros_like(early_ref)

        transform(real_ref, imag_ref, 0)

        @pl.when(t < times - 1)
        def _():
            for g in range(2, groups):
                tail_copy(g - 2, t + 1).wait_send()
                tail_copy(g, t + 1).start()

    columns = (frames + taps - 1) * local_inputs
    coarse = kept >> ((kept.bit_length() - 1) // 2)
    pl.run_scoped(
        front,
        pltpu.VMEM((local_inputs, 2, frames, width), BF16),
        pltpu.VMEM((2, width // 128, frames * local_inputs, 128), F32),
        pltpu.VMEM((2, columns, width), BF16),
        pltpu.VMEM((kept, width), BF16),
        pltpu.VMEM((kept, width), BF16),
        pltpu.VMEM((4, coarse, width), F32),
        pltpu.VMEM((kept, late * local_inputs), F32),
        pltpu.VMEM((kept, late * local_inputs), F32),
    )

    def back(y_ref, sum_ref, bits_ref):
        position = lax.broadcasted_iota(jnp.int32, (8, inputs), 1)
        column = lax.div(position, inputs // 4)
        row = lax.broadcasted_iota(jnp.int32, (8, inputs), 0)
        factor = jnp.where(row == 0, column * 64, position - column * (inputs // 4))
        factor = jnp.where(row < 2, factor, 0).astype(F32).astype(BF16)
        chosen = steer_ref[...].astype(F32)
        chosen = jnp.concatenate([chosen, jnp.zeros((6, beam_count), F32)], axis=0).astype(BF16)
        product = lax.dot_general(chosen, factor, TN, preferred_element_type=F32)
        bits_ref[...] = product.astype(jnp.int32) & 255

        def tabulate(block, carry):
            at = pl.ds(pl.multiple_of(block * 16, 16), 16)
            index = bits_ref[at, :] - 128
            imag, real = short_sincos((index * middle).astype(F32) * (0.5 * unit))
            turned = index.astype(F32) * (unit * channels / 2)
            for k in range(terms):
                if k:
                    scale = turned * (1.0 / k)
                    real, imag = real * scale, imag * scale
                table[k, at, :inputs] = real.astype(BF16)
                table[k, at, inputs:] = imag.astype(BF16)
            return carry

        pack(0)
        lax.fori_loop(0, beam_count // 16, tabulate, 0)
        for h in range(2):
            send(h, h)

        def ready(g):
            load(g).wait()

            def some(i, carry):
                for j in range(8):
                    zeroth(g * SPAN + i * 8 + j)
                return carry

            lax.fori_loop(0, SPAN // 8, some, 0)

        for g in range(groups):
            if g + 1 < groups:
                pack(g + 1)
            ready(g)
            if g in (1, 2) and g + 1 < 2 * groups:
                pump(g - 1, (g - 1) % 2)

        def beams(start):
            count = y_ref.shape[0]

            def prepare(c, carry):
                x, gains = x_ref[start + c], gain_ref[start + c]
                flags = flag_ref[pl.ds(start + c, 1), :].astype(F32) * (1.0 / math.sqrt(inputs))
                hr, hi = gains[0:1] * flags, gains[1:2] * flags
                xr, xi = x[:planes].astype(F32), x[planes:].astype(F32)
                yr = (xr * hr - xi * hi).astype(BF16)
                yi = (xi * hr + xr * hi).astype(BF16)
                y_ref[c, :planes, :inputs] = yr
                y_ref[c, :planes, inputs:] = -yi
                y_ref[c, planes:, :inputs] = yi
                y_ref[c, planes:, inputs:] = yr
                return carry

            lax.fori_loop(0, count, prepare, 0, unroll=4)
            y = y_ref[...].reshape(count * 2 * planes, 2 * inputs)
            for k in range(terms):
                sum_ref[k] = dot_nt(y, table[k])

            def finish(c, carry):
                u = ((start + c).astype(F32) - (channels - 1) / 2) * (2.0 / channels)
                at = pl.ds(pl.multiple_of(c * 2 * planes, 2 * planes), 2 * planes)
                last = sum_ref[terms - 1, at, :]
                vr, vi = last[:planes], last[planes:]
                for k in reversed(range(terms - 1)):
                    term = sum_ref[k, at, :]
                    vr, vi = term[:planes] - u * vi, term[planes:] + u * vr
                power_ref[start + c] = vr * vr + vi * vi
                return carry

            lax.fori_loop(0, count, finish, 0, unroll=4)

        for q in range(2):
            if q + 2 < 2 * groups and not 1 <= q + 1 < groups:
                pump(q, q)
        collect(0, 0, 0)

        def group(g, carry):
            @pl.when(g < groups)
            def _():
                @pl.when(2 * g + 4 < 2 * groups)
                def _():
                    pump(2 * g + 2, 0)

                merge(2 * g, g, 0)
                each(first, g, 0)
                collect(2 * g + 1, g, 1)

                @pl.when(2 * g + 5 < 2 * groups)
                def _():
                    pump(2 * g + 3, 1)

            @pl.when(g >= 1)
            def _():
                sharing(g - 1, pl.multiple_of((1 - b) * mine, mine)).wait_recv()
                seconds(g - 1, 0)

            @pl.when(g < groups)
            def _():
                merge(2 * g + 1, g, 1)
                each(first, g, 1)
                store_x(g).start()

                @pl.when(lax.rem(g, 2) == 1)
                def _():
                    beams((g - 1) * SPAN)

                sharing(g, off).start()

            @pl.when(g + 1 < groups)
            def _():
                collect(2 * g + 2, g + 1, 0)

            @pl.when(g >= 1)
            def _():
                seconds(g - 1, 1)
                store_power(g - 1).start()

            return carry

        lax.fori_loop(0, groups + 1, group, 0)

    wide = 2 * SPAN * 2 * planes
    pl.run_scoped(
        back,
        pltpu.VMEM((2 * SPAN, 2 * planes, 2 * inputs), BF16),
        pltpu.VMEM((terms, wide, beam_count), F32),
        pltpu.VMEM((beam_count, inputs), jnp.int32),
    )

    def drain(g, carry):
        for h in range(2):
            passing(2 * g + h, b).wait_send()

        sharing(g, off).wait_send()
        store_x(g).wait()
        store_power(g).wait()
        return carry

    lax.fori_loop(0, groups, drain, 0)
    for q in range(2 * groups):
        sent(q)

    @pl.when(t < times - 1)
    def _():
        for g in range(max(groups - 2, 0), groups):
            tail_copy(g, t + 1).wait_send()


def solve_gains(samples, window_taps, model, gains, flags, beam_steering, chans, times, kept):
    local_inputs, _, width, frames = samples.shape
    taps = window_taps.shape[0]
    natural = jnp.transpose(samples, (0, 1, 3, 2))
    channels, _, mine, inputs = model.shape
    beams = beam_steering.shape[1]
    owners = chans * times
    groups, pairs, rows, lanes = channels // SPAN, SPAN // 2, 2 * frames, 2 * local_inputs
    terms = series_terms(channels, kept)
    vmem, apart = pl.BlockSpec(memory_space=pltpu.VMEM), pl.BlockSpec(memory_space=pl.ANY)
    dma = pltpu.SemaphoreType.DMA
    late = (taps - 1) * SPAN
    planes = times * frames
    return pl.pallas_call(
        functools.partial(gains_kernel, chans=chans, times=times, kept=kept),
        out_shape=[
            jax.ShapeDtypeStruct((channels, 2 * planes, inputs), BF16),
            jax.ShapeDtypeStruct((channels, 2, mine), F32),
            jax.ShapeDtypeStruct((channels, planes, beams), F32),
        ],
        in_specs=[apart, vmem, apart, vmem, vmem, vmem],
        out_specs=[apart, vmem, apart],
        scratch_shapes=[
            pltpu.VMEM((owners, groups, pairs, rows, lanes), BF16),
            pltpu.VMEM((groups, owners, late, lanes), BF16),
            pltpu.VMEM((groups, owners, late, lanes), BF16),
            pltpu.VMEM((2, groups, owners, pairs, rows, lanes), BF16),
            pltpu.VMEM(model.shape, BF16),
            pltpu.VMEM((channels, 2, inputs), F32),
            pltpu.VMEM((channels, 1, mine), F32),
            pltpu.VMEM((terms, beams, 2 * inputs), BF16),
            pltpu.VMEM((channels, 2 * planes, inputs), BF16),
            pltpu.VMEM((channels, planes, beams), F32),
            pltpu.VMEM((kept, frames * local_inputs), F32),
            pltpu.VMEM((kept, frames * local_inputs), F32),
            pltpu.VMEM((2, pairs * rows, lanes), F32),
            dma((2 * groups, owners - 1)), dma((2 * groups, owners - 1)), dma((groups,)),
            dma((groups,)), dma((groups,)),
            dma((2 * groups,)), dma((2 * groups,)),
            *[dma((groups,))] * 3,
            dma((2,)), dma((groups,)), dma((groups,)),
        ],
        compiler_params=pltpu.CompilerParams(
            collective_id=0, has_side_effects=True, vmem_limit_bytes=67043328
        ),
        cost_estimate=pl.CostEstimate(
            flops=40 * channels * mine * inputs * planes,
            bytes_accessed=2 * model.size, transcendentals=0,
        ),
        name="gains",
    )(natural, window_taps, model, gains, flags, beam_steering)


def correlate_only_kernel(
    x_hbm, new_hbm, power_hbm, vis_hbm, new_out, power_out,
    x_ref, new_ref, power_ref, vis_ref, x_sem, in_sem, out_sem, vis_sem,
):
    slots, block, _, mine, _ = vis_ref.shape
    channels, rows, _ = x_ref.shape
    half = rows // 2
    parts = x_sem.shape[0]
    off = pl.multiple_of(lax.axis_index("beam") * mine, mine)
    exact = half & (half - 1) == 0
    before, after = (1.0 / half, 1.0) if exact else (1.0, 1.0 / half)

    def fetch(k):
        part = pl.ds(k * (channels // parts), channels // parts)
        return pltpu.make_async_copy(x_hbm.at[part], x_ref.at[part], x_sem.at[k])

    for k in range(parts):
        fetch(k).start()
    ins = [pltpu.make_async_copy(new_hbm, new_ref, in_sem.at[0]),
           pltpu.make_async_copy(power_hbm, power_ref, in_sem.at[1])]
    outs = [pltpu.make_async_copy(new_ref, new_out, out_sem.at[0]),
            pltpu.make_async_copy(power_ref, power_out, out_sem.at[1])]
    for copy in ins:
        copy.start()

    def store(i, slot):
        part = pl.ds(i * block, block)
        return pltpu.make_async_copy(vis_ref.at[slot], vis_hbm.at[part], vis_sem.at[slot])

    def step(i, carry):
        slot = lax.rem(i, slots)

        @pl.when(i >= slots)
        def _():
            store(i - slots, slot).wait()

        for j in range(block):
            x = x_ref[i * block + j]
            own = x_ref[i * block + j, :, pl.ds(off, mine)]
            scaled = (own.astype(F32) * before).astype(BF16)
            rotated = jnp.concatenate([scaled[half:], -scaled[:half]], axis=0)
            for part, left in enumerate((scaled, rotated)):
                terms = lax.dot_general(left, x, TN, preferred_element_type=F32)
                vis_ref[slot, j, part] = (terms if exact else terms * after).astype(BF16)
        store(i, slot).start()
        return carry

    steps = channels // block
    each = steps // parts
    for k in range(parts):
        fetch(k).wait()
        lax.fori_loop(k * each, (k + 1) * each, step, 0)
        if k == 0:
            for first, last in zip(ins, outs):
                first.wait()
                last.start()
    for copy in outs:
        copy.wait()
    for i in range(max(steps - slots, 0), steps):
        store(i, i % slots).wait()


def correlate(x, new, power):
    channels, rows, inputs = x.shape
    mine = new.shape[2]
    block, parts, slots = 4, 4, 3
    apart = pl.BlockSpec(memory_space=pl.ANY)
    dma = pltpu.SemaphoreType.DMA
    return pl.pallas_call(
        correlate_only_kernel,
        out_shape=[
            jax.ShapeDtypeStruct((channels, 2, mine, inputs), BF16),
            jax.ShapeDtypeStruct(new.shape, F32),
            jax.ShapeDtypeStruct(power.shape, F32),
        ],
        in_specs=[apart] * 3,
        out_specs=[apart] * 3,
        scratch_shapes=[
            pltpu.VMEM(x.shape, BF16), pltpu.VMEM(new.shape, F32), pltpu.VMEM(power.shape, F32),
            pltpu.VMEM((slots, block, 2, mine, inputs), BF16),
            dma((parts,)), dma((2,)), dma((2,)), dma((slots,)),
        ],
        cost_estimate=pl.CostEstimate(
            flops=4 * channels * mine * inputs * rows,
            bytes_accessed=4 * channels * mine * inputs, transcendentals=0,
        ),
        name="correlate_only",
    )(x, new, power)


def series_terms(channels, chan_total):
    reach = 128 * (channels / 2) * 2.0 * math.pi / (512 * chan_total)
    terms, left = 1, reach
    while left >= 2.0**-23:
        terms += 1
        left *= reach / terms
    return terms


def tiled_shards(samples, window_taps, sky_model, prior_gains, beam_steering, input_flags):
    x, new, power = solve_gains(
        samples, window_taps, sky_model, prior_gains, input_flags, beam_steering,
        lax.axis_size("chan"), lax.axis_size("tm"), NCH,
    )
    visibilities, new, power = correlate(x, new, power)
    return visibilities, new, jnp.transpose(power, (0, 2, 1))


def tiles(samples, window_taps, sky_model, prior_gains, beam_steering, input_flags):
    owners = lax.axis_size("tm") * lax.axis_size("chan")
    local_inputs, frames = samples.shape[0], samples.shape[3]
    return (
        ITERS == 2
        and lax.axis_size("beam") == 2
        and owners > 1
        and 2 * local_inputs == 128
        and frames == 8
        and 1 < window_taps.shape[0] <= frames
        and samples.shape[2] & (samples.shape[2] - 1) == 0
        and lax.axis_size("tm") % 2 == 0
        and NCH % (2 * owners * SPAN) == 0
        and sky_model.size <= 1 << 24
    )


def any_shards(*args):
    return tiled_shards(*args) if tiles(*args) else shards(*args)


def solution(mesh):
    return jax.shard_map(
        any_shards,
        mesh=mesh,
        in_specs=(
            P(("group", "chan", "beam"), None, None, "tm"),
            P(),
            P(("group", "chan", "tm"), None, "beam", None),
            P(("group", "chan", "tm"), None, None),
            P(None, ("group", "beam")),
            P(("group", "chan", "tm"), None),
        ),
        out_specs=(
            P(("group", "chan", "tm"), None, "beam", None),
            P(("group", "chan", "tm"), None, "beam"),
            P(("group", "chan", "tm"), "beam", None),
        ),
        check_vma=False,
    )
```

```python
import functools
import math

import jax
import jax.numpy as jnp
from jax import lax
from jax.experimental import pallas as pl
from jax.experimental.pallas import tpu as pltpu
from jax.sharding import PartitionSpec as P

NCH = 512
ITERS = 2


damping = 0.5
epsilon = 1e-06
F32 = jnp.float32
BF16 = jnp.bfloat16


def from_behind(block, axis, distance):
    devices = range(lax.axis_size(axis))
    route = [(i - distance, i) for i in devices if i - distance in devices]
    return lax.ppermute(block, axis, route)


def unit_rows(rows, columns, transform_count):
    phases = (rows[:, None] * columns[None, :] % transform_count).astype(F32) * (
        2.0 * math.pi / transform_count
    )
    return jnp.cos(phases), jnp.sin(phases)


def transform_rows(kept_count, transform_count):
    fine = 1 << ((kept_count.bit_length() - 1) // 2)
    coarse = kept_count // fine
    columns = jnp.arange(transform_count, dtype=jnp.int32)
    high_c, high_s = unit_rows(jnp.arange(coarse, dtype=jnp.int32) * fine, columns, transform_count)
    low_c, low_s = unit_rows(jnp.arange(fine, dtype=jnp.int32), columns, transform_count)
    high_c, high_s, low_c, low_s = lax.optimization_barrier((high_c, high_s, low_c, low_s))
    scale = 1.0 / math.sqrt(transform_count)
    return high_c * scale, high_s * scale, low_c, low_s


def transform_table(kept_count, transform_count):
    high_c, high_s, low_c, low_s = transform_rows(kept_count, transform_count)
    cosine = high_c[:, None] * low_c[None] - high_s[:, None] * low_s[None]
    sine = high_s[:, None] * low_c[None] + high_c[:, None] * low_s[None]
    cosine = cosine.reshape(kept_count, transform_count).astype(BF16)
    sine = sine.reshape(kept_count, transform_count).astype(BF16)
    return cosine, sine


def windowed_frames(samples, window_taps, beside):
    frames = samples.shape[3]
    tap_count = window_taps.shape[0]
    framed = jnp.transpose(samples, (3, 1, 0, 2))
    previous = from_behind(framed[frames - tap_count + 1 :], "tm", 1)
    previous, beside = lax.optimization_barrier((previous, beside))
    extended = jnp.concatenate([previous, framed], axis=0).astype(F32)
    windowed = sum(
        extended[tap : tap + frames] * window_taps[tap][None, None, None, :]
        for tap in range(tap_count)
    )
    return windowed.astype(BF16), beside


def filter_bank(samples, window_taps, kept_count, beside):
    local_inputs, _, transform_count, frames = samples.shape
    windowed, beside = windowed_frames(samples, window_taps, beside)
    real_in = windowed[:, 0].reshape(frames * local_inputs, transform_count)
    imag_in = windowed[:, 1].reshape(frames * local_inputs, transform_count)
    cosine, sine = transform_table(kept_count, transform_count)
    real = dot_nt(cosine, real_in) + dot_nt(sine, imag_in)
    imag = dot_nt(cosine, imag_in) - dot_nt(sine, real_in)
    return real.astype(BF16), imag.astype(BF16), beside


NT = (((1,), (1,)), ((), ()))
TN = (((0,), (0,)), ((), ()))


def dot_nt(a, b):
    return lax.dot_general(a, b, NT, preferred_element_type=F32)


def complex_product(left_r, left_i, vr, vi):
    straight = jnp.concatenate([vr, vi], axis=0).astype(BF16)
    crossed = jnp.concatenate([-vi, vr], axis=0).astype(BF16)
    return (dot_nt(left_r, straight) + dot_nt(left_i, crossed)).T


def numerators(x, own, model, gains, flags):
    half = x.shape[0] // 2
    hr, hi = gains[0:1] * flags, gains[1:2] * flags
    xr, xi = x[:half].astype(F32), x[half:].astype(F32)
    z = complex_product(model[0], model[1], xr * hr + xi * hi, xi * hr - xr * hi)
    zr, zi = z[:half], z[half:]
    pr, pi = own[:half].astype(F32), own[half:].astype(F32)
    numer_r = jnp.sum(pr * zr + pi * zi, axis=0, keepdims=True) * (1.0 / half)
    numer_i = jnp.sum(pi * zr - pr * zi, axis=0, keepdims=True) * (1.0 / half)
    return jnp.concatenate([numer_r, numer_i], axis=0)


def denominators(model, gains, flags):
    power = flags * (gains[0:1] * gains[0:1] + gains[1:2] * gains[1:2])
    top = power.astype(BF16).astype(F32)
    wide = (8, top.shape[1])
    both = jnp.concatenate(
        [jnp.broadcast_to(top, wide), jnp.broadcast_to(power - top, wide)], axis=0
    ).astype(BF16)
    mr, mi = model[0], model[1]
    d = dot_nt(mr * mr + mi * mi, both).T
    return d[0:1] + d[8:9] + epsilon


def damped(older, numer, denom):
    return damping * older + (1.0 - damping) * (numer / denom)


def denominator_kernel(model_ref, gain_ref, flag_ref, out_ref):
    for c in range(model_ref.shape[0]):
        out_ref[c] = denominators(model_ref.at[c], gain_ref[c], flag_ref[c].astype(F32))


def first_denominators(model, gains, flags):
    channels, _, mine, inputs = model.shape
    block = math.gcd(channels, 8)
    whole = lambda *shape: pl.BlockSpec((block, *shape), lambda c: (c,) + (0,) * len(shape))
    return pl.pallas_call(
        denominator_kernel,
        out_shape=jax.ShapeDtypeStruct((channels, 1, mine), F32),
        grid=(channels // block,),
        in_specs=[whole(2, mine, inputs), whole(2, inputs), whole(1, inputs)],
        out_specs=whole(1, mine),
        cost_estimate=pl.CostEstimate(
            flops=16 * model.size, bytes_accessed=2 * model.size, transcendentals=0
        ),
        name="denominators",
    )(model, gains, flags)


def correlate_kernel(beam_ref, x_ref, own_ref, model_ref, gain_ref, older_ref, flag_ref, denom_ref, vis_ref, new_ref):
    for c in range(x_ref.shape[0]):
        x, own = x_ref[c], own_ref[c]
        half = x.shape[0] // 2
        exact = half & (half - 1) == 0
        before, after = (1.0 / half, 1.0) if exact else (1.0, 1.0 / half)
        scaled = (own.astype(F32) * before).astype(BF16)
        rotated = jnp.concatenate([scaled[half:], -scaled[:half]], axis=0)
        for part, left in enumerate((scaled, rotated)):
            terms = lax.dot_general(left, x, TN, preferred_element_type=F32)
            vis_ref[c, part] = (terms if exact else terms * after).astype(BF16)
        numer = numerators(x, own, model_ref.at[c], gain_ref[c], flag_ref[c].astype(F32))
        new_ref[c] = damped(older_ref[c], numer, denom_ref[c])


def update_kernel(beam_ref, x_ref, own_ref, model_ref, gain_ref, older_ref, flag_ref, new_ref):
    for c in range(x_ref.shape[0]):
        model, gains, flags = model_ref.at[c], gain_ref[c], flag_ref[c].astype(F32)
        numer = numerators(x_ref[c], own_ref[c], model, gains, flags)
        new_ref[c] = damped(older_ref[c], numer, denominators(model, gains, flags))


def turn_kernel(me_ref, in_ref, out_ref, rows_ref, *, inputs, chans, times):
    beams, _, paired, lanes = in_ref.shape
    frames = lanes // inputs
    planes = times * frames
    width = rows_ref.shape[2]
    for b in range(beams):
        for z in range(chans):
            column = (z * beams + b) * inputs
            at = column % width
            for t in range(times):
                slab = in_ref[b ^ me_ref[1], (z * times + t) ^ me_ref[0]].astype(F32)
                for f in range(frames):
                    plane = t * frames + f
                    rows_ref[
                        column // width, plane * paired : (plane + 1) * paired, at : at + inputs
                    ] = slab[:, f * inputs : (f + 1) * inputs]

    def gather(k, carry):
        for q in range(rows_ref.shape[0]):
            parts = [
                rows_ref.at[q][pl.ds(s * (paired // 2) + k, planes, stride=paired), :]
                for s in range(2)
            ]
            out_ref[k, :, q * width : (q + 1) * width] = jnp.concatenate(parts, axis=0).astype(BF16)
        return carry

    lax.fori_loop(0, paired // 2, gather, 0)


def turn(me, joined, inputs, chans, times):
    beams, _, paired, lanes = joined.shape
    planes = times * (lanes // inputs)
    total = chans * beams * inputs
    width = 128
    whole = lambda *shape: pl.BlockSpec(shape, lambda c, m: (0,) * len(shape))
    out_dims = (paired // 2, 2 * planes, total)
    return pl.pallas_call(
        functools.partial(turn_kernel, inputs=inputs, chans=chans, times=times),
        out_shape=jax.ShapeDtypeStruct(out_dims, BF16),
        grid_spec=pltpu.PrefetchScalarGridSpec(
            num_scalar_prefetch=1,
            grid=(1,),
            in_specs=[whole(*joined.shape)],
            out_specs=whole(*out_dims),
            scratch_shapes=[pltpu.VMEM((total // width, planes * paired, width), F32)],
        ),
        cost_estimate=pl.CostEstimate(
            flops=0, bytes_accessed=8 * joined.size, transcendentals=0
        ),
        name="turn",
    )(me, joined)


def other_core(block):
    return lax.ppermute(block, "beam", [(0, 1), (1, 0)])


def exchange(blocks, me, axes):
    owners = blocks.shape[0]
    if owners > 8 or owners & (owners - 1):
        mixed = lax.all_to_all(blocks, axes, split_axis=0, concat_axis=0, tiled=True)
        return [mixed], jnp.zeros_like(me)
    parts = []
    for step in range(owners):
        block = lax.dynamic_slice_in_dim(blocks, me ^ step, 1, 0)
        if step:
            block = lax.ppermute(block, axes, [(i, i ^ step) for i in range(owners)])
        parts.append(block)
    return parts, me


def gain_call(beam_index, x, model, gains, older, flags, denom=None):
    correlate = denom is not None
    channels, rows, inputs = x.shape
    mine = model.shape[2]
    block = math.gcd(channels, 8)
    whole = lambda *shape: pl.BlockSpec((block, *shape), lambda c, b: (c,) + (0,) * len(shape))
    part = lambda r: pl.BlockSpec((block, r, mine), lambda c, b: (c, 0, b[0]))
    older_spec = part(2) if older.shape[2] == inputs else whole(2, mine)
    new_shape = jax.ShapeDtypeStruct((channels, 2, mine), F32)
    if correlate:
        out_shape = [jax.ShapeDtypeStruct(model.shape, BF16), new_shape]
        out_specs = [whole(2, mine, inputs), whole(2, mine)]
    else:
        out_shape, out_specs = new_shape, whole(2, mine)
    return pl.pallas_call(
        correlate_kernel if correlate else update_kernel,
        out_shape=out_shape,
        grid_spec=pltpu.PrefetchScalarGridSpec(
            num_scalar_prefetch=1,
            grid=(channels // block,),
            in_specs=[whole(rows, inputs), part(rows), whole(2, mine, inputs), whole(2, inputs),
                      older_spec, whole(1, inputs)] + [whole(1, mine)] * correlate,
            out_specs=out_specs,
        ),
        cost_estimate=pl.CostEstimate(
            flops=8 * channels * mine * inputs * rows,
            bytes_accessed=(4 + 4 * correlate) * model.size // 2,
            transcendentals=0,
        ),
        name="correlate" if correlate else "update",
    )(beam_index, x, x, model, gains, older, flags, *([denom] if correlate else []))


def steering_kernel(base_ref, bits_ref, rot_r, rot_i, cur_r, cur_i, one_r, one_i, *, unit):
    block = rot_r.shape[0]
    beams, inputs = cur_r.shape
    step = 16

    @pl.when(pl.program_id(0) == 0)
    def _():
        first = base_ref[0]

        def fill(r, carry):
            rows = pl.ds(r * 8, 8)
            bits = bits_ref[rows, :]
            angle = (bits * first).astype(F32) * unit
            cur_r[rows, :] = jnp.cos(angle)
            cur_i[rows, :] = jnp.sin(angle)
            small = bits.astype(F32) * unit
            one_r[rows, :] = jnp.cos(small)
            one_i[rows, :] = jnp.sin(small)
            return carry

        lax.fori_loop(0, beams // 8, fill, 0)

    def advance(r, carry):
        rows = pl.ds(r * step, step)
        ar, ai = cur_r[rows, :], cur_i[rows, :]
        br, bi = one_r[rows, :], one_i[rows, :]
        for c in range(block):
            rot_r[c, rows, :] = ar.astype(BF16)
            rot_i[c, rows, :] = ai.astype(BF16)
            ar, ai = ar * br - ai * bi, ar * bi + ai * br
        cur_r[rows, :] = ar
        cur_i[rows, :] = ai
        return carry

    lax.fori_loop(0, beams // step, advance, 0)


def steering(beam_steering, inputs, channels, first_channel, chan_total):
    beams = beam_steering.shape[1]
    positions = jnp.arange(inputs, dtype=jnp.int32)
    column = positions // (inputs // 4)
    within = positions % (inputs // 4)
    bits = (
        beam_steering[0][:, None] * column[None, :] * 64
        + beam_steering[1][:, None] * within[None, :]
    ) % 256
    block = math.gcd(channels, 8)
    rot = jax.ShapeDtypeStruct((channels, beams, inputs), BF16)
    rot_spec = pl.BlockSpec((block, beams, inputs), lambda c, b: (c, 0, 0))
    return pl.pallas_call(
        functools.partial(steering_kernel, unit=2.0 * math.pi / (512 * chan_total)),
        out_shape=[rot, rot],
        grid_spec=pltpu.PrefetchScalarGridSpec(
            num_scalar_prefetch=1,
            grid=(channels // block,),
            in_specs=[pl.BlockSpec((beams, inputs), lambda c, b: (0, 0))],
            out_specs=[rot_spec, rot_spec],
            scratch_shapes=[pltpu.VMEM((beams, inputs), F32)] * 4,
        ),
        cost_estimate=pl.CostEstimate(
            flops=8 * rot.size, bytes_accessed=6 * rot.size, transcendentals=0
        ),
        name="steering",
    )(jnp.reshape(chan_total + first_channel, (1,)), bits)


def beam_kernel(x_ref, gain_ref, flag_ref, rot_r, rot_i, power_ref, *, scale):
    for c in range(x_ref.shape[0]):
        x, gains = x_ref[c], gain_ref[c]
        flags = flag_ref[c].astype(F32) * scale
        half = x.shape[0] // 2
        hr, hi = gains[0:1] * flags, gains[1:2] * flags
        xr, xi = x[:half].astype(F32), x[half:].astype(F32)
        v = complex_product(rot_r[c], rot_i[c], xr * hr - xi * hi, xi * hr + xr * hi)
        vr, vi = v[:half], v[half:]
        power_ref[c] = vr * vr + vi * vi


def form_beams(x, gains, flags, rot_r, rot_i):
    channels, rows, inputs = x.shape
    beams = rot_r.shape[1]
    block = math.gcd(channels, 16)
    whole = lambda *shape: pl.BlockSpec((block, *shape), lambda c: (c,) + (0,) * len(shape))
    return pl.pallas_call(
        functools.partial(beam_kernel, scale=1.0 / math.sqrt(inputs)),
        out_shape=jax.ShapeDtypeStruct((channels, rows // 2, beams), F32),
        grid=(channels // block,),
        in_specs=[whole(rows, inputs), whole(2, inputs), whole(1, inputs),
                  whole(beams, inputs), whole(beams, inputs)],
        out_specs=whole(rows // 2, beams),
        cost_estimate=pl.CostEstimate(
            flops=8 * channels * beams * inputs * rows,
            bytes_accessed=4 * rot_r.size, transcendentals=0,
        ),
        name="beams",
    )(x, gains, flags, rot_r, rot_i)


def shards(samples, window_taps, sky_model, prior_gains, beam_steering, input_flags):
    local_inputs = samples.shape[0]
    frames = samples.shape[3]
    kept_count = NCH
    time_count = lax.axis_size("tm")
    chan_count = lax.axis_size("chan")
    beam_count = lax.axis_size("beam")
    owners = time_count * chan_count
    chan_local = kept_count // owners
    me = (lax.axis_index("chan") * time_count + lax.axis_index("tm")).astype(jnp.int32)
    flags = input_flags[:, None, :]
    denom = first_denominators(sky_model, prior_gains, flags)
    real, imag, denom = filter_bank(samples, window_taps, kept_count, denom)
    by_owner = (owners, chan_local, frames * local_inputs)
    spectra = jnp.concatenate([real.reshape(by_owner), imag.reshape(by_owner)], axis=1)
    spectra, beam_steering = lax.optimization_barrier((spectra, beam_steering))
    parts, origin = exchange(spectra, me, ("chan", "tm"))
    input_count = local_inputs * chan_count * beam_count
    rot_r, rot_i = steering(
        beam_steering, input_count, chan_local, me * chan_local, kept_count
    )
    parts, rot_r, rot_i = lax.optimization_barrier((parts, rot_r, rot_i))
    beam = lax.axis_index("beam").astype(jnp.int32)
    mixed = jnp.concatenate(parts, axis=0)
    if beam_count == 2:
        joined, core = jnp.stack([mixed, other_core(mixed)]), beam
    else:
        joined, core = lax.all_gather(mixed, "beam", axis=0), jnp.zeros_like(beam)
    x = turn(jnp.stack([origin, core]), joined, local_inputs, chan_count, time_count)
    beam_index = jnp.reshape(lax.axis_index("beam"), (1,)).astype(jnp.int32)
    visibilities, updated = gain_call(
        beam_index, x, sky_model, prior_gains, prior_gains, flags, denom
    )
    beam_power = form_beams(x, prior_gains, flags, rot_r, rot_i)
    for _ in range(ITERS - 1):
        if beam_count == 2:
            other, beam_power = lax.optimization_barrier((other_core(updated), beam_power))
            current = jnp.where(
                beam == 0,
                jnp.concatenate([updated, other], axis=2),
                jnp.concatenate([other, updated], axis=2),
            )
        else:
            current = lax.all_gather(updated, "beam", axis=2, tiled=True)
        updated = gain_call(beam_index, x, sky_model, current, updated, flags)
    return (visibilities, updated, jnp.transpose(beam_power, (0, 2, 1)))


SPAN = 16
MESH = pl.DeviceIdType.MESH


def row_product(vr, vi, left):
    straight = jnp.concatenate([vr, vi], axis=0).astype(BF16)
    crossed = jnp.concatenate([-vi, vr], axis=0).astype(BF16)
    return dot_nt(straight, left[0]) + dot_nt(crossed, left[1])


def row_numerators(x, own, model, gains, flags):
    half = x.shape[0] // 2
    hr, hi = gains[0:1] * flags, gains[1:2] * flags
    xr, xi = x[:half].astype(F32), x[half:].astype(F32)
    z = row_product(xr * hr + xi * hi, xi * hr - xr * hi, model)
    zr, zi = z[:half], z[half:]
    pr, pi = own[:half].astype(F32), own[half:].astype(F32)
    numer_r = jnp.sum(pr * zr + pi * zi, axis=0, keepdims=True) * (1.0 / half)
    numer_i = jnp.sum(pi * zr - pr * zi, axis=0, keepdims=True) * (1.0 / half)
    return jnp.concatenate([numer_r, numer_i], axis=0)


def row_denominators(model, gains, flags):
    power = flags * (gains[0:1] * gains[0:1] + gains[1:2] * gains[1:2])
    top = power.astype(BF16).astype(F32)
    wide = (8, top.shape[1])
    both = jnp.concatenate(
        [jnp.broadcast_to(top, wide), jnp.broadcast_to(power - top, wide)], axis=0
    ).astype(BF16)
    mr, mi = model[0], model[1]
    d = dot_nt(both, mr * mr + mi * mi)
    return d[0:1] + d[8:9] + epsilon


def short_sincos(angle):
    q = angle * 0.25
    w = q * q
    sine = q * (1.0 + w * (-1.0 / 6 + w * (1.0 / 120 + w * (-1.0 / 5040 + w * (1.0 / 362880)))))
    less = w * (0.5 + w * (-1.0 / 24 + w * (1.0 / 720 + w * (-1.0 / 40320 + w * (1.0 / 3628800)))))
    for _ in range(2):
        cosine = 1.0 - less
        less, sine = 2.0 * sine * sine, 2.0 * sine * cosine
    return sine, 1.0 - less


def phase_rows(count, stride, width):
    row = lax.broadcasted_iota(jnp.int32, (count, width), 0) * stride
    column = lax.broadcasted_iota(jnp.int32, (count, width), 1)
    index = (row * column) & (width - 1)
    index = jnp.where(index >= width // 2, index - width, index)
    return short_sincos(index.astype(F32) * (2.0 * math.pi / width))


def spread_samples(sample_ref, frame_ref, r):
    inputs, _, frames, width = sample_ref.shape

    def spread(i, carry):
        for tile in range(width // 128):
            piece = sample_ref[i, r, :, tile * 128 : (tile + 1) * 128].astype(F32)
            frame_ref[r, tile, pl.ds(i, frames, stride=inputs), :] = piece
        return carry

    lax.fori_loop(0, inputs, spread, 0, unroll=8)


def fill_transform(cos_ref, sin_ref, high_ref):
    kept, width = cos_ref.shape
    coarse = high_ref.shape[1]
    fine = kept // coarse
    scale = 1.0 / math.sqrt(width)
    high_s, high_c = phase_rows(coarse, fine, width)
    high_ref[0], high_ref[1] = high_c * scale, high_s * scale
    low_s, low_c = phase_rows(fine, 1, width)
    high_ref[2, :fine], high_ref[3, :fine] = low_c, low_s

    def rotate(h, carry):
        hc, hs = high_ref[0, pl.ds(h, 1), :], high_ref[1, pl.ds(h, 1), :]
        lc, ls = high_ref[2, :fine], high_ref[3, :fine]
        at = pl.ds(pl.multiple_of(h * fine, fine), fine)
        cos_ref[at, :] = (hc * lc - hs * ls).astype(BF16)
        sin_ref[at, :] = (hs * lc + hc * ls).astype(BF16)
        return carry

    lax.fori_loop(0, coarse, rotate, 0, unroll=2)


def window_frames(frame_ref, tap_ref, win_ref, inputs):
    taps = tap_ref.shape[0]
    after = taps - 1
    frames = frame_ref.shape[2] // inputs

    def window(tile, carry):
        at = pl.ds(pl.multiple_of(tile * 128, 128), 128)
        weight = [jnp.broadcast_to(tap_ref[tap : tap + 1, at], (16, 128)) for tap in range(taps)]
        for r in range(2):
            for block in range(inputs // 16):
                held = [
                    frame_ref[r, tile, f * inputs + block * 16 : f * inputs + block * 16 + 16, :]
                    for f in range(frames)
                ]
                for g in range(frames + after):
                    terms = [
                        held[g + tap - after] * weight[tap]
                        for tap in range(taps) if 0 <= g + tap - after < frames
                    ]
                    to = g * inputs + block * 16
                    win_ref[r, to : to + 16, at] = sum(terms[1:], terms[0]).astype(BF16)
        return carry

    lax.fori_loop(0, frame_ref.shape[1], window, 0)


def paired_denominators(models, gains, flags):
    sums = []
    for model, g, flag in zip(models, gains, flags):
        power = (flag * (g[0:1] * g[0:1] + g[1:2] * g[1:2])).astype(BF16)
        total = None
        for tile in range(power.shape[1] // 128):
            at = slice(tile * 128, (tile + 1) * 128)
            mr, mi = model[0, :, at], model[1, :, at]
            term = (mr * mr + mi * mi) * power[:, at]
            total = term if total is None else total + term
        sums.append(total)
    lane = lax.broadcasted_iota(jnp.int32, (16, 256), 1)
    row = lax.broadcasted_iota(jnp.int32, (16, 256), 0)
    chosen = jnp.where((lane < 128) == (row < 8), 1.0, 0.0).astype(BF16)
    d = dot_nt(chosen, jnp.concatenate(sums, axis=1))
    return d[0:1] + epsilon, d[8:9] + epsilon


def joined_rows(ref, row, pairs, plane, half):
    at = slice(plane * half, (plane + 1) * half)
    low = ref[pl.ds(pl.multiple_of(row, pairs), pairs), at]
    high = ref[pl.ds(pl.multiple_of(row + pairs, pairs), pairs), at]
    return jnp.concatenate([low, high], axis=1)


def pack_tails(real_ref, imag_ref, tail_ref, pairs):
    groups, owners, rows, lanes = tail_ref.shape
    half, late = lanes // 2, rows // (2 * pairs)

    def pack(owner, carry):
        for group in range(groups):
            row = (owner * groups + group) * 2 * pairs
            planes = [
                joined_rows(ref, row, pairs, plane, half)
                for ref in (real_ref, imag_ref) for plane in range(late)
            ]
            tail_ref[group, owner] = jnp.concatenate(planes, axis=0).astype(BF16)
        return carry

    lax.fori_loop(0, owners, pack, 0)


def pack_bodies(real_ref, imag_ref, rows_ref, early_ref, out_ref, group):
    owners, groups, pairs, rows, lanes = out_ref.shape
    half, frames = lanes // 2, rows // 2
    late = early_ref.shape[2] // (2 * pairs)

    def pack(owner, carry):
        row = (owner * groups + group) * 2 * pairs
        early = early_ref[group, owner].astype(F32)
        for s, ref in enumerate((real_ref, imag_ref)):
            for plane in range(frames):
                joined = joined_rows(ref, row, pairs, plane, half)
                if plane < late:
                    at = (s * late + plane) * pairs
                    joined = joined + early[at : at + pairs]
                to = pl.ds(s * frames + plane, pairs, stride=rows)
                rows_ref.at[lax.rem(owner, 2)][to, :] = joined
        packed = rows_ref[lax.rem(owner, 2)].reshape(pairs, rows, lanes).astype(BF16)
        out_ref[owner, group] = packed
        return carry

    lax.fori_loop(0, owners, pack, 0, unroll=2)


def gains_kernel(
    sample_hbm, tap_ref, model_hbm, gain_ref, flag_ref, steer_ref, x_hbm, new_ref, power_hbm,
    send_ref, tail_ref, early_ref, recv, model, full, denom, table, x_ref, power_ref,
    real_ref, imag_ref, rows_ref, send_sem, recv_sem, keep_sem, tail_send, tail_recv,
    pass_send, pass_recv, gain_send, gain_recv, load_sem,
    sample_sem, x_sem, power_sem,
    *, chans, times, kept,
):
    z, t, b = lax.axis_index("chan"), lax.axis_index("tm"), lax.axis_index("beam")
    owners, groups, pairs, rows, lanes = send_ref.shape
    channels, _, mine, inputs = model.shape
    local_inputs, _, frames, width = sample_hbm.shape
    terms, beam_count, _ = table.shape
    taps = tap_ref.shape[0]
    me = z * times + t
    off = pl.multiple_of(b * mine, mine)
    half = lanes // 2
    late = taps - 1
    planes = frames * times
    quad = pairs // 2
    other = {"beam": 1 - b}

    def place(step):
        device = lax.rem(me + step, owners)
        return device, {"chan": lax.div(device, times), "tm": lax.rem(device, times)}

    barrier = pltpu.get_barrier_semaphore()
    for step in range(1, owners):
        pl.semaphore_signal(barrier, inc=1, device_id=place(step)[1], device_id_type=MESH)
    pl.semaphore_signal(barrier, inc=1, device_id=other, device_id_type=MESH)

    def load(g):
        part = pl.ds(g * SPAN, SPAN)
        return pltpu.make_async_copy(model_hbm.at[part], model.at[part], load_sem.at[g])

    def quarter(q):
        return lax.div(q, 2), pl.ds(lax.rem(q, 2) * quad, quad)

    def body_copy(q, step, device, source, where):
        g, cut = quarter(q)
        return pltpu.make_async_remote_copy(
            src_ref=send_ref.at[device, g, cut], dst_ref=recv.at[b, g, source, cut],
            send_sem=send_sem.at[q, step - 1], recv_sem=recv_sem.at[q, step - 1],
            device_id=where, device_id_type=MESH,
        )

    def tail_copy(g, where):
        return pltpu.make_async_remote_copy(
            src_ref=tail_ref.at[g], dst_ref=early_ref.at[g],
            send_sem=tail_send.at[g], recv_sem=tail_recv.at[g],
            device_id={"tm": where}, device_id_type=MESH,
        )

    def outgoing(q, step):
        device, where = place(step)
        return body_copy(q, step, device, me, where)

    def incoming(q, step):
        device, where = place(owners - step)
        return body_copy(q, step, device, device, where)

    def keep(g):
        return pltpu.make_async_copy(send_ref.at[me, g], recv.at[b, g, me], keep_sem.at[g])

    def passing(q, core):
        g, cut = quarter(q)
        part = recv.at[core, g, :, cut]
        return pltpu.make_async_remote_copy(
            src_ref=part, dst_ref=part, send_sem=pass_send.at[q], recv_sem=pass_recv.at[q],
            device_id=other, device_id_type=MESH,
        )

    def sharing(g, start):
        part = full.at[pl.ds(g * SPAN, SPAN), :, pl.ds(start, mine)]
        return pltpu.make_async_remote_copy(
            src_ref=part, dst_ref=part, send_sem=gain_send.at[g], recv_sem=gain_recv.at[g],
            device_id=other, device_id_type=MESH,
        )

    def store_x(g):
        part = pl.ds(g * SPAN, SPAN)
        return pltpu.make_async_copy(x_ref.at[part], x_hbm.at[part], x_sem.at[g])

    def store_power(g):
        part = pl.ds(g * SPAN, SPAN)
        return pltpu.make_async_copy(power_ref.at[part], power_hbm.at[part], power_sem.at[g])

    def send(q, h):
        for step in range(1, owners):
            outgoing(q, step).start()
        if h == 0:
            keep(lax.div(q, 2)).start()

    def sent(q):
        for step in range(1, owners):
            outgoing(q, step).wait_send()

    def pump(q, h):
        send(q + 2, h)

    def pack(g):
        @pl.when(t > 0)
        def _():
            tail_copy(g, t - 1).wait_recv()

        pack_bodies(real_ref, imag_ref, rows_ref, early_ref, send_ref, g)

    def collect(q, g, h):
        for step in range(1, owners):
            incoming(q, step).wait_recv()
        if h == 0:
            keep(g).wait()
        passing(q, b).start()

    def merge(q, g, h):
        passing(q, 1 - b).wait_recv()

        def pair(i, carry):
            p = h * quad + i
            for zz in range(chans):
                sides = []
                for core in range(2):
                    got = [recv[core, g, zz * times + tt, p].astype(F32) for tt in range(times)]
                    sides.append(jnp.concatenate(
                        [r[:frames] for r in got] + [r[frames:] for r in got], axis=0))
                at = slice(zz * lanes, (zz + 1) * lanes)
                for k, cut in enumerate((slice(0, half), slice(half, lanes))):
                    joined = jnp.concatenate([side[:, cut] for side in sides], axis=1)
                    x_ref[g * SPAN + k * pairs + p, :, at] = joined.astype(BF16)
            return carry

        lax.fori_loop(0, quad, pair, 0, unroll=2)

    def zeroth(c):
        flags = flag_ref[pl.ds(c, 1), :].astype(F32)
        denom[c] = row_denominators(model.at[c], gain_ref[c], flags)

    def first(c):
        flags = flag_ref[pl.ds(c, 1), :].astype(F32)
        own = x_ref[c, :, pl.ds(off, mine)]
        numer = row_numerators(x_ref[c], own, model.at[c], gain_ref[c], flags)
        older = gain_ref[c, :, pl.ds(off, mine)]
        full[c, :, pl.ds(off, mine)] = damped(older, numer, denom[c])

    def second(*pair):
        flags = [flag_ref[pl.ds(c, 1), :].astype(F32) for c in pair]
        denoms = paired_denominators([model.at[c] for c in pair], [full[c] for c in pair], flags)
        for c, flag, denominator in zip(pair, flags, denoms):
            own = x_ref[c, :, pl.ds(off, mine)]
            numer = row_numerators(x_ref[c], own, model.at[c], full[c], flag)
            new_ref[c] = damped(full[c, :, pl.ds(off, mine)], numer, denominator)

    def seconds(g, h):
        start = g * SPAN + h * quad
        for k in range(2):
            for j in range(0, quad, 2):
                second(start + k * pairs + j, start + k * pairs + j + 1)

    def each(stage, g, h):
        start = g * SPAN + h * quad
        for k in range(2):
            for j in range(quad):
                stage(start + k * pairs + j)

    unit = 2.0 * math.pi / (512 * kept)
    middle = 2 * (kept + me * channels) + channels - 1

    def front(
        sample_ref, frame_ref, win_ref, cos_ref, sin_ref, high_ref, real_late, imag_late,
    ):
        def fetch(r):
            return pltpu.make_async_copy(
                sample_hbm.at[:, pl.ds(r, 1)], sample_ref.at[:, pl.ds(r, 1)], sample_sem.at[r])

        for r in range(2):
            fetch(r).start()
        fill_transform(cos_ref, sin_ref, high_ref)
        for r in range(2):
            fetch(r).wait()
            spread_samples(sample_ref, frame_ref, r)
            if r == 0:
                for g in range(groups):
                    load(g).start()
        window_frames(frame_ref, tap_ref, win_ref, local_inputs)

        def transform(real_out, imag_out, start):
            at = pl.ds(start, real_out.shape[1])
            real_in, imag_in = win_ref[0, at, :], win_ref[1, at, :]
            real_out[...] = dot_nt(cos_ref[...], real_in) + dot_nt(sin_ref[...], imag_in)
            imag_out[...] = dot_nt(cos_ref[...], imag_in) - dot_nt(sin_ref[...], real_in)

        transform(real_late, imag_late, frames * local_inputs)
        pack_tails(real_late, imag_late, tail_ref, pairs)
        pl.semaphore_wait(barrier, owners)

        @pl.when(t < times - 1)
        def _():
            for g in range(min(2, groups)):
                tail_copy(g, t + 1).start()

        @pl.when(t == 0)
        def _():
            early_ref[...] = jnp.zeros_like(early_ref)

        transform(real_ref, imag_ref, 0)

        @pl.when(t < times - 1)
        def _():
            for g in range(2, groups):
                tail_copy(g - 2, t + 1).wait_send()
                tail_copy(g, t + 1).start()

    columns = (frames + taps - 1) * local_inputs
    coarse = kept >> ((kept.bit_length() - 1) // 2)
    pl.run_scoped(
        front,
        pltpu.VMEM((local_inputs, 2, frames, width), BF16),
        pltpu.VMEM((2, width // 128, frames * local_inputs, 128), F32),
        pltpu.VMEM((2, columns, width), BF16),
        pltpu.VMEM((kept, width), BF16),
        pltpu.VMEM((kept, width), BF16),
        pltpu.VMEM((4, coarse, width), F32),
        pltpu.VMEM((kept, late * local_inputs), F32),
        pltpu.VMEM((kept, late * local_inputs), F32),
    )

    def back(y_ref, sum_ref, bits_ref):
        position = lax.broadcasted_iota(jnp.int32, (8, inputs), 1)
        column = lax.div(position, inputs // 4)
        row = lax.broadcasted_iota(jnp.int32, (8, inputs), 0)
        factor = jnp.where(row == 0, column * 64, position - column * (inputs // 4))
        factor = jnp.where(row < 2, factor, 0).astype(F32).astype(BF16)
        chosen = steer_ref[...].astype(F32)
        chosen = jnp.concatenate([chosen, jnp.zeros((6, beam_count), F32)], axis=0).astype(BF16)
        product = lax.dot_general(chosen, factor, TN, preferred_element_type=F32)
        bits_ref[...] = product.astype(jnp.int32) & 255

        def tabulate(block, carry):
            at = pl.ds(pl.multiple_of(block * 16, 16), 16)
            index = bits_ref[at, :] - 128
            imag, real = short_sincos((index * middle).astype(F32) * (0.5 * unit))
            turned = index.astype(F32) * (unit * channels / 2)
            for k in range(terms):
                if k:
                    scale = turned * (1.0 / k)
                    real, imag = real * scale, imag * scale
                table[k, at, :inputs] = real.astype(BF16)
                table[k, at, inputs:] = imag.astype(BF16)
            return carry

        pack(0)
        lax.fori_loop(0, beam_count // 16, tabulate, 0)
        for h in range(2):
            send(h, h)

        def ready(g):
            load(g).wait()

            def some(i, carry):
                for j in range(8):
                    zeroth(g * SPAN + i * 8 + j)
                return carry

            lax.fori_loop(0, SPAN // 8, some, 0)

        for g in range(groups):
            if g + 1 < groups:
                pack(g + 1)
            ready(g)
            if g in (1, 2) and g + 1 < 2 * groups:
                pump(g - 1, (g - 1) % 2)

        def beams(start):
            count = y_ref.shape[0]

            def prepare(c, carry):
                x, gains = x_ref[start + c], gain_ref[start + c]
                flags = flag_ref[pl.ds(start + c, 1), :].astype(F32) * (1.0 / math.sqrt(inputs))
                hr, hi = gains[0:1] * flags, gains[1:2] * flags
                xr, xi = x[:planes].astype(F32), x[planes:].astype(F32)
                yr = (xr * hr - xi * hi).astype(BF16)
                yi = (xi * hr + xr * hi).astype(BF16)
                y_ref[c, :planes, :inputs] = yr
                y_ref[c, :planes, inputs:] = -yi
                y_ref[c, planes:, :inputs] = yi
                y_ref[c, planes:, inputs:] = yr
                return carry

            lax.fori_loop(0, count, prepare, 0, unroll=4)
            y = y_ref[...].reshape(count * 2 * planes, 2 * inputs)
            for k in range(terms):
                sum_ref[k] = dot_nt(y, table[k])

            def finish(c, carry):
                u = ((start + c).astype(F32) - (channels - 1) / 2) * (2.0 / channels)
                at = pl.ds(pl.multiple_of(c * 2 * planes, 2 * planes), 2 * planes)
                last = sum_ref[terms - 1, at, :]
                vr, vi = last[:planes], last[planes:]
                for k in reversed(range(terms - 1)):
                    term = sum_ref[k, at, :]
                    vr, vi = term[:planes] - u * vi, term[planes:] + u * vr
                power_ref[start + c] = vr * vr + vi * vi
                return carry

            lax.fori_loop(0, count, finish, 0, unroll=4)

        for q in range(2):
            if q + 2 < 2 * groups and not 1 <= q + 1 < groups:
                pump(q, q)
        collect(0, 0, 0)

        def group(g, carry):
            @pl.when(g < groups)
            def _():
                @pl.when(2 * g + 4 < 2 * groups)
                def _():
                    pump(2 * g + 2, 0)

                merge(2 * g, g, 0)
                each(first, g, 0)
                collect(2 * g + 1, g, 1)

                @pl.when(2 * g + 5 < 2 * groups)
                def _():
                    pump(2 * g + 3, 1)

            @pl.when(g >= 1)
            def _():
                sharing(g - 1, pl.multiple_of((1 - b) * mine, mine)).wait_recv()
                seconds(g - 1, 0)

            @pl.when(g < groups)
            def _():
                merge(2 * g + 1, g, 1)
                each(first, g, 1)
                store_x(g).start()

                @pl.when(lax.rem(g, 2) == 1)
                def _():
                    beams((g - 1) * SPAN)

                sharing(g, off).start()

            @pl.when(g + 1 < groups)
            def _():
                collect(2 * g + 2, g + 1, 0)

            @pl.when(g >= 1)
            def _():
                seconds(g - 1, 1)
                store_power(g - 1).start()

            return carry

        lax.fori_loop(0, groups + 1, group, 0)

    wide = 2 * SPAN * 2 * planes
    pl.run_scoped(
        back,
        pltpu.VMEM((2 * SPAN, 2 * planes, 2 * inputs), BF16),
        pltpu.VMEM((terms, wide, beam_count), F32),
        pltpu.VMEM((beam_count, inputs), jnp.int32),
    )

    def drain(g, carry):
        for h in range(2):
            passing(2 * g + h, b).wait_send()

        sharing(g, off).wait_send()
        store_x(g).wait()
        store_power(g).wait()
        return carry

    lax.fori_loop(0, groups, drain, 0)
    for q in range(2 * groups):
        sent(q)

    @pl.when(t < times - 1)
    def _():
        for g in range(max(groups - 2, 0), groups):
            tail_copy(g, t + 1).wait_send()


def solve_gains(samples, window_taps, model, gains, flags, beam_steering, chans, times, kept):
    local_inputs, _, width, frames = samples.shape
    taps = window_taps.shape[0]
    natural = jnp.transpose(samples, (0, 1, 3, 2))
    channels, _, mine, inputs = model.shape
    beams = beam_steering.shape[1]
    owners = chans * times
    groups, pairs, rows, lanes = channels // SPAN, SPAN // 2, 2 * frames, 2 * local_inputs
    terms = series_terms(channels, kept)
    vmem, apart = pl.BlockSpec(memory_space=pltpu.VMEM), pl.BlockSpec(memory_space=pl.ANY)
    dma = pltpu.SemaphoreType.DMA
    late = (taps - 1) * SPAN
    planes = times * frames
    return pl.pallas_call(
        functools.partial(gains_kernel, chans=chans, times=times, kept=kept),
        out_shape=[
            jax.ShapeDtypeStruct((channels, 2 * planes, inputs), BF16),
            jax.ShapeDtypeStruct((channels, 2, mine), F32),
            jax.ShapeDtypeStruct((channels, planes, beams), F32),
        ],
        in_specs=[apart, vmem, apart, vmem, vmem, vmem],
        out_specs=[apart, vmem, apart],
        scratch_shapes=[
            pltpu.VMEM((owners, groups, pairs, rows, lanes), BF16),
            pltpu.VMEM((groups, owners, late, lanes), BF16),
            pltpu.VMEM((groups, owners, late, lanes), BF16),
            pltpu.VMEM((2, groups, owners, pairs, rows, lanes), BF16),
            pltpu.VMEM(model.shape, BF16),
            pltpu.VMEM((channels, 2, inputs), F32),
            pltpu.VMEM((channels, 1, mine), F32),
            pltpu.VMEM((terms, beams, 2 * inputs), BF16),
            pltpu.VMEM((channels, 2 * planes, inputs), BF16),
            pltpu.VMEM((channels, planes, beams), F32),
            pltpu.VMEM((kept, frames * local_inputs), F32),
            pltpu.VMEM((kept, frames * local_inputs), F32),
            pltpu.VMEM((2, pairs * rows, lanes), F32),
            dma((2 * groups, owners - 1)), dma((2 * groups, owners - 1)), dma((groups,)),
            dma((groups,)), dma((groups,)),
            dma((2 * groups,)), dma((2 * groups,)),
            *[dma((groups,))] * 3,
            dma((2,)), dma((groups,)), dma((groups,)),
        ],
        compiler_params=pltpu.CompilerParams(
            collective_id=0, has_side_effects=True, vmem_limit_bytes=67043328
        ),
        cost_estimate=pl.CostEstimate(
            flops=40 * channels * mine * inputs * planes,
            bytes_accessed=2 * model.size, transcendentals=0,
        ),
        name="gains",
    )(natural, window_taps, model, gains, flags, beam_steering)


def correlate_only_kernel(
    x_hbm, new_hbm, power_hbm, vis_hbm, new_out, power_out,
    x_ref, new_ref, power_ref, vis_ref, x_sem, in_sem, out_sem, vis_sem,
):
    slots, block, _, mine, _ = vis_ref.shape
    channels, rows, _ = x_ref.shape
    half = rows // 2
    parts = x_sem.shape[0]
    off = pl.multiple_of(lax.axis_index("beam") * mine, mine)
    exact = half & (half - 1) == 0
    before, after = (1.0 / half, 1.0) if exact else (1.0, 1.0 / half)

    def fetch(k):
        part = pl.ds(k * (channels // parts), channels // parts)
        return pltpu.make_async_copy(x_hbm.at[part], x_ref.at[part], x_sem.at[k])

    for k in range(parts):
        fetch(k).start()
    ins = [pltpu.make_async_copy(new_hbm, new_ref, in_sem.at[0]),
           pltpu.make_async_copy(power_hbm, power_ref, in_sem.at[1])]
    outs = [pltpu.make_async_copy(new_ref, new_out, out_sem.at[0]),
            pltpu.make_async_copy(power_ref, power_out, out_sem.at[1])]
    for copy in ins:
        copy.start()

    def store(i, slot):
        part = pl.ds(i * block, block)
        return pltpu.make_async_copy(vis_ref.at[slot], vis_hbm.at[part], vis_sem.at[slot])

    def step(i, carry):
        slot = lax.rem(i, slots)

        @pl.when(i >= slots)
        def _():
            store(i - slots, slot).wait()

        for j in range(block):
            x = x_ref[i * block + j]
            own = x_ref[i * block + j, :, pl.ds(off, mine)]
            scaled = (own.astype(F32) * before).astype(BF16)
            rotated = jnp.concatenate([scaled[half:], -scaled[:half]], axis=0)
            for part, left in enumerate((scaled, rotated)):
                terms = lax.dot_general(left, x, TN, preferred_element_type=F32)
                vis_ref[slot, j, part] = (terms if exact else terms * after).astype(BF16)
        store(i, slot).start()
        return carry

    steps = channels // block
    each = steps // parts
    for k in range(parts):
        fetch(k).wait()
        lax.fori_loop(k * each, (k + 1) * each, step, 0)
        if k == 0:
            for first, last in zip(ins, outs):
                first.wait()
                last.start()
    for copy in outs:
        copy.wait()
    for i in range(max(steps - slots, 0), steps):
        store(i, i % slots).wait()


def correlate(x, new, power):
    channels, rows, inputs = x.shape
    mine = new.shape[2]
    block, parts, slots = 4, 4, 3
    apart = pl.BlockSpec(memory_space=pl.ANY)
    dma = pltpu.SemaphoreType.DMA
    return pl.pallas_call(
        correlate_only_kernel,
        out_shape=[
            jax.ShapeDtypeStruct((channels, 2, mine, inputs), BF16),
            jax.ShapeDtypeStruct(new.shape, F32),
            jax.ShapeDtypeStruct(power.shape, F32),
        ],
        in_specs=[apart] * 3,
        out_specs=[apart] * 3,
        scratch_shapes=[
            pltpu.VMEM(x.shape, BF16), pltpu.VMEM(new.shape, F32), pltpu.VMEM(power.shape, F32),
            pltpu.VMEM((slots, block, 2, mine, inputs), BF16),
            dma((parts,)), dma((2,)), dma((2,)), dma((slots,)),
        ],
        cost_estimate=pl.CostEstimate(
            flops=4 * channels * mine * inputs * rows,
            bytes_accessed=4 * channels * mine * inputs, transcendentals=0,
        ),
        name="correlate_only",
    )(x, new, power)


def series_terms(channels, chan_total):
    reach = 128 * (channels / 2) * 2.0 * math.pi / (512 * chan_total)
    terms, left = 1, reach
    while left >= 2.0**-23:
        terms += 1
        left *= reach / terms
    return terms


def tiled_shards(samples, window_taps, sky_model, prior_gains, beam_steering, input_flags):
    x, new, power = solve_gains(
        samples, window_taps, sky_model, prior_gains, input_flags, beam_steering,
        lax.axis_size("chan"), lax.axis_size("tm"), NCH,
    )
    visibilities, new, power = correlate(x, new, power)
    return visibilities, new, jnp.transpose(power, (0, 2, 1))


def tiles(samples, window_taps, sky_model, prior_gains, beam_steering, input_flags):
    owners = lax.axis_size("tm") * lax.axis_size("chan")
    local_inputs, frames = samples.shape[0], samples.shape[3]
    return (
        ITERS == 2
        and lax.axis_size("beam") == 2
        and owners > 1
        and 2 * local_inputs == 128
        and frames == 8
        and 1 < window_taps.shape[0] <= frames
        and samples.shape[2] & (samples.shape[2] - 1) == 0
        and lax.axis_size("tm") % 2 == 0
        and NCH % (2 * owners * SPAN) == 0
        and sky_model.size <= 1 << 24
    )


def any_shards(*args):
    return tiled_shards(*args) if tiles(*args) else shards(*args)


def solution(mesh):
    return jax.shard_map(
        any_shards,
        mesh=mesh,
        in_specs=(
            P(("group", "chan", "beam"), None, None, "tm"),
            P(),
            P(("group", "chan", "tm"), None, "beam", None),
            P(("group", "chan", "tm"), None, None),
            P(None, ("group", "beam")),
            P(("group", "chan", "tm"), None),
        ),
        out_specs=(
            P(("group", "chan", "tm"), None, "beam", None),
            P(("group", "chan", "tm"), None, "beam"),
            P(("group", "chan", "tm"), "beam", None),
        ),
        check_vma=False,
    )
```
